128 devices in a mesh: cores: 8 (over y, core), samp: 16 (over z, x).
Axes of the slice: x: 4, y: 4, z: 4, core: 2. Of those that a mesh axis runs over, the one named last changes fastest.
Arguments:
- cores: float32 [8, 512, 2304], P('cores'), may hold values from -0.875 to 0.875
- indices: int32 [16384, 8], P('samp'), may hold values from 0 to 511
- observed: float32 [16384], P('samp'), may hold values from -6 to 6
- step_size: float32 [], replicated, may hold values from 0.2 to 0.6
Outputs:
- new_cores: float32 [8, 512, 2304], P('cores', 'samp')
The draws below stay inside these ranges and needn't reach their ends.
All inputs are finite; a program needn't handle non-finite values.
Results may differ from the reference program's by a relative error of at most 0.0003.
Values sent between devices are 32-bit elements; how exact they have to be, the bound alone decides.
No kernel may reach another device: no remote copies, remote signals or barrier semaphores. Data moves between devices by JAX's collectives and lax.ppermute only.
A program may use at most 128 MiB of HBM per device.

```python
import math
import jax
import jax.numpy as jnp
from jax import lax

R = 48
N = 512
MODES = 8
SAMPLES = 16384


def draw_cores(key, part):
    factor_scale = R ** (-0.5)
    values = jax.random.normal(jax.random.fold_in(key, 13), (MODES, N, R * R), jnp.float32) * factor_scale
    return jnp.clip(values, -0.875, 0.875)


def with_ends(array, stream_key, smallest, high):
    index_at = [jax.random.randint(jax.random.fold_in(stream_key, axis), (), 0, length) for axis, length in enumerate(array.shape)]
    widest = array.shape.index(max(array.shape))
    next_to = index_at[:widest] + [(index_at[widest] + 1) % array.shape[widest]] + index_at[widest + 1:]
    return array.at[tuple(index_at)].set(smallest).at[tuple(next_to)].set(high)


def steps_of(rng, extent, shards, least, high):
    loudness, own = 1.0, jax.random.fold_in(rng, 6)
    for dim, parts in shards:
        heights = jnp.exp(jax.random.uniform(jax.random.fold_in(own, dim), (parts,), jnp.float32, least / len(shards), high / len(shards)))
        loudness = loudness * jnp.repeat(heights, extent[dim] // parts).reshape([-1 if axis == dim else 1 for axis in range(len(extent))])
    return loudness


def scatter_about(key, extent, width, bound, cuts=(), held_as=jnp.bfloat16):
    entries = jax.random.normal(key, extent, jnp.float32) * width
    if len(cuts) > 0:
        entries = steps_of(key, extent, cuts, -0.22, 0.18) * entries
    return jnp.clip(entries, min=-bound, max=bound).astype(held_as)


def setup_inputs(seed: int = 0) -> dict:
    streams_of = jax.random.split(jax.random.key(seed), 5)
    return {
        "cores": draw_cores(jax.random.fold_in(streams_of[4], 71), 0),
        "indices": with_ends(jax.random.randint(streams_of[1], (SAMPLES, MODES), 0, N), jax.random.fold_in(streams_of[1], 1), 0, N - 1).astype(jnp.int32),
        "observed": scatter_about(streams_of[2], (SAMPLES,), 1.0, 6.0, ((0, 16),), jnp.float32),
        "step_size": jnp.clip(jnp.exp(jax.random.uniform(streams_of[3], (), jnp.float32, math.log(0.2), math.log(0.6))), 0.2, 0.6),
    }


HIGH = lax.Precision.HIGHEST

def reference(cores, indices, observed, step_size):
    count = indices.shape[0]
    unit = (jnp.arange(R) == 0).astype(jnp.float32)
    mats = []
    for k in range(MODES):
        mats.append(jnp.take(cores[k], indices[:, k], axis=0).reshape(count, R, R))
    lefts = []
    vec = jnp.broadcast_to(unit, (count, R))
    for k in range(MODES):
        lefts.append(vec)
        vec = jnp.einsum('sa,sab->sb', vec, mats[k], precision=HIGH)
    rights = [None] * MODES
    vec = jnp.broadcast_to(unit, (count, R))
    for k in range(MODES - 1, -1, -1):
        rights[k] = vec
        vec = jnp.einsum('sab,sb->sa', mats[k], vec, precision=HIGH)
    mats = None
    predicted = jnp.sum(jnp.einsum('sa,sab->sb', lefts[0], jnp.take(cores[0], indices[:, 0], axis=0).reshape(count, R, R), precision=HIGH) * rights[0], axis=1)
    residual = predicted - observed
    carry = jnp.eye(R, dtype=jnp.float32)
    results = []
    for k in range(MODES):
        outer = (lefts[k][:, :, None] * (residual[:, None] * rights[k])[:, None, :]).reshape(count, R * R)
        gradient = jax.ops.segment_sum(outer, indices[:, k], num_segments=N)
        updated = (cores[k] - step_size * gradient).reshape(N, R, R)
        product = jnp.einsum('ac,icb->iab', carry, updated, precision=HIGH)
        if k < MODES - 1:
            gram = jnp.einsum('iab,iac->bc', product, product, precision=HIGH) / N
            lower = jnp.linalg.cholesky(gram)
            flat = product.reshape(N * R, R)
            ortho = lax.linalg.triangular_solve(lower, flat, left_side=False, lower=True, transpose_a=True)
            results.append(ortho.reshape(N, R * R))
            carry = lower.T
        else:
            results.append(product.reshape(N, R * R))
    return jnp.stack(results)
```

```python
import functools

import jax
import jax.numpy as jnp
from jax import lax
from jax.experimental import pallas as pl
from jax.experimental.pallas import tpu as pltpu
from jax.sharding import PartitionSpec as P

R = 48
N = 512
MODES = 8
RR = R * R
GROUPS = 8
WIDE = 4
ROWS = GROUPS * R
LANES = WIDE * 64
FEATS = 104
SLOTS = 128
HIGH = lax.Precision.HIGHEST
F32 = jnp.float32
BF16 = jnp.bfloat16
COLS = 384
BIG = 48 << 20


def dot_rows(a, b):
    return lax.dot_general(a, b, (((0,), (0,)), ((), ())), preferred_element_type=F32)


def dot_lanes(a, b, precision=None):
    return lax.dot_general(
        a, b, (((1,), (1,)), ((), ())), preferred_element_type=F32, precision=precision
    )


def halves(x):
    hi = x.astype(BF16)
    return hi, (x - hi.astype(F32)).astype(BF16)


def iota(shape, dim):
    return lax.broadcasted_iota(jnp.int32, shape, dim)


def ranks(row, peers, slab):
    count = row.shape[1]
    chunks = count // 128
    dest = row // slab
    hit = (iota((peers, count), 0) == dest).astype(F32)
    stacked = jnp.concatenate([hit[:, c * 128 : (c + 1) * 128] for c in range(chunks)], axis=0)
    upper = (iota((128, 128), 0) <= iota((128, 128), 1)).astype(BF16)
    inside = jnp.dot(stacked.astype(BF16), upper, preferred_element_type=F32)
    before = jnp.zeros((peers, 1), F32)
    out = []
    for c in range(chunks):
        part = inside[c * peers : (c + 1) * peers]
        mine = hit[:, c * 128 : (c + 1) * 128]
        out.append(jnp.sum(mine * (part + before), axis=0, keepdims=True))
        before = before + part[:, 127:128]
    return jnp.concatenate(out, axis=1).astype(jnp.int32) - 1, dest


def gather_kernel(idx_ref, table_ref, mats_ref, sent_ref, slot_ref, most_ref, hot_ref, *, peers):
    step = pl.program_id(0)
    mode = lax.axis_index("cores")
    leftward = mode < MODES // 2
    slab = N // peers

    @pl.when(step == 0)
    def _():
        row = idx_ref[pl.ds(mode, 1), :]
        count = row.shape[1]
        hot_ref[...] = (iota((N, count), 0) == row).astype(BF16)
        place, dest = ranks(row, peers, slab)
        slot_ref[0:1, :] = place
        slot_ref[1:2, :] = dest
        slot_ref[2:3, :] = row - dest * slab
        slot_ref[3:8, :] = jnp.zeros((5, count), jnp.int32)
        every = idx_ref[...] // slab
        most = jnp.zeros((MODES, 1), F32)
        for j in range(peers):
            most = jnp.maximum(most, jnp.sum((every == j).astype(F32), axis=1, keepdims=True))
        most_ref[...] = jnp.broadcast_to(jnp.max(most, axis=0, keepdims=True), (8, 128))

    hot = hot_ref[...]
    hi, lo = halves(table_ref[...])
    out = dot_rows(hi, hot) + dot_rows(lo, hot)
    mats_ref[...] = out

    @pl.when(jnp.logical_and(leftward, step == 0))
    def _():
        sent_ref[...] = out[0:R]

    @pl.when(jnp.logical_not(leftward))
    def _():
        per = COLS // R
        rows = jnp.concatenate([out[i * R : i * R + 1] for i in range(per)], axis=0)
        sent_ref[pl.ds(pl.multiple_of(step * per, per), per), :] = rows


def times_left(mats_ref, vec_ref, out_ref):
    count = vec_ref.shape[1]

    def chunk(c, _):
        lanes = pl.ds(pl.multiple_of(c * 128, 128), 128)
        acc = [jnp.zeros((R, 128), F32) for _ in range(2)]
        for a in range(R):
            acc[a % 2] = acc[a % 2] + mats_ref[a * R : (a + 1) * R, lanes] * vec_ref[a : a + 1, lanes]
        out_ref[:, lanes] = acc[0] + acc[1]
        return 0

    lax.fori_loop(0, count // 128, chunk, 0)


def times_right(mats_ref, vec_ref, out_ref):
    count = vec_ref.shape[1]

    def chunk(c, _):
        lanes = pl.ds(pl.multiple_of(c * 128, 128), 128)
        vec = vec_ref[:, lanes]
        for a in range(0, R, 8):
            rows = [
                jnp.sum(mats_ref[(a + i) * R : (a + i + 1) * R, lanes] * vec, axis=0, keepdims=True)
                for i in range(8)
            ]
            out_ref[a : a + 8, lanes] = jnp.concatenate(rows, axis=0)
        return 0

    lax.fori_loop(0, count // 128, chunk, 0)


def apply(left, mats_ref, vec_ref, out_ref):
    @pl.when(left)
    def _():
        times_left(mats_ref, vec_ref, out_ref)

    @pl.when(jnp.logical_not(left))
    def _():
        times_right(mats_ref, vec_ref, out_ref)


def hop_kernel(mats_ref, vec_ref, out_ref, *, second):
    mode = lax.axis_index("cores")
    left = (mode >= MODES // 2) if second else (mode < MODES // 2)
    apply(left, mats_ref, vec_ref, out_ref)


def spread(values, slot_ref, most_ref, turn, pay_ref):
    place = slot_ref[0:1, :] - turn * SLOTS
    fits = jnp.logical_and(place >= 0, place < SLOTS)
    key = jnp.where(fits, slot_ref[1:2, :] * SLOTS + place, -1)
    hi, lo = halves(values)
    both = jnp.concatenate([hi, lo], axis=0)
    peers = pay_ref.shape[0]
    count = values.shape[1]
    for pair in range(peers // 2):
        base = pair * 2 * SLOTS
        hot = (iota((2 * SLOTS, count), 0) + base == key).astype(BF16)
        out = dot_lanes(both, hot)
        out = out[:FEATS] + out[FEATS:]
        pay_ref[2 * pair] = out[:, :SLOTS]
        pay_ref[2 * pair + 1] = out[:, SLOTS:]
    for peer in range(peers):
        pay_ref[peer, 97:98, :] = most_ref[0:1, :]


def route_kernel(mats_ref, one_ref, two_ref, obs_ref, slot_ref, most_ref, pay_ref, val_ref, tmp_ref):
    mode = lax.axis_index("cores")
    early = mode < MODES // 2
    apply(jnp.logical_not(early), mats_ref, two_ref, tmp_ref)
    one = one_ref[...]
    two = two_ref[...]
    predicted = jnp.sum(tmp_ref[...] * one, axis=0, keepdims=True)
    residual = predicted - obs_ref[...]
    flag = jnp.where(early, 1.0, 0.0)
    left = jnp.where(flag > 0.5, one, two)
    right = jnp.where(flag > 0.5, two, one) * residual
    count = one.shape[1]
    values = jnp.concatenate(
        [left, right, slot_ref[2:3, :].astype(F32), jnp.zeros((FEATS - 97, count), F32)], axis=0
    )
    val_ref[...] = values
    spread(values, slot_ref, most_ref, 0, pay_ref)


def again_kernel(turn_ref, val_ref, slot_ref, most_ref, pay_ref):
    spread(val_ref[...], slot_ref, most_ref, turn_ref[0], pay_ref)


def collect_kernel(step_ref, recv_ref, base_ref, out_ref, turns_ref):
    peers = recv_ref.shape[0]
    left = jnp.concatenate([recv_ref[s, 0:R, :] for s in range(peers)], axis=1)
    right = jnp.concatenate([recv_ref[s, R : 2 * R, :] for s in range(peers)], axis=1)
    loc = jnp.concatenate([recv_ref[s, 96:97, :] for s in range(peers)], axis=1).astype(jnp.int32)
    row_of = loc // WIDE
    lane_of = loc - row_of * WIDE
    count = loc.shape[1]

    def picked(x, key, n, pad):
        hi = x.astype(BF16).astype(F32)
        lo = x - hi
        tail = [jnp.zeros((pad, count), BF16)] if pad else []
        his, los = [], []
        for i in range(n):
            here = key == i
            his += [jnp.where(here, hi, 0.0).astype(BF16)] + tail
            los += [jnp.where(here, lo, 0.0).astype(BF16)] + tail
        return jnp.concatenate(his, axis=0), jnp.concatenate(los, axis=0)

    xh, xl = picked(left, row_of, GROUPS, 0)
    yh, yl = picked(right, lane_of, WIDE, 16)
    grad = dot_lanes(xh, yh) + (dot_lanes(xh, yl) + dot_lanes(xl, yh))
    out_ref[...] = base_ref[...] - step_ref[0] * grad
    most = jnp.max(recv_ref[:, 97, :]).astype(jnp.int32)
    turns_ref[0] = (most + SLOTS - 1) // SLOTS


def unpacked(packed):
    return jnp.concatenate([packed, pltpu.roll(packed, 64, 1)], axis=0)[:, :R]


def gram_kernel(*refs, turn):
    if turn == 0:
        own_ref, other_ref, out_ref, prod_ref = refs
    else:
        recv_ref, own_ref, other_ref, out_ref, sum_ref, prod_ref = refs
    mode = lax.axis_index("cores")
    mine = jnp.where(mode % 2 == turn % 2, 1.0, 0.0)
    core = jnp.where(mine > 0.5, own_ref[...], other_ref[...])
    if turn == 0:
        prod = core
    else:
        packed = jnp.sum(recv_ref[...], axis=0)
        sum_ref[...] = packed
        before = unpacked(packed)
        for g in range(GROUPS):
            prod_ref[g * R : (g + 1) * R, :] = jnp.dot(
                before, core[g * R : (g + 1) * R], preferred_element_type=F32, precision=HIGH
            )
        prod = prod_ref[...]
    even = jnp.zeros((64, 128), F32)
    odd = jnp.zeros((64, 128), F32)
    for part in range(2):
        z = lax.dot_general(
            core[:, part * 128 : (part + 1) * 128],
            prod[:, part * 128 : (part + 1) * 128],
            (((0,), (0,)), ((), ())),
            preferred_element_type=F32,
            precision=HIGH,
        )
        even = even + z[0:64]
        odd = odd + z[64:128]
    low = even + pltpu.roll(odd, 64, 1)
    high = pltpu.roll(even, 64, 1) + odd
    packed = jnp.where(iota((24, 128), 1) < 64, low[0:24], high[24:48])
    live = jnp.where(mode // 2 == turn // 2, 1.0 / N, 0.0)
    packed = packed * live
    for peer in range(out_ref.shape[0]):
        out_ref[peer] = packed


def final_kernel(*refs):
    sums = refs[: MODES - 2]
    recv_ref, own_ref, out_ref, prod_ref, block_ref = refs[MODES - 2 :]
    mode = lax.axis_index("cores")
    every = [s[...] for s in sums] + [jnp.sum(recv_ref[...], axis=0)]
    own = jnp.zeros((24, 128), F32)
    prev = jnp.zeros((24, 128), F32)
    for t in range(MODES - 1):
        own = own + every[t] * jnp.where(mode == t, 1.0, 0.0)
        prev = prev + every[t] * jnp.where(mode == t + 1, 1.0, 0.0)
    row = iota((R, 128), 0)
    lane = iota((R, 128), 1)
    eye = jnp.where(lane == row, 1.0, 0.0)
    side = jnp.where(lane == row + 64, 1.0, 0.0)

    def start(packed, absent):
        full = jnp.concatenate([packed, pltpu.roll(packed, 64, 1)], axis=0)
        full = jnp.where(lane < R, full, 0.0)
        return full + eye * absent + side

    mats = [
        start(own, jnp.where(mode == MODES - 1, 1.0, 0.0)),
        start(prev, jnp.where(mode == 0, 1.0, 0.0)),
    ]
    for j in range(R):
        for w in range(2):
            m = mats[w]
            pivot = m[j : j + 1, :]
            scale = 1.0 / m[j : j + 1, j : j + 1]
            col = jnp.where(row[:, 0:1] > j, m[:, j : j + 1] * scale, 0.0)
            mats[w] = m - col * pivot
    tri = []
    for w in range(2):
        diag = jnp.sum(jnp.where(lane == row, mats[w], 0.0), axis=1, keepdims=True)
        tri.append(mats[w] * (1.0 / jnp.sqrt(diag)))
    carry = tri[1][:, :R]
    inv = jnp.where(lane >= 64, tri[0], 0.0)
    turned = pltpu.roll(inv, 64, 1)
    block_ref[...] = jnp.zeros((LANES, LANES), F32)
    for h in range(WIDE):
        block_ref[h * 64 : h * 64 + R, (h // 2) * 128 : (h // 2 + 1) * 128] = inv if h % 2 else turned
    for g in range(GROUPS):
        prod_ref[g * R : (g + 1) * R, :] = jnp.dot(
            carry, own_ref[g * R : (g + 1) * R, :], preferred_element_type=F32, precision=HIGH
        )
    out_ref[...] = dot_lanes(prod_ref[...], block_ref[...], HIGH)


def vmem():
    return pl.BlockSpec(memory_space=pltpu.VMEM)


def smem():
    return pl.BlockSpec(memory_space=pltpu.SMEM)


def call(kernel, outs, ins, scratch=(), name=None):
    return pl.pallas_call(
        kernel,
        out_shape=outs,
        in_specs=ins,
        out_specs=jax.tree.map(lambda o: smem() if o.dtype == jnp.int32 and o.size == 1 else vmem(), outs),
        scratch_shapes=list(scratch),
        compiler_params=pltpu.CompilerParams(vmem_limit_bytes=BIG),
        name=name,
    )


def shape(*dims, dtype=F32):
    return jax.ShapeDtypeStruct(dims, dtype)


def on_device(cores, indices, observed, step_size):
    peers = lax.axis_size("samp")
    count = indices.shape[0]
    slab = N // peers
    table = cores[0]
    idx = indices.T
    step = step_size.reshape(1)

    mats, sent, slot, most = pl.pallas_call(
        functools.partial(gather_kernel, peers=peers),
        grid=(RR // COLS,),
        in_specs=[
            pl.BlockSpec((MODES, count), lambda i: (0, 0)),
            pl.BlockSpec((N, COLS), lambda i: (0, i)),
        ],
        out_specs=[
            pl.BlockSpec((COLS, count), lambda i: (i, 0)),
            pl.BlockSpec((R, count), lambda i: (0, 0)),
            pl.BlockSpec((8, count), lambda i: (0, 0)),
            pl.BlockSpec((8, 128), lambda i: (0, 0)),
        ],
        out_shape=[shape(RR, count), shape(R, count), shape(8, count, dtype=jnp.int32), shape(8, 128)],
        scratch_shapes=[pltpu.VMEM((N, count), BF16)],
        compiler_params=pltpu.CompilerParams(vmem_limit_bytes=BIG),
        name="gather",
    )(idx, table)

    first = lax.axis_index("samp") * slab
    kept = lax.dynamic_slice_in_dim(table, first, slab, 0)
    base = kept.reshape(GROUPS, WIDE, R, R).transpose(0, 2, 1, 3)
    base = jnp.pad(base, ((0, 0), (0, 0), (0, 0), (0, 64 - R))).reshape(ROWS, LANES)

    mode = lax.axis_index("cores")
    edge = jnp.logical_or(mode == 0, mode == MODES - 1)
    unit = jnp.broadcast_to((jnp.arange(R) == 0).astype(F32)[:, None], (R, count))
    one = jnp.where(edge, unit, 0.0)
    two = jnp.zeros((R, count), F32)
    for turn in range(MODES - 1):
        if turn > 0:
            sent = call(
                functools.partial(hop_kernel, second=turn >= MODES // 2),
                shape(R, count),
                [vmem(), vmem()],
                name=f"hop{turn}",
            )(mats, moved)
        moved = lax.ppermute(sent, "cores", [(turn, turn + 1), (7 - turn, 6 - turn)])
        if turn < 3:
            one = one + moved
        else:
            two = two + moved

    pay, values = call(
        route_kernel,
        (shape(peers, FEATS, SLOTS), shape(FEATS, count)),
        [vmem()] * 6,
        [pltpu.VMEM((R, count), F32)],
        name="route",
    )(mats, one, two, observed.reshape(1, count), slot, most)

    def exchanged(block):
        return lax.all_to_all(block, "samp", 0, 0, tiled=True)

    def collected(recv, so_far):
        return call(
            collect_kernel,
            (shape(ROWS, LANES), shape(1, dtype=jnp.int32)),
            [smem(), vmem(), vmem()],
            name="collect",
        )(step, recv, so_far)

    updated, turns = collected(exchanged(pay), base)

    def more(state):
        return state[0] < turns[0]

    def another(state):
        turn, so_far = state
        pay = call(
            again_kernel,
            shape(peers, FEATS, SLOTS),
            [smem(), vmem(), vmem(), vmem()],
            name="again",
        )(turn.reshape(1), values, slot, most)
        return turn + 1, collected(exchanged(pay), so_far)[0]

    _, updated = lax.while_loop(more, another, (jnp.int32(1), updated))

    other = lax.ppermute(updated, "cores", [(i, i ^ 1) for i in range(MODES)])

    sums = []
    recv = None
    for turn in range(MODES - 1):
        odd = turn % 2 == 1
        size = 2 * peers if odd else peers
        outs = [shape(size, 24, 128)] + ([shape(24, 128)] if turn else [])
        res = call(
            functools.partial(gram_kernel, turn=turn),
            outs,
            [vmem()] * (2 if turn == 0 else 3),
            [pltpu.VMEM((ROWS, LANES), F32)],
            name=f"gram{turn}",
        )(*([] if turn == 0 else [recv]), updated, other)
        if turn:
            sums.append(res[1])
        if odd:
            here = turn // 2
            groups = []
            for c in (here, here + 2):
                for h in range(2):
                    pair = [(2 * (c % 4) + h), (2 * ((c + 1) % 4) + h)]
                    groups.append([m * peers + j for m in pair for j in range(peers)])
            recv = lax.all_to_all(
                res[0], ("cores", "samp"), 0, 0, axis_index_groups=groups, tiled=True
            )
        else:
            recv = lax.all_to_all(res[0], "samp", 0, 0, tiled=True)

    out = call(
        final_kernel,
        shape(ROWS, LANES),
        [vmem()] * (MODES),
        [pltpu.VMEM((ROWS, LANES), F32), pltpu.VMEM((LANES, LANES), F32)],
        name="final",
    )(*sums, recv, updated)
    out = out.reshape(GROUPS, R, WIDE, 64)[..., :R].transpose(0, 2, 1, 3)
    return out.reshape(1, slab, RR)


def solution(mesh):
    in_specs = (P("cores", None, None), P("samp", None), P("samp"), P())
    out_specs = P("cores", "samp", None)
    return jax.shard_map(
        on_device, mesh=mesh, in_specs=in_specs, out_specs=out_specs, check_vma=False
    )
```

```python
import functools

import jax
import jax.numpy as jnp
from jax import lax
from jax.experimental import pallas as pl
from jax.experimental.pallas import tpu as pltpu
from jax.sharding import PartitionSpec as P

R = 48
N = 512
MODES = 8
RR = R * R
GROUPS = 8
WIDE = 4
ROWS = GROUPS * R
LANES = WIDE * 64
FEATS = 104
SLOTS = 128
HIGH = lax.Precision.HIGHEST
F32 = jnp.float32
BF16 = jnp.bfloat16
COLS = 384
BIG = 14 << 20


def dot_rows(a, b):
    return lax.dot_general(a, b, (((0,), (0,)), ((), ())), preferred_element_type=F32)


def dot_lanes(a, b, precision=None):
    return lax.dot_general(
        a, b, (((1,), (1,)), ((), ())), preferred_element_type=F32, precision=precision
    )


def halves(x):
    hi = x.astype(BF16)
    return hi, (x - hi.astype(F32)).astype(BF16)


def iota(shape, dim):
    return lax.broadcasted_iota(jnp.int32, shape, dim)


def ranks(row, peers, slab):
    count = row.shape[1]
    chunks = count // 128
    dest = row // slab
    hit = (iota((peers, count), 0) == dest).astype(F32)
    stacked = jnp.concatenate([hit[:, c * 128 : (c + 1) * 128] for c in range(chunks)], axis=0)
    upper = (iota((128, 128), 0) <= iota((128, 128), 1)).astype(BF16)
    inside = jnp.dot(stacked.astype(BF16), upper, preferred_element_type=F32)
    before = jnp.zeros((peers, 1), F32)
    out = []
    for c in range(chunks):
        part = inside[c * peers : (c + 1) * peers]
        mine = hit[:, c * 128 : (c + 1) * 128]
        out.append(jnp.sum(mine * (part + before), axis=0, keepdims=True))
        before = before + part[:, 127:128]
    return jnp.concatenate(out, axis=1).astype(jnp.int32) - 1, dest


def gather_kernel(idx_ref, table_ref, mats_ref, sent_ref, slot_ref, most_ref, hot_ref, *, peers):
    step = pl.program_id(0)
    mode = lax.axis_index("cores")
    leftward = mode < MODES // 2
    slab = N // peers

    @pl.when(step == 0)
    def _():
        row = idx_ref[pl.ds(mode, 1), :]
        count = row.shape[1]
        hot_ref[...] = (iota((N, count), 0) == row).astype(BF16)
        place, dest = ranks(row, peers, slab)
        slot_ref[0:1, :] = place
        slot_ref[1:2, :] = dest
        slot_ref[2:3, :] = row - dest * slab
        slot_ref[3:8, :] = jnp.zeros((5, count), jnp.int32)
        every = idx_ref[...] // slab
        most = jnp.zeros((MODES, 1), F32)
        for j in range(peers):
            most = jnp.maximum(most, jnp.sum((every == j).astype(F32), axis=1, keepdims=True))
        most_ref[...] = jnp.broadcast_to(jnp.max(most, axis=0, keepdims=True), (8, 128))

    hot = hot_ref[...]
    hi, lo = halves(table_ref[...])
    out = dot_rows(hi, hot) + dot_rows(lo, hot)
    mats_ref[...] = out

    @pl.when(jnp.logical_and(leftward, step == 0))
    def _():
        sent_ref[...] = out[0:R]

    @pl.when(jnp.logical_not(leftward))
    def _():
        per = COLS // R
        rows = jnp.concatenate([out[i * R : i * R + 1] for i in range(per)], axis=0)
        sent_ref[pl.ds(pl.multiple_of(step * per, per), per), :] = rows


def times_left(mats_ref, vec_ref, out_ref):
    count = vec_ref.shape[1]

    def chunk(c, _):
        lanes = pl.ds(pl.multiple_of(c * 128, 128), 128)
        acc = [jnp.zeros((R, 128), F32) for _ in range(2)]
        for a in range(R):
            acc[a % 2] = acc[a % 2] + mats_ref[a * R : (a + 1) * R, lanes] * vec_ref[a : a + 1, lanes]
        out_ref[:, lanes] = acc[0] + acc[1]
        return 0

    lax.fori_loop(0, count // 128, chunk, 0)


def times_right(mats_ref, vec_ref, out_ref):
    count = vec_ref.shape[1]

    def chunk(c, _):
        lanes = pl.ds(pl.multiple_of(c * 128, 128), 128)
        vec = vec_ref[:, lanes]
        for a in range(0, R, 8):
            rows = [
                jnp.sum(mats_ref[(a + i) * R : (a + i + 1) * R, lanes] * vec, axis=0, keepdims=True)
                for i in range(8)
            ]
            out_ref[a : a + 8, lanes] = jnp.concatenate(rows, axis=0)
        return 0

    lax.fori_loop(0, count // 128, chunk, 0)


def apply(left, mats_ref, vec_ref, out_ref):
    @pl.when(left)
    def _():
        times_left(mats_ref, vec_ref, out_ref)

    @pl.when(jnp.logical_not(left))
    def _():
        times_right(mats_ref, vec_ref, out_ref)


def hop_kernel(mats_ref, vec_ref, out_ref, *, second):
    mode = lax.axis_index("cores")
    left = (mode >= MODES // 2) if second else (mode < MODES // 2)
    apply(left, mats_ref, vec_ref, out_ref)


def spread(values, slot_ref, most_ref, turn, pay_ref):
    place = slot_ref[0:1, :] - turn * SLOTS
    fits = jnp.logical_and(place >= 0, place < SLOTS)
    key = jnp.where(fits, slot_ref[1:2, :] * SLOTS + place, -1)
    hi, lo = halves(values)
    both = jnp.concatenate([hi, lo], axis=0)
    peers = pay_ref.shape[0]
    count = values.shape[1]
    for pair in range(peers // 2):
        base = pair * 2 * SLOTS
        hot = (iota((2 * SLOTS, count), 0) + base == key).astype(BF16)
        out = dot_lanes(both, hot)
        out = out[:FEATS] + out[FEATS:]
        pay_ref[2 * pair] = out[:, :SLOTS]
        pay_ref[2 * pair + 1] = out[:, SLOTS:]
    for peer in range(peers):
        pay_ref[peer, 97:98, :] = most_ref[0:1, :]


def route_kernel(mats_ref, *refs):
    moved = refs[: MODES - 1]
    obs_ref, slot_ref, most_ref, pay_ref, val_ref, one_ref, two_ref, tmp_ref = refs[MODES - 1 :]
    mode = lax.axis_index("cores")
    early = mode < MODES // 2
    edge = jnp.where(jnp.logical_or(mode == 0, mode == MODES - 1), 1.0, 0.0)
    one = jnp.where(iota(one_ref.shape, 0) == 0, edge, 0.0)
    one_ref[...] = one + ((moved[0][...] + moved[1][...]) + moved[2][...])
    two_ref[...] = (moved[3][...] + moved[4][...]) + (moved[5][...] + moved[6][...])
    apply(jnp.logical_not(early), mats_ref, two_ref, tmp_ref)
    one = one_ref[...]
    two = two_ref[...]
    predicted = jnp.sum(tmp_ref[...] * one, axis=0, keepdims=True)
    residual = predicted - obs_ref[...]
    flag = jnp.where(early, 1.0, 0.0)
    left = jnp.where(flag > 0.5, one, two)
    right = jnp.where(flag > 0.5, two, one) * residual
    count = one.shape[1]
    values = jnp.concatenate(
        [left, right, slot_ref[2:3, :].astype(F32), jnp.zeros((FEATS - 97, count), F32)], axis=0
    )
    val_ref[...] = values
    spread(values, slot_ref, most_ref, 0, pay_ref)


def again_kernel(turn_ref, val_ref, slot_ref, most_ref, pay_ref):
    spread(val_ref[...], slot_ref, most_ref, turn_ref[0], pay_ref)


def collect_kernel(step_ref, recv_ref, base_ref, out_ref, turns_ref):
    peers = recv_ref.shape[0]
    left = jnp.concatenate([recv_ref[s, 0:R, :] for s in range(peers)], axis=1)
    right = jnp.concatenate([recv_ref[s, R : 2 * R, :] for s in range(peers)], axis=1)
    loc = jnp.concatenate([recv_ref[s, 96:97, :] for s in range(peers)], axis=1).astype(jnp.int32)
    row_of = loc // WIDE
    lane_of = loc - row_of * WIDE
    count = loc.shape[1]

    def picked(x, key, n, pad):
        hi = x.astype(BF16).astype(F32)
        lo = x - hi
        tail = [jnp.zeros((pad, count), BF16)] if pad else []
        his, los = [], []
        for i in range(n):
            here = key == i
            his += [jnp.where(here, hi, 0.0).astype(BF16)] + tail
            los += [jnp.where(here, lo, 0.0).astype(BF16)] + tail
        return jnp.concatenate(his, axis=0), jnp.concatenate(los, axis=0)

    xh, xl = picked(left, row_of, GROUPS, 0)
    yh, yl = picked(right, lane_of, WIDE, 16)
    grad = dot_lanes(xh, yh) + (dot_lanes(xh, yl) + dot_lanes(xl, yh))
    out_ref[...] = base_ref[...] - step_ref[0] * grad
    most = jnp.max(recv_ref[:, 97, :]).astype(jnp.int32)
    turns_ref[0] = (most + SLOTS - 1) // SLOTS


def halved(full, parity):
    lane = iota((8, 128), 1)
    even = jnp.where(lane < 80, pltpu.roll(full[16:24], 32, 1), pltpu.roll(full[32:40], 48, 1))
    even = jnp.where(lane < 48, full[0:8], jnp.where(lane < 96, even, 0.0))
    odd = jnp.where(lane < 64, pltpu.roll(full[24:32], 16, 1), pltpu.roll(full[40:48], 24, 1))
    odd = jnp.where(lane < 40, pltpu.roll(full[8:16], 120, 1), jnp.where(lane < 72, odd, 0.0))
    return jnp.where(parity == 0, even, odd)


def whole(even, odd):
    rows = [
        even,
        pltpu.roll(odd, 8, 1),
        pltpu.roll(even, 96, 1),
        pltpu.roll(odd, 112, 1),
        pltpu.roll(even, 80, 1),
        pltpu.roll(odd, 104, 1),
    ]
    full = jnp.concatenate(rows, axis=0)
    block = iota((R, 128), 0) // 8
    lane = iota((R, 128), 1)
    upper = jnp.where(jnp.logical_and(lane >= 8 * block, lane < R), full, 0.0)
    above = jnp.where(lane // 8 > block, upper, 0.0)
    square = jnp.concatenate([above, jnp.zeros((128 - R, 128), F32)], axis=0)
    return upper + square.T[:R]


def gram_kernel(*refs, turn):
    mode = lax.axis_index("cores")
    parity = mode % 2
    if turn == 0:
        own_ref, other_ref, out_ref, prod_ref = refs
    else:
        recv_ref, swap_ref, own_ref, other_ref, out_ref, sum_ref, prod_ref = refs
    mine = jnp.where(parity == turn % 2, 1.0, 0.0)
    core = jnp.where(mine > 0.5, own_ref[...], other_ref[...])
    if turn == 0:
        prod = core
    else:
        one = jnp.sum(recv_ref[...], axis=0)
        two = jnp.sum(swap_ref[...], axis=0)
        even = jnp.where(parity == 0, one, two)
        odd = jnp.where(parity == 0, two, one)
        sum_ref[0:8] = even
        sum_ref[8:16] = odd
        before = whole(even, odd)[:, :R]
        for g in range(GROUPS):
            prod_ref[g * R : (g + 1) * R, :] = jnp.dot(
                before, core[g * R : (g + 1) * R], preferred_element_type=F32, precision=HIGH
            )
        prod = prod_ref[...]
    even = jnp.zeros((64, 128), F32)
    odd = jnp.zeros((64, 128), F32)
    for part in range(2):
        z = lax.dot_general(
            core[:, part * 128 : (part + 1) * 128],
            prod[:, part * 128 : (part + 1) * 128],
            (((0,), (0,)), ((), ())),
            preferred_element_type=F32,
            precision=HIGH,
        )
        even = even + z[0:64]
        odd = odd + z[64:128]
    live = jnp.where(mode // 2 == turn // 2, 1.0 / N, 0.0)
    half = halved((even + pltpu.roll(odd, 64, 1)) * live, parity)
    for peer in range(out_ref.shape[0]):
        out_ref[peer] = half


def final_kernel(*refs):
    sums = refs[: MODES - 2]
    recv_ref, swap_ref, own_ref, out_ref, prod_ref, block_ref = refs[MODES - 2 :]
    mode = lax.axis_index("cores")
    parity = mode % 2
    one = jnp.sum(recv_ref[...], axis=0)
    two = jnp.sum(swap_ref[...], axis=0)
    last = jnp.concatenate([jnp.where(parity == 0, one, two), jnp.where(parity == 0, two, one)], axis=0)
    every = [s[...] for s in sums] + [last]
    own = jnp.zeros((16, 128), F32)
    prev = jnp.zeros((16, 128), F32)
    for t in range(MODES - 1):
        own = own + every[t] * jnp.where(mode == t, 1.0, 0.0)
        prev = prev + every[t] * jnp.where(mode == t + 1, 1.0, 0.0)
    row = iota((R, 128), 0)
    lane = iota((R, 128), 1)
    eye = jnp.where(lane == row, 1.0, 0.0)
    side = jnp.where(lane == row + 64, 1.0, 0.0)

    def start(packed, absent):
        return whole(packed[0:8], packed[8:16]) + eye * absent + side

    mats = [
        start(own, jnp.where(mode == MODES - 1, 1.0, 0.0)),
        start(prev, jnp.where(mode == 0, 1.0, 0.0)),
    ]
    for j in range(R):
        for w in range(2):
            m = mats[w]
            pivot = m[j : j + 1, :]
            scale = 1.0 / m[j : j + 1, j : j + 1]
            col = jnp.where(row[:, 0:1] > j, m[:, j : j + 1] * scale, 0.0)
            mats[w] = m - col * pivot
    tri = []
    for w in range(2):
        diag = jnp.sum(jnp.where(lane == row, mats[w], 0.0), axis=1, keepdims=True)
        tri.append(mats[w] * (1.0 / jnp.sqrt(diag)))
    carry = tri[1][:, :R]
    inv = jnp.where(lane >= 64, tri[0], 0.0)
    turned = pltpu.roll(inv, 64, 1)
    block_ref[...] = jnp.zeros((LANES, LANES), F32)
    for h in range(WIDE):
        block_ref[h * 64 : h * 64 + R, (h // 2) * 128 : (h // 2 + 1) * 128] = inv if h % 2 else turned
    for g in range(GROUPS):
        prod_ref[g * R : (g + 1) * R, :] = jnp.dot(
            carry, own_ref[g * R : (g + 1) * R, :], preferred_element_type=F32, precision=HIGH
        )
    out_ref[...] = dot_lanes(prod_ref[...], block_ref[...], HIGH)


def vmem():
    return pl.BlockSpec(memory_space=pltpu.VMEM)


def smem():
    return pl.BlockSpec(memory_space=pltpu.SMEM)


def call(kernel, outs, ins, scratch=(), name=None):
    return pl.pallas_call(
        kernel,
        out_shape=outs,
        in_specs=ins,
        out_specs=jax.tree.map(lambda o: smem() if o.dtype == jnp.int32 and o.size == 1 else vmem(), outs),
        scratch_shapes=list(scratch),
        compiler_params=pltpu.CompilerParams(vmem_limit_bytes=BIG),
        name=name,
    )


def shape(*dims, dtype=F32):
    return jax.ShapeDtypeStruct(dims, dtype)


def on_device(cores, indices, observed, step_size):
    peers = lax.axis_size("samp")
    count = indices.shape[0]
    slab = N // peers
    table = cores[0]
    idx = indices.T
    step = step_size.reshape(1)

    mats, sent, slot, most = pl.pallas_call(
        functools.partial(gather_kernel, peers=peers),
        grid=(RR // COLS,),
        in_specs=[
            pl.BlockSpec((MODES, count), lambda i: (0, 0)),
            pl.BlockSpec((N, COLS), lambda i: (0, i)),
        ],
        out_specs=[
            pl.BlockSpec((COLS, count), lambda i: (i, 0)),
            pl.BlockSpec((R, count), lambda i: (0, 0)),
            pl.BlockSpec((8, count), lambda i: (0, 0)),
            pl.BlockSpec((8, 128), lambda i: (0, 0)),
        ],
        out_shape=[shape(RR, count), shape(R, count), shape(8, count, dtype=jnp.int32), shape(8, 128)],
        scratch_shapes=[pltpu.VMEM((N, count), BF16)],
        compiler_params=pltpu.CompilerParams(vmem_limit_bytes=BIG),
        name="gather",
    )(idx, pltpu.with_memory_space_constraint(table, pltpu.HBM))

    first = lax.axis_index("samp") * slab
    kept = lax.dynamic_slice_in_dim(table, first, slab, 0)
    base = kept.reshape(GROUPS, WIDE, R, R).transpose(0, 2, 1, 3)
    base = jnp.pad(base, ((0, 0), (0, 0), (0, 0), (0, 64 - R))).reshape(ROWS, LANES)

    every = []
    for turn in range(MODES - 1):
        if turn > 0:
            sent = call(
                functools.partial(hop_kernel, second=turn >= MODES // 2),
                shape(R, count),
                [vmem(), vmem()],
                name=f"hop{turn}",
            )(mats, moved)
        moved = lax.ppermute(sent, "cores", [(turn, turn + 1), (7 - turn, 6 - turn)])
        every.append(moved)

    pay, values = call(
        route_kernel,
        (shape(peers, FEATS, SLOTS), shape(FEATS, count)),
        [vmem()] * (MODES + 3),
        [pltpu.VMEM((R, count), F32)] * 3,
        name="route",
    )(mats, *every, observed.reshape(1, count), slot, most)

    def exchanged(block):
        return lax.all_to_all(block, "samp", 0, 0, tiled=True)

    def collected(recv, so_far):
        return call(
            collect_kernel,
            (shape(ROWS, LANES), shape(1, dtype=jnp.int32)),
            [smem(), vmem(), vmem()],
            name="collect",
        )(step, recv, so_far)

    updated, turns = collected(exchanged(pay), base)

    def more(state):
        return state[0] < turns[0]

    def another(state):
        turn, so_far = state
        pay = call(
            again_kernel,
            shape(peers, FEATS, SLOTS),
            [smem(), vmem(), vmem(), vmem()],
            name="again",
        )(turn.reshape(1), values, slot, most)
        return turn + 1, collected(exchanged(pay), so_far)[0]

    _, updated = lax.while_loop(more, another, (jnp.int32(1), updated))

    siblings = [(i, i ^ 1) for i in range(MODES)]
    other = lax.ppermute(updated, "cores", siblings)

    sums = []
    recv = None
    for turn in range(MODES - 1):
        odd = turn % 2 == 1
        size = 2 * peers if odd else peers
        outs = [shape(size, 8, 128)] + ([shape(16, 128)] if turn else [])
        res = call(
            functools.partial(gram_kernel, turn=turn),
            outs,
            [vmem()] * (2 if turn == 0 else 4),
            [pltpu.VMEM((ROWS, LANES), F32)],
            name=f"gram{turn}",
        )(*([] if turn == 0 else [recv, swap]), updated, other)
        if turn:
            sums.append(res[1])
        if odd:
            here = turn // 2
            groups = []
            for c in (here, here + 2):
                for h in range(2):
                    pair = [(2 * (c % 4) + h), (2 * ((c + 1) % 4) + h)]
                    groups.append([m * peers + j for m in pair for j in range(peers)])
            recv = lax.all_to_all(
                res[0], ("cores", "samp"), 0, 0, axis_index_groups=groups, tiled=True
            )
        else:
            recv = lax.all_to_all(res[0], "samp", 0, 0, tiled=True)
        swap = lax.ppermute(recv, "cores", siblings)

    out = call(
        final_kernel,
        shape(ROWS, LANES),
        [vmem()] * (MODES + 1),
        [pltpu.VMEM((ROWS, LANES), F32), pltpu.VMEM((LANES, LANES), F32)],
        name="final",
    )(*sums, recv, swap, updated)
    out = out.reshape(GROUPS, R, WIDE, 64)[..., :R].transpose(0, 2, 1, 3)
    return out.reshape(1, slab, RR)


def solution(mesh):
    in_specs = (P("cores", None, None), P("samp", None), P("samp"), P())
    out_specs = P("cores", "samp", None)
    return jax.shard_map(
        on_device, mesh=mesh, in_specs=in_specs, out_specs=out_specs, check_vma=False
    )
```

```python
import functools

import jax
import jax.numpy as jnp
from jax import lax
from jax.experimental import pallas as pl
from jax.experimental.pallas import tpu as pltpu
from jax.sharding import PartitionSpec as P

R = 48
N = 512
MODES = 8
RR = R * R
GROUPS = 4
WIDE = 8
ROWS = GROUPS * R
LANES = WIDE * R
FEATS = 104
SLOTS = 128
WAYS = 4
HIGH = lax.Precision.HIGHEST
F32 = jnp.float32
BF16 = jnp.bfloat16
COLS = 384
BIG = 14 << 20


def dot_rows(a, b):
    return lax.dot_general(a, b, (((0,), (0,)), ((), ())), preferred_element_type=F32)


def dot_lanes(a, b, precision=None):
    return lax.dot_general(
        a, b, (((1,), (1,)), ((), ())), preferred_element_type=F32, precision=precision
    )


def halves(x):
    hi = x.astype(BF16)
    return hi, (x - hi.astype(F32)).astype(BF16)


def iota(shape, dim):
    return lax.broadcasted_iota(jnp.int32, shape, dim)


def ranks(row, peers, slab):
    count = row.shape[1]
    chunks = count // 128
    dest = row // slab
    hit = (iota((peers, count), 0) == dest).astype(F32)
    stacked = jnp.concatenate([hit[:, c * 128 : (c + 1) * 128] for c in range(chunks)], axis=0)
    upper = (iota((128, 128), 0) <= iota((128, 128), 1)).astype(BF16)
    inside = jnp.dot(stacked.astype(BF16), upper, preferred_element_type=F32)
    before = jnp.zeros((peers, 1), F32)
    out = []
    for c in range(chunks):
        part = inside[c * peers : (c + 1) * peers]
        mine = hit[:, c * 128 : (c + 1) * 128]
        out.append(jnp.sum(mine * (part + before), axis=0, keepdims=True))
        before = before + part[:, 127:128]
    return jnp.concatenate(out, axis=1).astype(jnp.int32) - 1, dest


def gather_kernel(idx_ref, table_ref, mats_ref, sent_ref, slot_ref, most_ref, hot_ref, *, peers):
    step = pl.program_id(0)
    mode = lax.axis_index("cores")
    leftward = mode < MODES // 2
    slab = N // peers

    @pl.when(step == 0)
    def _():
        row = idx_ref[pl.ds(mode, 1), :]
        count = row.shape[1]
        hot_ref[...] = (iota((N, count), 0) == row).astype(BF16)
        place, dest = ranks(row, peers, slab)
        slot_ref[0:1, :] = place
        slot_ref[1:2, :] = dest
        slot_ref[2:3, :] = row - dest * slab
        slot_ref[3:8, :] = jnp.zeros((5, count), jnp.int32)
        every = idx_ref[...] // slab
        most = jnp.zeros((MODES, 1), F32)
        for j in range(peers):
            most = jnp.maximum(most, jnp.sum((every == j).astype(F32), axis=1, keepdims=True))
        most_ref[...] = jnp.broadcast_to(jnp.max(most, axis=0, keepdims=True), (8, 128))

    hot = hot_ref[...]
    hi, lo = halves(table_ref[...])
    out = dot_rows(hi, hot) + dot_rows(lo, hot)
    mats_ref[...] = out

    @pl.when(jnp.logical_and(leftward, step == 0))
    def _():
        sent_ref[...] = out[0:R]

    @pl.when(jnp.logical_not(leftward))
    def _():
        per = COLS // R
        rows = jnp.concatenate([out[i * R : i * R + 1] for i in range(per)], axis=0)
        sent_ref[pl.ds(pl.multiple_of(step * per, per), per), :] = rows


def times_left(mats_ref, vec_ref, out_ref):
    count = vec_ref.shape[1]

    def chunk(c, _):
        lanes = pl.ds(pl.multiple_of(c * 128, 128), 128)
        acc = [jnp.zeros((R, 128), F32) for _ in range(2)]
        for a in range(R):
            acc[a % 2] = acc[a % 2] + mats_ref[a * R : (a + 1) * R, lanes] * vec_ref[a : a + 1, lanes]
        out_ref[:, lanes] = acc[0] + acc[1]
        return 0

    lax.fori_loop(0, count // 128, chunk, 0)


def times_right(mats_ref, vec_ref, out_ref):
    count = vec_ref.shape[1]

    def chunk(c, _):
        lanes = pl.ds(pl.multiple_of(c * 128, 128), 128)
        vec = vec_ref[:, lanes]
        for a in range(0, R, 8):
            rows = [
                jnp.sum(mats_ref[(a + i) * R : (a + i + 1) * R, lanes] * vec, axis=0, keepdims=True)
                for i in range(8)
            ]
            out_ref[a : a + 8, lanes] = jnp.concatenate(rows, axis=0)
        return 0

    lax.fori_loop(0, count // 128, chunk, 0)


def apply(left, mats_ref, vec_ref, out_ref):
    @pl.when(left)
    def _():
        times_left(mats_ref, vec_ref, out_ref)

    @pl.when(jnp.logical_not(left))
    def _():
        times_right(mats_ref, vec_ref, out_ref)


def hop_kernel(mats_ref, vec_ref, out_ref, *, second):
    mode = lax.axis_index("cores")
    left = (mode >= MODES // 2) if second else (mode < MODES // 2)
    apply(left, mats_ref, vec_ref, out_ref)


def spread(values, slot_ref, most_ref, turn, pay_ref):
    place = slot_ref[0:1, :] - turn * SLOTS
    fits = jnp.logical_and(place >= 0, place < SLOTS)
    key = jnp.where(fits, slot_ref[1:2, :] * SLOTS + place, -1)
    hi, lo = halves(values)
    both = jnp.concatenate([hi, lo], axis=0)
    peers = pay_ref.shape[0]
    count = values.shape[1]
    for pair in range(peers // 2):
        base = pair * 2 * SLOTS
        hot = (iota((2 * SLOTS, count), 0) + base == key).astype(BF16)
        out = dot_lanes(both, hot)
        out = out[:FEATS] + out[FEATS:]
        pay_ref[2 * pair] = out[:, :SLOTS]
        pay_ref[2 * pair + 1] = out[:, SLOTS:]
    for peer in range(peers):
        pay_ref[peer, 97:98, :] = most_ref[0:1, :]


def route_kernel(mats_ref, *refs):
    moved = refs[: MODES - 1]
    obs_ref, slot_ref, most_ref, pay_ref, val_ref, one_ref, two_ref, tmp_ref = refs[MODES - 1 :]
    mode = lax.axis_index("cores")
    early = mode < MODES // 2
    edge = jnp.where(jnp.logical_or(mode == 0, mode == MODES - 1), 1.0, 0.0)
    one = jnp.where(iota(one_ref.shape, 0) == 0, edge, 0.0)
    one_ref[...] = one + ((moved[0][...] + moved[1][...]) + moved[2][...])
    two_ref[...] = (moved[3][...] + moved[4][...]) + (moved[5][...] + moved[6][...])
    apply(jnp.logical_not(early), mats_ref, two_ref, tmp_ref)
    one = one_ref[...]
    two = two_ref[...]
    predicted = jnp.sum(tmp_ref[...] * one, axis=0, keepdims=True)
    residual = predicted - obs_ref[...]
    flag = jnp.where(early, 1.0, 0.0)
    left = jnp.where(flag > 0.5, one, two)
    right = jnp.where(flag > 0.5, two, one) * residual
    count = one.shape[1]
    values = jnp.concatenate(
        [left, right, slot_ref[2:3, :].astype(F32), jnp.zeros((FEATS - 97, count), F32)], axis=0
    )
    val_ref[...] = values
    spread(values, slot_ref, most_ref, 0, pay_ref)


def again_kernel(turn_ref, val_ref, slot_ref, most_ref, pay_ref):
    spread(val_ref[...], slot_ref, most_ref, turn_ref[0], pay_ref)


def collect_kernel(step_ref, recv_ref, base_ref, out_ref, turns_ref):
    peers = recv_ref.shape[0]
    left = jnp.concatenate([recv_ref[s, 0:R, :] for s in range(peers)], axis=1)
    right = jnp.concatenate([recv_ref[s, R : 2 * R, :] for s in range(peers)], axis=1)
    loc = jnp.concatenate([recv_ref[s, 96:97, :] for s in range(peers)], axis=1).astype(jnp.int32)
    row_of = loc // WIDE
    lane_of = loc - row_of * WIDE
    count = loc.shape[1]

    def picked(x, key, n):
        hi = x.astype(BF16).astype(F32)
        lo = x - hi
        his, los = [], []
        for i in range(n):
            here = key == i
            his += [jnp.where(here, hi, 0.0).astype(BF16)]
            los += [jnp.where(here, lo, 0.0).astype(BF16)]
        return jnp.concatenate(his, axis=0), jnp.concatenate(los, axis=0)

    xh, xl = picked(left, row_of, GROUPS)
    yh, yl = picked(right, lane_of, WIDE)
    grad = dot_lanes(xh, yh) + (dot_lanes(xh, yl) + dot_lanes(xl, yh))
    out_ref[...] = base_ref[...] - step_ref[0] * grad
    most = jnp.max(recv_ref[:, 97, :]).astype(jnp.int32)
    turns_ref[0] = (most + SLOTS - 1) // SLOTS


def arrange_kernel(*refs):
    own = refs[:WAYS]
    other = refs[WAYS : 2 * WAYS]
    outs = refs[2 * WAYS :]
    even_first = jnp.where(lax.axis_index("cores") % 2 == 0, 1.0, 0.0)
    for w in range(WAYS):
        rows = slice(w * ROWS, (w + 1) * ROWS)
        mine = own[w][...]
        theirs = other[w][...]
        for k in range(2):
            flag = even_first if k == 0 else 1.0 - even_first
            core = jnp.where(flag > 0.5, mine, theirs)
            outs[4 * k][rows, :], outs[4 * k + 1][rows, :] = halves(core)
            outs[4 * k + 2][:, rows], outs[4 * k + 3][:, rows] = halves(core.T)


def three(a, b):
    (ah, al), (bh, bl) = a, b
    mul = functools.partial(jnp.dot, preferred_element_type=F32)
    return mul(ah, bh) + (mul(ah, bl) + mul(al, bh))


def packed_of(full):
    lane = iota((24, 128), 1)
    return jnp.where(lane < 64, full[0:24], pltpu.roll(full[24:48], 64, 1))


def whole(packed):
    both = jnp.concatenate([packed, pltpu.roll(packed, 64, 1)], axis=0)
    return jnp.where(iota((R, 128), 1) < R, both, 0.0)


def pulled(before, core, prod_ref):
    high, low, high_t, low_t = core
    if before is None:
        prod = (high[...], low[...])
    else:
        weights = halves(before[:, :R])
        for g in range(WAYS * GROUPS):
            rows = slice(g * R, (g + 1) * R)
            prod_ref[rows, :] = three(weights, (high[rows, :], low[rows, :]))
        prod = halves(prod_ref[...])
    total = jnp.zeros((R, 256), F32)
    for part, slices in ((0, range(5)), (128, range(5, WIDE))):
        cols = slice(part, part + 256)
        z = three((high_t[cols, :], low_t[cols, :]), (prod[0][:, cols], prod[1][:, cols]))
        for h in slices:
            at = h * R - part
            block = z[at : at + R]
            total = total + (pltpu.roll(block, 256 - at, 1) if at else block)
    return jnp.where(iota((R, 128), 1) < R, total[:, :128], 0.0) * (1.0 / N)


def pair_kernel(*refs, pair):
    last = pair == MODES // 2 - 1
    refs = list(refs)
    recv_ref = refs.pop(0) if pair else None
    saved = [refs.pop(0) for _ in range(pair)] if last else []
    even = [refs.pop(0) for _ in range(4)]
    odd = None if last else [refs.pop(0) for _ in range(4)]
    prod_ref = refs.pop()
    if pair:
        sum_ref = refs.pop()
        arrived = jnp.sum(recv_ref[...], axis=0)
        sum_ref[...] = arrived
        before = whole(arrived)
    else:
        before = None
    chip = lax.axis_index("cores") // 2
    live = jnp.where(chip == pair, 1.0, 0.0)
    middle = pulled(before, even, prod_ref) * live
    kept = packed_of(middle)
    if last:
        for s in saved:
            kept = kept + s[...]
        refs[0][...] = kept
        return
    out_ref, save_ref = refs
    save_ref[...] = kept
    packed = packed_of(pulled(middle, odd, prod_ref))
    for peer in range(out_ref.shape[0]):
        out_ref[peer] = packed


def final_kernel(*refs):
    pairs = MODES // 2 - 1
    sums = refs[:pairs]
    parts = refs[pairs : pairs + WAYS]
    own_ref, out_ref, prod_ref, block_ref = refs[pairs + WAYS :]
    mode = lax.axis_index("cores")
    chip = mode // 2
    first = jnp.where(mode % 2 == 0, 1.0, 0.0)
    second = 1.0 - first
    level = (parts[0][...] + parts[1][...]) + (parts[2][...] + parts[3][...])
    own = level * first
    prev = level * second
    for p in range(pairs):
        own = own + sums[p][...] * jnp.where(chip == p, second, 0.0)
        prev = prev + sums[p][...] * jnp.where(chip == p + 1, first, 0.0)
    row = iota((R, 128), 0)
    lane = iota((R, 128), 1)
    eye = jnp.where(lane == row, 1.0, 0.0)
    side = jnp.where(lane == row + 64, 1.0, 0.0)

    def start(packed, absent):
        return whole(packed) + eye * absent + side

    mats = [
        start(own, jnp.where(mode == MODES - 1, 1.0, 0.0)),
        start(prev, jnp.where(mode == 0, 1.0, 0.0)),
    ]
    for j in range(R):
        for w in range(2):
            m = mats[w]
            pivot = m[j : j + 1, :]
            scale = 1.0 / m[j : j + 1, j : j + 1]
            col = jnp.where(row[:, 0:1] > j, m[:, j : j + 1] * scale, 0.0)
            mats[w] = m - col * pivot
    tri = []
    for w in range(2):
        diag = jnp.sum(jnp.where(lane == row, mats[w], 0.0), axis=1, keepdims=True)
        tri.append(mats[w] * (1.0 / jnp.sqrt(diag)))
    carry = tri[1][:, :R]
    inv = jnp.where(lane >= 64, tri[0], 0.0)
    turned = pltpu.roll(inv, 64, 1)
    wide = jnp.concatenate([jnp.where(lane < R, turned, 0.0), jnp.zeros((R, LANES - 128), F32)], axis=1)
    for h in range(WIDE):
        block_ref[h * R : (h + 1) * R, :] = pltpu.roll(wide, h * R, 1) if h else wide
    for g in range(GROUPS):
        prod_ref[g * R : (g + 1) * R, :] = jnp.dot(
            carry, own_ref[g * R : (g + 1) * R, :], preferred_element_type=F32, precision=HIGH
        )
    out_ref[...] = dot_lanes(prod_ref[...], block_ref[...], HIGH)


def vmem():
    return pl.BlockSpec(memory_space=pltpu.VMEM)


def smem():
    return pl.BlockSpec(memory_space=pltpu.SMEM)


def call(kernel, outs, ins, scratch=(), name=None):
    return pl.pallas_call(
        kernel,
        out_shape=outs,
        in_specs=ins,
        out_specs=jax.tree.map(lambda o: smem() if o.dtype == jnp.int32 and o.size == 1 else vmem(), outs),
        scratch_shapes=list(scratch),
        compiler_params=pltpu.CompilerParams(vmem_limit_bytes=BIG),
        name=name,
    )


def shape(*dims, dtype=F32):
    return jax.ShapeDtypeStruct(dims, dtype)


def on_device(cores, indices, observed, step_size):
    peers = lax.axis_size("samp")
    count = indices.shape[0]
    slab = N // peers
    table = cores[0]
    idx = indices.T
    step = step_size.reshape(1)

    mats, sent, slot, most = pl.pallas_call(
        functools.partial(gather_kernel, peers=peers),
        grid=(RR // COLS,),
        in_specs=[
            pl.BlockSpec((MODES, count), lambda i: (0, 0)),
            pl.BlockSpec((N, COLS), lambda i: (0, i)),
        ],
        out_specs=[
            pl.BlockSpec((COLS, count), lambda i: (i, 0)),
            pl.BlockSpec((R, count), lambda i: (0, 0)),
            pl.BlockSpec((8, count), lambda i: (0, 0)),
            pl.BlockSpec((8, 128), lambda i: (0, 0)),
        ],
        out_shape=[shape(RR, count), shape(R, count), shape(8, count, dtype=jnp.int32), shape(8, 128)],
        scratch_shapes=[pltpu.VMEM((N, count), BF16)],
        compiler_params=pltpu.CompilerParams(vmem_limit_bytes=BIG),
        name="gather",
    )(idx, pltpu.with_memory_space_constraint(table, pltpu.HBM))

    first = lax.axis_index("samp") * slab
    kept = lax.dynamic_slice_in_dim(table, first, slab, 0)
    base = kept.reshape(GROUPS, WIDE, R, R).transpose(0, 2, 1, 3)
    base = base.reshape(ROWS, LANES)

    every = []
    for turn in range(MODES - 1):
        if turn > 0:
            sent = call(
                functools.partial(hop_kernel, second=turn >= MODES // 2),
                shape(R, count),
                [vmem(), vmem()],
                name=f"hop{turn}",
            )(mats, moved)
        moved = lax.ppermute(sent, "cores", [(turn, turn + 1), (7 - turn, 6 - turn)])
        every.append(moved)

    pay, values = call(
        route_kernel,
        (shape(peers, FEATS, SLOTS), shape(FEATS, count)),
        [vmem()] * (MODES + 3),
        [pltpu.VMEM((R, count), F32)] * 3,
        name="route",
    )(mats, *every, observed.reshape(1, count), slot, most)

    def exchanged(block):
        return lax.all_to_all(block, "samp", 0, 0, tiled=True)

    def collected(recv, so_far):
        return call(
            collect_kernel,
            (shape(ROWS, LANES), shape(1, dtype=jnp.int32)),
            [smem(), vmem(), vmem()],
            name="collect",
        )(step, recv, so_far)

    updated, turns = collected(exchanged(pay), base)

    def more(state):
        return state[0] < turns[0]

    def another(state):
        turn, so_far = state
        pay = call(
            again_kernel,
            shape(peers, FEATS, SLOTS),
            [smem(), vmem(), vmem(), vmem()],
            name="again",
        )(turn.reshape(1), values, slot, most)
        return turn + 1, collected(exchanged(pay), so_far)[0]

    _, updated = lax.while_loop(more, another, (jnp.int32(1), updated))

    side = int(peers**0.5)

    def along(mode, peer, by):
        z, x = peer // side, peer % side
        return z * side + (x + by) % side if mode % 2 == 0 else (z + by) % side * side + x

    ring = [
        [(m * peers + p, m * peers + along(m, p, by)) for m in range(MODES) for p in range(peers)]
        for by in range(1, side)
    ]
    level = [[(p, along(1, p, by)) for p in range(peers)] for by in range(1, side)]
    siblings = [(m, m ^ 1) for m in range(MODES)]
    own = [updated] + [lax.ppermute(updated, ("cores", "samp"), pairs) for pairs in ring]
    other = [lax.ppermute(o, "cores", siblings) for o in own]
    tall = shape(WAYS * ROWS, LANES, dtype=BF16)
    flat = shape(LANES, WAYS * ROWS, dtype=BF16)
    arranged = call(arrange_kernel, [tall, tall, flat, flat] * 2, [vmem()] * 8, name="arrange")(*own, *other)
    even, odd = list(arranged[:4]), list(arranged[4:])

    saved, sums = [], []
    recv = None
    for pair in range(MODES // 2):
        last = pair == MODES // 2 - 1
        ins = ([recv] if pair else []) + (saved if last else []) + even + ([] if last else odd)
        outs = [shape(24, 128)] if last else [shape(2 * peers, 24, 128), shape(24, 128)]
        if pair:
            outs.append(shape(24, 128))
        res = call(
            functools.partial(pair_kernel, pair=pair),
            outs,
            [vmem()] * len(ins),
            [pltpu.VMEM((WAYS * ROWS, LANES), F32)],
            name=f"pair{pair}",
        )(*ins)
        if pair:
            sums.append(res[-1])
        if last:
            parts = [res[0]] + [lax.ppermute(res[0], "samp", pairs) for pairs in level]
        else:
            saved.append(res[1])
            groups = []
            for c in (pair, pair + 2):
                for h in range(2):
                    both = [2 * (c % 4) + h, 2 * ((c + 1) % 4) + h]
                    groups.append([m * peers + j for m in both for j in range(peers)])
            recv = lax.all_to_all(
                res[0], ("cores", "samp"), 0, 0, axis_index_groups=groups, tiled=True
            )

    out = call(
        final_kernel,
        shape(ROWS, LANES),
        [vmem()] * (MODES // 2 - 1 + WAYS + 1),
        [pltpu.VMEM((ROWS, LANES), F32), pltpu.VMEM((LANES, LANES), F32)],
        name="final",
    )(*sums, *parts, updated)
    out = out.reshape(GROUPS, R, WIDE, R).transpose(0, 2, 1, 3)
    return out.reshape(1, slab, RR)


def solution(mesh):
    in_specs = (P("cores", None, None), P("samp", None), P("samp"), P())
    out_specs = P("cores", "samp", None)
    return jax.shard_map(
        on_device, mesh=mesh, in_specs=in_specs, out_specs=out_specs, check_vma=False
    )
```

```python
import functools

import jax
import jax.numpy as jnp
from jax import lax
from jax.experimental import pallas as pl
from jax.experimental.pallas import tpu as pltpu
from jax.sharding import PartitionSpec as P

R = 48
N = 512
MODES = 8
RR = R * R
GROUPS = 4
WIDE = 8
ROWS = GROUPS * R
LANES = WIDE * R
FEATS = 104
SLOTS = 128
WAYS = 4
HIGH = lax.Precision.HIGHEST
F32 = jnp.float32
BF16 = jnp.bfloat16
COLS = 384
BIG = 14 << 20


def dot_rows(a, b):
    return lax.dot_general(a, b, (((0,), (0,)), ((), ())), preferred_element_type=F32)


def dot_lanes(a, b, precision=None):
    return lax.dot_general(
        a, b, (((1,), (1,)), ((), ())), preferred_element_type=F32, precision=precision
    )


def halves(x):
    hi = x.astype(BF16)
    return hi, (x - hi.astype(F32)).astype(BF16)


def iota(shape, dim):
    return lax.broadcasted_iota(jnp.int32, shape, dim)


def ranks(row, peers, slab):
    count = row.shape[1]
    chunks = count // 128
    dest = row // slab
    hit = (iota((peers, count), 0) == dest).astype(F32)
    stacked = jnp.concatenate([hit[:, c * 128 : (c + 1) * 128] for c in range(chunks)], axis=0)
    upper = (iota((128, 128), 0) <= iota((128, 128), 1)).astype(BF16)
    inside = jnp.dot(stacked.astype(BF16), upper, preferred_element_type=F32)
    before = jnp.zeros((peers, 1), F32)
    out = []
    for c in range(chunks):
        part = inside[c * peers : (c + 1) * peers]
        mine = hit[:, c * 128 : (c + 1) * 128]
        out.append(jnp.sum(mine * (part + before), axis=0, keepdims=True))
        before = before + part[:, 127:128]
    return jnp.concatenate(out, axis=1).astype(jnp.int32) - 1, dest


def gather_kernel(idx_ref, table_ref, mats_ref, sent_ref, slot_ref, most_ref, hot_ref, *, peers):
    step = pl.program_id(0)
    mode = lax.axis_index("cores")
    leftward = mode < MODES // 2
    slab = N // peers

    @pl.when(step == 0)
    def _():
        row = idx_ref[pl.ds(mode, 1), :]
        count = row.shape[1]
        hot_ref[...] = (iota((N, count), 0) == row).astype(BF16)
        place, dest = ranks(row, peers, slab)
        slot_ref[0:1, :] = place
        slot_ref[1:2, :] = dest
        slot_ref[2:3, :] = row - dest * slab
        slot_ref[3:8, :] = jnp.zeros((5, count), jnp.int32)
        every = idx_ref[...] // slab
        most = jnp.zeros((MODES, 1), F32)
        for j in range(peers):
            most = jnp.maximum(most, jnp.sum((every == j).astype(F32), axis=1, keepdims=True))
        most_ref[...] = jnp.broadcast_to(jnp.max(most, axis=0, keepdims=True), (8, 128))

    hot = hot_ref[...]
    hi, lo = halves(table_ref[...])
    out = dot_rows(hi, hot) + dot_rows(lo, hot)
    mats_ref[...] = out

    @pl.when(jnp.logical_and(leftward, step == 0))
    def _():
        sent_ref[...] = out[0:R]

    @pl.when(jnp.logical_not(leftward))
    def _():
        per = COLS // R
        rows = jnp.concatenate([out[i * R : i * R + 1] for i in range(per)], axis=0)
        sent_ref[pl.ds(pl.multiple_of(step * per, per), per), :] = rows


def times_left(mats_ref, vec_ref, out_ref):
    count = vec_ref.shape[1]

    def chunk(c, _):
        lanes = pl.ds(pl.multiple_of(c * 128, 128), 128)
        acc = [jnp.zeros((R, 128), F32) for _ in range(2)]
        for a in range(R):
            acc[a % 2] = acc[a % 2] + mats_ref[a * R : (a + 1) * R, lanes] * vec_ref[a : a + 1, lanes]
        out_ref[:, lanes] = acc[0] + acc[1]
        return 0

    lax.fori_loop(0, count // 128, chunk, 0)


def times_right(mats_ref, vec_ref, out_ref):
    count = vec_ref.shape[1]

    def chunk(c, _):
        lanes = pl.ds(pl.multiple_of(c * 128, 128), 128)
        vec = vec_ref[:, lanes]
        for a in range(0, R, 8):
            rows = [
                jnp.sum(mats_ref[(a + i) * R : (a + i + 1) * R, lanes] * vec, axis=0, keepdims=True)
                for i in range(8)
            ]
            out_ref[a : a + 8, lanes] = jnp.concatenate(rows, axis=0)
        return 0

    lax.fori_loop(0, count // 128, chunk, 0)


def apply(left, mats_ref, vec_ref, out_ref):
    @pl.when(left)
    def _():
        times_left(mats_ref, vec_ref, out_ref)

    @pl.when(jnp.logical_not(left))
    def _():
        times_right(mats_ref, vec_ref, out_ref)


def hop_kernel(mats_ref, vec_ref, out_ref, *, second):
    mode = lax.axis_index("cores")
    left = (mode >= MODES // 2) if second else (mode < MODES // 2)
    apply(left, mats_ref, vec_ref, out_ref)


def spread(values, slot_ref, most_ref, turn, pay_ref):
    place = slot_ref[0:1, :] - turn * SLOTS
    fits = jnp.logical_and(place >= 0, place < SLOTS)
    key = jnp.where(fits, slot_ref[1:2, :] * SLOTS + place, -1)
    hi, lo = halves(values)
    both = jnp.concatenate([hi, lo], axis=0)
    peers = pay_ref.shape[0]
    count = values.shape[1]
    for pair in range(peers // 2):
        base = pair * 2 * SLOTS
        hot = (iota((2 * SLOTS, count), 0) + base == key).astype(BF16)
        out = dot_lanes(both, hot)
        out = out[:FEATS] + out[FEATS:]
        pay_ref[2 * pair] = out[:, :SLOTS]
        pay_ref[2 * pair + 1] = out[:, SLOTS:]
    for peer in range(peers):
        pay_ref[peer, 97:98, :] = most_ref[0:1, :]


def route_kernel(mats_ref, *refs):
    moved = refs[: MODES - 1]
    obs_ref, slot_ref, most_ref, pay_ref, val_ref, one_ref, two_ref, tmp_ref = refs[MODES - 1 :]
    mode = lax.axis_index("cores")
    early = mode < MODES // 2
    edge = jnp.where(jnp.logical_or(mode == 0, mode == MODES - 1), 1.0, 0.0)
    one = jnp.where(iota(one_ref.shape, 0) == 0, edge, 0.0)
    one_ref[...] = one + ((moved[0][...] + moved[1][...]) + moved[2][...])
    two_ref[...] = (moved[3][...] + moved[4][...]) + (moved[5][...] + moved[6][...])
    apply(jnp.logical_not(early), mats_ref, two_ref, tmp_ref)
    one = one_ref[...]
    two = two_ref[...]
    predicted = jnp.sum(tmp_ref[...] * one, axis=0, keepdims=True)
    residual = predicted - obs_ref[...]
    flag = jnp.where(early, 1.0, 0.0)
    left = jnp.where(flag > 0.5, one, two)
    right = jnp.where(flag > 0.5, two, one) * residual
    count = one.shape[1]
    values = jnp.concatenate(
        [left, right, slot_ref[2:3, :].astype(F32), jnp.zeros((FEATS - 97, count), F32)], axis=0
    )
    val_ref[...] = values
    spread(values, slot_ref, most_ref, 0, pay_ref)


def again_kernel(turn_ref, val_ref, slot_ref, most_ref, pay_ref):
    spread(val_ref[...], slot_ref, most_ref, turn_ref[0], pay_ref)


def collect_kernel(step_ref, recv_ref, base_ref, out_ref, turns_ref):
    peers = recv_ref.shape[0]
    left = jnp.concatenate([recv_ref[s, 0:R, :] for s in range(peers)], axis=1)
    right = jnp.concatenate([recv_ref[s, R : 2 * R, :] for s in range(peers)], axis=1)
    loc = jnp.concatenate([recv_ref[s, 96:97, :] for s in range(peers)], axis=1).astype(jnp.int32)
    row_of = loc // WIDE
    lane_of = loc - row_of * WIDE
    count = loc.shape[1]

    def picked(x, key, n):
        hi = x.astype(BF16).astype(F32)
        lo = x - hi
        his, los = [], []
        for i in range(n):
            here = key == i
            his += [jnp.where(here, hi, 0.0).astype(BF16)]
            los += [jnp.where(here, lo, 0.0).astype(BF16)]
        return jnp.concatenate(his, axis=0), jnp.concatenate(los, axis=0)

    xh, xl = picked(left, row_of, GROUPS)
    yh, yl = picked(right, lane_of, WIDE)
    grad = dot_lanes(xh, yh) + (dot_lanes(xh, yl) + dot_lanes(xl, yh))
    out_ref[...] = base_ref[...] - step_ref[0] * grad
    most = jnp.max(recv_ref[:, 97, :]).astype(jnp.int32)
    turns_ref[0] = (most + SLOTS - 1) // SLOTS


def arrange_kernel(*refs):
    own = refs[:WAYS]
    other = refs[WAYS : 2 * WAYS]
    outs = refs[2 * WAYS :]
    even_first = jnp.where(lax.axis_index("cores") % 2 == 0, 1.0, 0.0)
    for w in range(WAYS):
        rows = slice(w * ROWS, (w + 1) * ROWS)
        mine = own[w][...]
        theirs = other[w][...]
        for k in range(2):
            flag = even_first if k == 0 else 1.0 - even_first
            core = jnp.where(flag > 0.5, mine, theirs)
            outs[4 * k][rows, :], outs[4 * k + 1][rows, :] = halves(core)
            outs[4 * k + 2][:, rows], outs[4 * k + 3][:, rows] = halves(core.T)


def three(a, b):
    (ah, al), (bh, bl) = a, b
    mul = functools.partial(jnp.dot, preferred_element_type=F32)
    return mul(ah, bh) + (mul(ah, bl) + mul(al, bh))


def packed_of(full):
    lane = iota((24, 128), 1)
    return jnp.where(lane < 64, full[0:24], pltpu.roll(full[24:48], 64, 1))


def whole(packed):
    both = jnp.concatenate([packed, pltpu.roll(packed, 64, 1)], axis=0)
    return jnp.where(iota((R, 128), 1) < R, both, 0.0)


def folded(turned, prod):
    total = jnp.zeros((R, 256), F32)
    for part, slices in ((0, range(5)), (128, range(5, WIDE))):
        cols = slice(part, part + 256)
        z = three([t[cols, :] for t in turned], [p[:, cols] for p in prod])
        for h in slices:
            at = h * R - part
            block = z[at : at + R]
            total = total + (pltpu.roll(block, 256 - at, 1) if at else block)
    return jnp.where(iota((R, 128), 1) < R, total[:, :128], 0.0) * (1.0 / N)


def pulled(before, core, prod_ref):
    high, low, high_t, low_t = core
    weights = halves(before[:, :R])
    for g in range(WAYS * GROUPS):
        rows = slice(g * R, (g + 1) * R)
        prod_ref[rows, :] = three(weights, (high[rows, :], low[rows, :]))
    return folded((high_t, low_t), halves(prod_ref[...]))


def first_kernel(own_ref, out_ref):
    parts = halves(own_ref[...])
    turned = halves(own_ref[...].T)
    packed = packed_of(folded(turned, parts))
    for peer in range(out_ref.shape[0]):
        out_ref[peer] = packed


def pair_kernel(*refs, pair):
    last = pair == MODES // 2 - 1
    refs = list(refs)
    recv_ref = refs.pop(0)
    swap_ref = None if pair else refs.pop(0)
    saved = [refs.pop(0) for _ in range(pair)] if last else []
    even = [refs.pop(0) for _ in range(4)] if pair else None
    odd = None if last else [refs.pop(0) for _ in range(4)]
    prod_ref = refs.pop()
    mode = lax.axis_index("cores")
    live = jnp.where(mode // 2 == pair, 1.0, 0.0)
    arrived = jnp.sum(recv_ref[...], axis=0)
    if pair:
        sum_ref = refs.pop()
        sum_ref[...] = arrived
        middle = pulled(whole(arrived), even, prod_ref) * live
    else:
        arrived = jnp.where(mode % 2 == 0, arrived, jnp.sum(swap_ref[...], axis=0))
        middle = whole(arrived) * (live / WAYS)
    kept = packed_of(middle)
    if last:
        for s in saved:
            kept = kept + s[...]
        refs[0][...] = kept
        return
    out_ref, save_ref = refs
    save_ref[...] = kept
    packed = packed_of(pulled(middle, odd, prod_ref))
    for peer in range(out_ref.shape[0]):
        out_ref[peer] = packed


def final_kernel(*refs):
    pairs = MODES // 2 - 1
    sums = refs[:pairs]
    parts = refs[pairs : pairs + WAYS]
    own_ref, out_ref, prod_ref, block_ref = refs[pairs + WAYS :]
    mode = lax.axis_index("cores")
    chip = mode // 2
    first = jnp.where(mode % 2 == 0, 1.0, 0.0)
    second = 1.0 - first
    level = (parts[0][...] + parts[1][...]) + (parts[2][...] + parts[3][...])
    own = level * first
    prev = level * second
    for p in range(pairs):
        own = own + sums[p][...] * jnp.where(chip == p, second, 0.0)
        prev = prev + sums[p][...] * jnp.where(chip == p + 1, first, 0.0)
    row = iota((R, 128), 0)
    lane = iota((R, 128), 1)
    eye = jnp.where(lane == row, 1.0, 0.0)
    side = jnp.where(lane == row + 64, 1.0, 0.0)

    def start(packed, absent):
        return whole(packed) + eye * absent + side

    mats = [
        start(own, jnp.where(mode == MODES - 1, 1.0, 0.0)),
        start(prev, jnp.where(mode == 0, 1.0, 0.0)),
    ]
    for j in range(R):
        for w in range(2):
            m = mats[w]
            pivot = m[j : j + 1, :]
            scale = 1.0 / m[j : j + 1, j : j + 1]
            col = jnp.where(row[:, 0:1] > j, m[:, j : j + 1] * scale, 0.0)
            mats[w] = m - col * pivot
    tri = []
    for w in range(2):
        diag = jnp.sum(jnp.where(lane == row, mats[w], 0.0), axis=1, keepdims=True)
        tri.append(mats[w] * (1.0 / jnp.sqrt(diag)))
    carry = tri[1][:, :R]
    inv = jnp.where(lane >= 64, tri[0], 0.0)
    turned = pltpu.roll(inv, 64, 1)
    wide = jnp.concatenate([jnp.where(lane < R, turned, 0.0), jnp.zeros((R, LANES - 128), F32)], axis=1)
    for h in range(WIDE):
        block_ref[h * R : (h + 1) * R, :] = pltpu.roll(wide, h * R, 1) if h else wide
    for g in range(GROUPS):
        prod_ref[g * R : (g + 1) * R, :] = jnp.dot(
            carry, own_ref[g * R : (g + 1) * R, :], preferred_element_type=F32, precision=HIGH
        )
    out_ref[...] = dot_lanes(prod_ref[...], block_ref[...], HIGH)


def vmem():
    return pl.BlockSpec(memory_space=pltpu.VMEM)


def smem():
    return pl.BlockSpec(memory_space=pltpu.SMEM)


def call(kernel, outs, ins, scratch=(), name=None):
    return pl.pallas_call(
        kernel,
        out_shape=outs,
        in_specs=ins,
        out_specs=jax.tree.map(lambda o: smem() if o.dtype == jnp.int32 and o.size == 1 else vmem(), outs),
        scratch_shapes=list(scratch),
        compiler_params=pltpu.CompilerParams(vmem_limit_bytes=BIG),
        name=name,
    )


def shape(*dims, dtype=F32):
    return jax.ShapeDtypeStruct(dims, dtype)


def on_device(cores, indices, observed, step_size):
    peers = lax.axis_size("samp")
    count = indices.shape[0]
    slab = N // peers
    table = cores[0]
    idx = indices.T
    step = step_size.reshape(1)

    mats, sent, slot, most = pl.pallas_call(
        functools.partial(gather_kernel, peers=peers),
        grid=(RR // COLS,),
        in_specs=[
            pl.BlockSpec((MODES, count), lambda i: (0, 0)),
            pl.BlockSpec((N, COLS), lambda i: (0, i)),
        ],
        out_specs=[
            pl.BlockSpec((COLS, count), lambda i: (i, 0)),
            pl.BlockSpec((R, count), lambda i: (0, 0)),
            pl.BlockSpec((8, count), lambda i: (0, 0)),
            pl.BlockSpec((8, 128), lambda i: (0, 0)),
        ],
        out_shape=[shape(RR, count), shape(R, count), shape(8, count, dtype=jnp.int32), shape(8, 128)],
        scratch_shapes=[pltpu.VMEM((N, count), BF16)],
        compiler_params=pltpu.CompilerParams(vmem_limit_bytes=BIG),
        name="gather",
    )(idx, pltpu.with_memory_space_constraint(table, pltpu.HBM))

    first = lax.axis_index("samp") * slab
    kept = lax.dynamic_slice_in_dim(table, first, slab, 0)
    base = kept.reshape(GROUPS, WIDE, R, R).transpose(0, 2, 1, 3)
    base = base.reshape(ROWS, LANES)

    every = []
    for turn in range(MODES - 1):
        if turn > 0:
            sent = call(
                functools.partial(hop_kernel, second=turn >= MODES // 2),
                shape(R, count),
                [vmem(), vmem()],
                name=f"hop{turn}",
            )(mats, moved)
        moved = lax.ppermute(sent, "cores", [(turn, turn + 1), (7 - turn, 6 - turn)])
        every.append(moved)

    pay, values = call(
        route_kernel,
        (shape(peers, FEATS, SLOTS), shape(FEATS, count)),
        [vmem()] * (MODES + 3),
        [pltpu.VMEM((R, count), F32)] * 3,
        name="route",
    )(mats, *every, observed.reshape(1, count), slot, most)

    def exchanged(block):
        return lax.all_to_all(block, "samp", 0, 0, tiled=True)

    def collected(recv, so_far):
        return call(
            collect_kernel,
            (shape(ROWS, LANES), shape(1, dtype=jnp.int32)),
            [smem(), vmem(), vmem()],
            name="collect",
        )(step, recv, so_far)

    updated, turns = collected(exchanged(pay), base)

    def more(state):
        return state[0] < turns[0]

    def another(state):
        turn, so_far = state
        pay = call(
            again_kernel,
            shape(peers, FEATS, SLOTS),
            [smem(), vmem(), vmem(), vmem()],
            name="again",
        )(turn.reshape(1), values, slot, most)
        return turn + 1, collected(exchanged(pay), so_far)[0]

    _, updated = lax.while_loop(more, another, (jnp.int32(1), updated))

    side = int(peers**0.5)

    def along(mode, peer, by):
        z, x = peer // side, peer % side
        return z * side + (x + by) % side if mode % 2 == 0 else (z + by) % side * side + x

    ring = [
        [(m * peers + p, m * peers + along(m, p, by)) for m in range(MODES) for p in range(peers)]
        for by in range(1, side)
    ]
    level = [[(p, along(1, p, by)) for p in range(peers)] for by in range(1, side)]
    siblings = [(m, m ^ 1) for m in range(MODES)]
    own = [updated] + [lax.ppermute(updated, ("cores", "samp"), pairs) for pairs in ring]
    other = [lax.ppermute(o, "cores", siblings) for o in own]
    first = call(first_kernel, shape(peers, 24, 128), [vmem()], name="first")(updated)
    recv = lax.all_to_all(first, "samp", 0, 0, tiled=True)
    swap = lax.ppermute(recv, "cores", siblings)
    tall = shape(WAYS * ROWS, LANES, dtype=BF16)
    flat = shape(LANES, WAYS * ROWS, dtype=BF16)
    arranged = call(arrange_kernel, [tall, tall, flat, flat] * 2, [vmem()] * 8, name="arrange")(*own, *other)
    even, odd = list(arranged[:4]), list(arranged[4:])

    saved, sums = [], []
    for pair in range(MODES // 2):
        last = pair == MODES // 2 - 1
        ins = [recv] + (saved + even if last else even + odd if pair else [swap] + odd)
        outs = [shape(24, 128)] if last else [shape(2 * peers, 24, 128), shape(24, 128)]
        if pair:
            outs.append(shape(24, 128))
        res = call(
            functools.partial(pair_kernel, pair=pair),
            outs,
            [vmem()] * len(ins),
            [pltpu.VMEM((WAYS * ROWS, LANES), F32)],
            name=f"pair{pair}",
        )(*ins)
        if pair:
            sums.append(res[-1])
        if last:
            parts = [res[0]] + [lax.ppermute(res[0], "samp", pairs) for pairs in level]
        else:
            saved.append(res[1])
            groups = []
            for c in (pair, pair + 2):
                for h in range(2):
                    both = [2 * (c % 4) + h, 2 * ((c + 1) % 4) + h]
                    groups.append([m * peers + j for m in both for j in range(peers)])
            recv = lax.all_to_all(
                res[0], ("cores", "samp"), 0, 0, axis_index_groups=groups, tiled=True
            )

    out = call(
        final_kernel,
        shape(ROWS, LANES),
        [vmem()] * (MODES // 2 - 1 + WAYS + 1),
        [pltpu.VMEM((ROWS, LANES), F32), pltpu.VMEM((LANES, LANES), F32)],
        name="final",
    )(*sums, *parts, updated)
    out = out.reshape(GROUPS, R, WIDE, R).transpose(0, 2, 1, 3)
    return out.reshape(1, slab, RR)


def solution(mesh):
    in_specs = (P("cores", None, None), P("samp", None), P("samp"), P())
    out_specs = P("cores", "samp", None)
    return jax.shard_map(
        on_device, mesh=mesh, in_specs=in_specs, out_specs=out_specs, check_vma=False
    )
```

```python
import functools

import jax
import jax.numpy as jnp
from jax import lax
from jax.experimental import pallas as pl
from jax.experimental.pallas import tpu as pltpu
from jax.sharding import PartitionSpec as P

R = 48
N = 512
MODES = 8
RR = R * R
GROUPS = 4
WIDE = 8
ROWS = GROUPS * R
LANES = WIDE * R
FEATS = 104
SLOTS = 128
WAYS = 4
PARTS = 2
HIGH = lax.Precision.HIGHEST
F32 = jnp.float32
BF16 = jnp.bfloat16
COLS = 384
BIG = 14 << 20


def dot_rows(a, b):
    return lax.dot_general(a, b, (((0,), (0,)), ((), ())), preferred_element_type=F32)


def dot_lanes(a, b, precision=None):
    return lax.dot_general(
        a, b, (((1,), (1,)), ((), ())), preferred_element_type=F32, precision=precision
    )


def halves(x):
    hi = x.astype(BF16)
    return hi, (x - hi.astype(F32)).astype(BF16)


def iota(shape, dim):
    return lax.broadcasted_iota(jnp.int32, shape, dim)


def ranks(row, peers, slab):
    count = row.shape[1]
    chunks = count // 128
    dest = row // slab
    hit = (iota((peers, count), 0) == dest).astype(F32)
    stacked = jnp.concatenate([hit[:, c * 128 : (c + 1) * 128] for c in range(chunks)], axis=0)
    upper = (iota((128, 128), 0) <= iota((128, 128), 1)).astype(BF16)
    inside = jnp.dot(stacked.astype(BF16), upper, preferred_element_type=F32)
    before = jnp.zeros((peers, 1), F32)
    out = []
    for c in range(chunks):
        part = inside[c * peers : (c + 1) * peers]
        mine = hit[:, c * 128 : (c + 1) * 128]
        out.append(jnp.sum(mine * (part + before), axis=0, keepdims=True))
        before = before + part[:, 127:128]
    return jnp.concatenate(out, axis=1).astype(jnp.int32) - 1, dest


def gather_kernel(idx_ref, table_ref, mats_ref, *refs, peers):
    sent_refs = refs[:PARTS]
    slot_ref, most_ref, hot_ref = refs[PARTS:]
    width = sent_refs[0].shape[1]
    step = pl.program_id(0)
    mode = lax.axis_index("cores")
    leftward = mode < MODES // 2
    slab = N // peers

    @pl.when(step == 0)
    def _():
        row = idx_ref[pl.ds(mode, 1), :]
        count = row.shape[1]
        hot_ref[...] = (iota((N, count), 0) == row).astype(BF16)
        place, dest = ranks(row, peers, slab)
        slot_ref[0:1, :] = place
        slot_ref[1:2, :] = dest
        slot_ref[2:3, :] = row - dest * slab
        slot_ref[3:8, :] = jnp.zeros((5, count), jnp.int32)
        every = idx_ref[...] // slab
        most = jnp.zeros((MODES, 1), F32)
        for j in range(peers):
            most = jnp.maximum(most, jnp.sum((every == j).astype(F32), axis=1, keepdims=True))
        most_ref[...] = jnp.broadcast_to(jnp.max(most, axis=0, keepdims=True), (8, 128))

    hot = hot_ref[...]
    hi, lo = halves(table_ref[...])
    out = dot_rows(hi, hot) + dot_rows(lo, hot)
    mats_ref[...] = out

    @pl.when(jnp.logical_and(leftward, step == 0))
    def _():
        for p in range(PARTS):
            sent_refs[p][...] = out[0:R, p * width : (p + 1) * width]

    @pl.when(jnp.logical_not(leftward))
    def _():
        per = COLS // R
        rows = jnp.concatenate([out[i * R : i * R + 1] for i in range(per)], axis=0)
        for p in range(PARTS):
            sent_refs[p][pl.ds(pl.multiple_of(step * per, per), per), :] = rows[:, p * width : (p + 1) * width]


def times_left(mats_ref, vec_ref, out_ref, first):
    count = vec_ref.shape[1]

    def chunk(c, _):
        lanes = pl.ds(pl.multiple_of(c * 128, 128), 128)
        from_ = pl.ds(pl.multiple_of(c * 128 + first, 128), 128)
        acc = [jnp.zeros((R, 128), F32) for _ in range(2)]
        for a in range(R):
            acc[a % 2] = acc[a % 2] + mats_ref[a * R : (a + 1) * R, from_] * vec_ref[a : a + 1, lanes]
        out_ref[:, lanes] = acc[0] + acc[1]
        return 0

    lax.fori_loop(0, count // 128, chunk, 0)


def times_right(mats_ref, vec_ref, out_ref, first):
    count = vec_ref.shape[1]

    def chunk(c, _):
        lanes = pl.ds(pl.multiple_of(c * 128, 128), 128)
        from_ = pl.ds(pl.multiple_of(c * 128 + first, 128), 128)
        vec = vec_ref[:, lanes]
        for a in range(0, R, 8):
            rows = [
                jnp.sum(mats_ref[(a + i) * R : (a + i + 1) * R, from_] * vec, axis=0, keepdims=True)
                for i in range(8)
            ]
            out_ref[a : a + 8, lanes] = jnp.concatenate(rows, axis=0)
        return 0

    lax.fori_loop(0, count // 128, chunk, 0)


def apply(left, mats_ref, vec_ref, out_ref, first=0):
    @pl.when(left)
    def _():
        times_left(mats_ref, vec_ref, out_ref, first)

    @pl.when(jnp.logical_not(left))
    def _():
        times_right(mats_ref, vec_ref, out_ref, first)


def hop_kernel(mats_ref, vec_ref, out_ref, *, second, part):
    mode = lax.axis_index("cores")
    left = (mode >= MODES // 2) if second else (mode < MODES // 2)
    apply(left, mats_ref, vec_ref, out_ref, part * vec_ref.shape[1])


def spread(values, slot_ref, most_ref, turn, pay_ref):
    place = slot_ref[0:1, :] - turn * SLOTS
    fits = jnp.logical_and(place >= 0, place < SLOTS)
    key = jnp.where(fits, slot_ref[1:2, :] * SLOTS + place, -1)
    hi, lo = halves(values)
    both = jnp.concatenate([hi, lo], axis=0)
    peers = pay_ref.shape[0]
    count = values.shape[1]
    for pair in range(peers // 2):
        base = pair * 2 * SLOTS
        hot = (iota((2 * SLOTS, count), 0) + base == key).astype(BF16)
        out = dot_lanes(both, hot)
        out = out[:FEATS] + out[FEATS:]
        pay_ref[2 * pair] = out[:, :SLOTS]
        pay_ref[2 * pair + 1] = out[:, SLOTS:]
    for peer in range(peers):
        pay_ref[peer, 97:98, :] = most_ref[0:1, :]


def route_kernel(mats_ref, *refs):
    turns = MODES - 1
    obs_ref, slot_ref, most_ref, pay_ref, val_ref, one_ref, two_ref, tmp_ref = refs[turns * PARTS :]
    width = refs[0].shape[1]
    mode = lax.axis_index("cores")
    early = mode < MODES // 2
    edge = jnp.where(jnp.logical_or(mode == 0, mode == MODES - 1), 1.0, 0.0)
    for p in range(PARTS):
        moved = refs[p * turns : (p + 1) * turns]
        lanes = slice(p * width, (p + 1) * width)
        one = jnp.where(iota((R, width), 0) == 0, edge, 0.0)
        one_ref[:, lanes] = one + ((moved[0][...] + moved[1][...]) + moved[2][...])
        two_ref[:, lanes] = (moved[3][...] + moved[4][...]) + (moved[5][...] + moved[6][...])
    apply(jnp.logical_not(early), mats_ref, two_ref, tmp_ref)
    one = one_ref[...]
    two = two_ref[...]
    predicted = jnp.sum(tmp_ref[...] * one, axis=0, keepdims=True)
    residual = predicted - obs_ref[...]
    flag = jnp.where(early, 1.0, 0.0)
    left = jnp.where(flag > 0.5, one, two)
    right = jnp.where(flag > 0.5, two, one) * residual
    count = one.shape[1]
    values = jnp.concatenate(
        [left, right, slot_ref[2:3, :].astype(F32), jnp.zeros((FEATS - 97, count), F32)], axis=0
    )
    val_ref[...] = values
    spread(values, slot_ref, most_ref, 0, pay_ref)


def again_kernel(turn_ref, val_ref, slot_ref, most_ref, pay_ref):
    spread(val_ref[...], slot_ref, most_ref, turn_ref[0], pay_ref)


def collect_kernel(step_ref, recv_ref, base_ref, out_ref, turns_ref):
    peers = recv_ref.shape[0]
    left = jnp.concatenate([recv_ref[s, 0:R, :] for s in range(peers)], axis=1)
    right = jnp.concatenate([recv_ref[s, R : 2 * R, :] for s in range(peers)], axis=1)
    loc = jnp.concatenate([recv_ref[s, 96:97, :] for s in range(peers)], axis=1).astype(jnp.int32)
    row_of = loc // WIDE
    lane_of = loc - row_of * WIDE
    count = loc.shape[1]

    def picked(x, key, n):
        hi = x.astype(BF16).astype(F32)
        lo = x - hi
        his, los = [], []
        for i in range(n):
            here = key == i
            his += [jnp.where(here, hi, 0.0).astype(BF16)]
            los += [jnp.where(here, lo, 0.0).astype(BF16)]
        return jnp.concatenate(his, axis=0), jnp.concatenate(los, axis=0)

    xh, xl = picked(left, row_of, GROUPS)
    yh, yl = picked(right, lane_of, WIDE)
    grad = dot_lanes(xh, yh) + (dot_lanes(xh, yl) + dot_lanes(xl, yh))
    out_ref[...] = base_ref[...] - step_ref[0] * grad
    most = jnp.max(recv_ref[:, 97, :]).astype(jnp.int32)
    turns_ref[0] = (most + SLOTS - 1) // SLOTS


def arrange_kernel(*refs):
    own = refs[:WAYS]
    other = refs[WAYS : 2 * WAYS]
    outs = refs[2 * WAYS :]
    even_first = jnp.where(lax.axis_index("cores") % 2 == 0, 1.0, 0.0)
    for w in range(WAYS):
        rows = slice(w * ROWS, (w + 1) * ROWS)
        mine = own[w][...]
        theirs = other[w][...]
        for k in range(2):
            flag = even_first if k == 0 else 1.0 - even_first
            core = jnp.where(flag > 0.5, mine, theirs)
            outs[4 * k][rows, :], outs[4 * k + 1][rows, :] = halves(core)
            outs[4 * k + 2][:, rows], outs[4 * k + 3][:, rows] = halves(core.T)


def three(a, b):
    (ah, al), (bh, bl) = a, b
    mul = functools.partial(jnp.dot, preferred_element_type=F32)
    return mul(ah, bh) + (mul(ah, bl) + mul(al, bh))


def packed_of(full):
    lane = iota((24, 128), 1)
    return jnp.where(lane < 64, full[0:24], pltpu.roll(full[24:48], 64, 1))


def whole(packed):
    both = jnp.concatenate([packed, pltpu.roll(packed, 64, 1)], axis=0)
    return jnp.where(iota((R, 128), 1) < R, both, 0.0)


def pulled(before, core, prod_ref):
    high, low, high_t, low_t = core
    if before is None:
        prod = (high[...], low[...])
    else:
        weights = halves(before[:, :R])
        for g in range(WAYS * GROUPS):
            rows = slice(g * R, (g + 1) * R)
            prod_ref[rows, :] = three(weights, (high[rows, :], low[rows, :]))
        prod = halves(prod_ref[...])
    total = jnp.zeros((R, 256), F32)
    for part, slices in ((0, range(5)), (128, range(5, WIDE))):
        cols = slice(part, part + 256)
        z = three((high_t[cols, :], low_t[cols, :]), (prod[0][:, cols], prod[1][:, cols]))
        for h in slices:
            at = h * R - part
            block = z[at : at + R]
            total = total + (pltpu.roll(block, 256 - at, 1) if at else block)
    return jnp.where(iota((R, 128), 1) < R, total[:, :128], 0.0) * (1.0 / N)


def pair_kernel(*refs, pair):
    last = pair == MODES // 2 - 1
    refs = list(refs)
    recv_ref = refs.pop(0) if pair else None
    saved = [refs.pop(0) for _ in range(pair)] if last else []
    even = [refs.pop(0) for _ in range(4)]
    odd = None if last else [refs.pop(0) for _ in range(4)]
    prod_ref = refs.pop()
    if pair:
        sum_ref = refs.pop()
        arrived = jnp.sum(recv_ref[...], axis=0)
        sum_ref[...] = arrived
        before = whole(arrived)
    else:
        before = None
    chip = lax.axis_index("cores") // 2
    live = jnp.where(chip == pair, 1.0, 0.0)
    middle = pulled(before, even, prod_ref) * live
    kept = packed_of(middle)
    if last:
        for s in saved:
            kept = kept + s[...]
        refs[0][...] = kept
        return
    out_ref, save_ref = refs
    save_ref[...] = kept
    packed = packed_of(pulled(middle, odd, prod_ref))
    for peer in range(out_ref.shape[0]):
        out_ref[peer] = packed


def final_kernel(*refs):
    pairs = MODES // 2 - 1
    sums = refs[:pairs]
    parts = refs[pairs : pairs + WAYS]
    own_ref, out_ref, prod_ref, block_ref = refs[pairs + WAYS :]
    mode = lax.axis_index("cores")
    chip = mode // 2
    first = jnp.where(mode % 2 == 0, 1.0, 0.0)
    second = 1.0 - first
    level = (parts[0][...] + parts[1][...]) + (parts[2][...] + parts[3][...])
    own = level * first
    prev = level * second
    for p in range(pairs):
        own = own + sums[p][...] * jnp.where(chip == p, second, 0.0)
        prev = prev + sums[p][...] * jnp.where(chip == p + 1, first, 0.0)
    row = iota((R, 128), 0)
    lane = iota((R, 128), 1)
    eye = jnp.where(lane == row, 1.0, 0.0)
    side = jnp.where(lane == row + 64, 1.0, 0.0)

    def start(packed, absent):
        return whole(packed) + eye * absent + side

    mats = [
        start(own, jnp.where(mode == MODES - 1, 1.0, 0.0)),
        start(prev, jnp.where(mode == 0, 1.0, 0.0)),
    ]
    for j in range(R):
        for w in range(2):
            m = mats[w]
            pivot = m[j : j + 1, :]
            scale = 1.0 / m[j : j + 1, j : j + 1]
            col = jnp.where(row[:, 0:1] > j, m[:, j : j + 1] * scale, 0.0)
            mats[w] = m - col * pivot
    tri = []
    for w in range(2):
        diag = jnp.sum(jnp.where(lane == row, mats[w], 0.0), axis=1, keepdims=True)
        tri.append(mats[w] * (1.0 / jnp.sqrt(diag)))
    carry = tri[1][:, :R]
    inv = jnp.where(lane >= 64, tri[0], 0.0)
    turned = pltpu.roll(inv, 64, 1)
    wide = jnp.concatenate([jnp.where(lane < R, turned, 0.0), jnp.zeros((R, LANES - 128), F32)], axis=1)
    for h in range(WIDE):
        block_ref[h * R : (h + 1) * R, :] = pltpu.roll(wide, h * R, 1) if h else wide
    for g in range(GROUPS):
        prod_ref[g * R : (g + 1) * R, :] = jnp.dot(
            carry, own_ref[g * R : (g + 1) * R, :], preferred_element_type=F32, precision=HIGH
        )
    out_ref[...] = dot_lanes(prod_ref[...], block_ref[...], HIGH)


def vmem():
    return pl.BlockSpec(memory_space=pltpu.VMEM)


def smem():
    return pl.BlockSpec(memory_space=pltpu.SMEM)


def call(kernel, outs, ins, scratch=(), name=None):
    return pl.pallas_call(
        kernel,
        out_shape=outs,
        in_specs=ins,
        out_specs=jax.tree.map(lambda o: smem() if o.dtype == jnp.int32 and o.size == 1 else vmem(), outs),
        scratch_shapes=list(scratch),
        compiler_params=pltpu.CompilerParams(vmem_limit_bytes=BIG),
        name=name,
    )


def shape(*dims, dtype=F32):
    return jax.ShapeDtypeStruct(dims, dtype)


def on_device(cores, indices, observed, step_size):
    peers = lax.axis_size("samp")
    count = indices.shape[0]
    slab = N // peers
    table = cores[0]
    idx = indices.T
    step = step_size.reshape(1)

    width = count // PARTS
    mats, *sent, slot, most = pl.pallas_call(
        functools.partial(gather_kernel, peers=peers),
        grid=(RR // COLS,),
        in_specs=[
            pl.BlockSpec((MODES, count), lambda i: (0, 0)),
            pl.BlockSpec((N, COLS), lambda i: (0, i)),
        ],
        out_specs=[
            pl.BlockSpec((COLS, count), lambda i: (i, 0)),
            *[pl.BlockSpec((R, width), lambda i: (0, 0))] * PARTS,
            pl.BlockSpec((8, count), lambda i: (0, 0)),
            pl.BlockSpec((8, 128), lambda i: (0, 0)),
        ],
        out_shape=[
            shape(RR, count),
            *[shape(R, width)] * PARTS,
            shape(8, count, dtype=jnp.int32),
            shape(8, 128),
        ],
        scratch_shapes=[pltpu.VMEM((N, count), BF16)],
        compiler_params=pltpu.CompilerParams(vmem_limit_bytes=BIG),
        name="gather",
    )(*[pltpu.with_memory_space_constraint(a, pltpu.HBM) for a in (idx, table)])

    first = lax.axis_index("samp") * slab
    kept = lax.dynamic_slice_in_dim(table, first, slab, 0)
    base = kept.reshape(GROUPS, WIDE, R, R).transpose(0, 2, 1, 3)
    base = base.reshape(ROWS, LANES)

    every = [[] for _ in range(PARTS)]
    for turn in range(MODES - 1):
        for p in range(PARTS):
            if turn > 0:
                sent[p] = call(
                    functools.partial(hop_kernel, second=turn >= MODES // 2, part=p),
                    shape(R, width),
                    [vmem(), vmem()],
                    name=f"hop{turn}_{p}",
                )(mats, every[p][-1])
            pairs = [(turn, turn + 1), (7 - turn, 6 - turn)]
            every[p].append(lax.ppermute(sent[p], "cores", pairs))

    pay, values = call(
        route_kernel,
        (shape(peers, FEATS, SLOTS), shape(FEATS, count)),
        [vmem()] * (PARTS * (MODES - 1) + 4),
        [pltpu.VMEM((R, count), F32)] * 3,
        name="route",
    )(mats, *sum(every, []), observed.reshape(1, count), slot, most)

    def exchanged(block):
        return lax.all_to_all(block, "samp", 0, 0, tiled=True)

    def collected(recv, so_far):
        return call(
            collect_kernel,
            (shape(ROWS, LANES), shape(1, dtype=jnp.int32)),
            [smem(), vmem(), vmem()],
            name="collect",
        )(step, recv, so_far)

    updated, turns = collected(exchanged(pay), base)

    def more(state):
        return state[0] < turns[0]

    def another(state):
        turn, so_far = state
        pay = call(
            again_kernel,
            shape(peers, FEATS, SLOTS),
            [smem(), vmem(), vmem(), vmem()],
            name="again",
        )(turn.reshape(1), values, slot, most)
        return turn + 1, collected(exchanged(pay), so_far)[0]

    _, updated = lax.while_loop(more, another, (jnp.int32(1), updated))

    side = int(peers**0.5)

    def along(mode, peer, by):
        z, x = peer // side, peer % side
        return z * side + (x + by) % side if mode % 2 == 0 else (z + by) % side * side + x

    ring = [
        [(m * peers + p, m * peers + along(m, p, by)) for m in range(MODES) for p in range(peers)]
        for by in range(1, side)
    ]
    level = [[(p, along(1, p, by)) for p in range(peers)] for by in range(1, side)]
    siblings = [(m, m ^ 1) for m in range(MODES)]
    own = [updated] + [lax.ppermute(updated, ("cores", "samp"), pairs) for pairs in ring]
    other = [lax.ppermute(o, "cores", siblings) for o in own]
    tall = shape(WAYS * ROWS, LANES, dtype=BF16)
    flat = shape(LANES, WAYS * ROWS, dtype=BF16)
    arranged = call(arrange_kernel, [tall, tall, flat, flat] * 2, [vmem()] * 8, name="arrange")(*own, *other)
    even, odd = list(arranged[:4]), list(arranged[4:])

    saved, sums = [], []
    recv = None
    for pair in range(MODES // 2):
        last = pair == MODES // 2 - 1
        ins = ([recv] if pair else []) + (saved if last else []) + even + ([] if last else odd)
        outs = [shape(24, 128)] if last else [shape(2 * peers, 24, 128), shape(24, 128)]
        if pair:
            outs.append(shape(24, 128))
        res = call(
            functools.partial(pair_kernel, pair=pair),
            outs,
            [vmem()] * len(ins),
            [pltpu.VMEM((WAYS * ROWS, LANES), F32)],
            name=f"pair{pair}",
        )(*ins)
        if pair:
            sums.append(res[-1])
        if last:
            parts = [res[0]] + [lax.ppermute(res[0], "samp", pairs) for pairs in level]
        else:
            saved.append(res[1])
            groups = []
            for c in (pair, pair + 2):
                for h in range(2):
                    both = [2 * (c % 4) + h, 2 * ((c + 1) % 4) + h]
                    groups.append([m * peers + j for m in both for j in range(peers)])
            recv = lax.all_to_all(
                res[0], ("cores", "samp"), 0, 0, axis_index_groups=groups, tiled=True
            )

    out = call(
        final_kernel,
        shape(ROWS, LANES),
        [vmem()] * (MODES // 2 - 1 + WAYS + 1),
        [pltpu.VMEM((ROWS, LANES), F32), pltpu.VMEM((LANES, LANES), F32)],
        name="final",
    )(*sums, *parts, updated)
    out = out.reshape(GROUPS, R, WIDE, R).transpose(0, 2, 1, 3)
    return out.reshape(1, slab, RR)


def solution(mesh):
    in_specs = (P("cores", None, None), P("samp", None), P("samp"), P())
    out_specs = P("cores", "samp", None)
    return jax.shard_map(
        on_device, mesh=mesh, in_specs=in_specs, out_specs=out_specs, check_vma=False
    )
```

```python
import functools

import jax
import jax.numpy as jnp
from jax import lax
from jax.experimental import pallas as pl
from jax.experimental.pallas import tpu as pltpu
from jax.sharding import PartitionSpec as P

R = 48
N = 512
MODES = 8
RR = R * R
GROUPS = 4
WIDE = 8
ROWS = GROUPS * R
LANES = WIDE * R
FEATS = 104
SLOTS = 128
WAYS = 4
HIGH = lax.Precision.HIGHEST
F32 = jnp.float32
BF16 = jnp.bfloat16
COLS = 768
BIG = 14 << 20


def dot_rows(a, b):
    return lax.dot_general(a, b, (((0,), (0,)), ((), ())), preferred_element_type=F32)


def dot_lanes(a, b, precision=None):
    return lax.dot_general(
        a, b, (((1,), (1,)), ((), ())), preferred_element_type=F32, precision=precision
    )


def halves(x):
    hi = x.astype(BF16)
    return hi, (x - hi.astype(F32)).astype(BF16)


def iota(shape, dim):
    return lax.broadcasted_iota(jnp.int32, shape, dim)


def ranks(row, peers, slab):
    count = row.shape[1]
    chunks = count // 128
    dest = row // slab
    hit = (iota((peers, count), 0) == dest).astype(F32)
    stacked = jnp.concatenate([hit[:, c * 128 : (c + 1) * 128] for c in range(chunks)], axis=0)
    upper = (iota((128, 128), 0) <= iota((128, 128), 1)).astype(BF16)
    inside = jnp.dot(stacked.astype(BF16), upper, preferred_element_type=F32)
    before = jnp.zeros((peers, 1), F32)
    out = []
    for c in range(chunks):
        part = inside[c * peers : (c + 1) * peers]
        mine = hit[:, c * 128 : (c + 1) * 128]
        out.append(jnp.sum(mine * (part + before), axis=0, keepdims=True))
        before = before + part[:, 127:128]
    return jnp.concatenate(out, axis=1).astype(jnp.int32) - 1, dest


def half_of(row, second):
    half = row.shape[1] // 2
    flag = jnp.where(second, 1.0, 0.0)
    return jnp.where(flag > 0.5, row[:, half:], row[:, :half])


def gather_kernel(idx_ref, table_ref, *refs, peers):
    own = peers is not None
    mats_ref, *outs, hot_ref = refs if own else refs[1:]
    step = pl.program_id(0)
    mode = lax.axis_index("cores")

    @pl.when(step == 0)
    def _():
        which = mode if own else mode + 1 - 2 * (mode % 2)
        row = idx_ref[pl.ds(which, 1), :]
        half = half_of(row, mode % 2 == 1)
        hot_ref[...] = (iota(hot_ref.shape, 0) == half).astype(BF16)
        if own:
            slot_ref, most_ref = outs
            slab = N // peers
            place, dest = ranks(row, peers, slab)
            slot_ref[0:1, :] = place
            slot_ref[1:2, :] = dest
            slot_ref[2:3, :] = row - dest * slab
            slot_ref[3:8, :] = jnp.zeros((5, row.shape[1]), jnp.int32)
            every = idx_ref[...] // slab
            most = jnp.zeros((MODES, 1), F32)
            for j in range(peers):
                most = jnp.maximum(most, jnp.sum((every == j).astype(F32), axis=1, keepdims=True))
            most_ref[...] = jnp.broadcast_to(jnp.max(most, axis=0, keepdims=True), (8, 128))

    hot = hot_ref[...]
    hi, lo = halves(table_ref[...])
    mats_ref[...] = dot_rows(hi, hot) + dot_rows(lo, hot)


def times(left, mats_ref, base, vec_ref, out_ref):
    count = vec_ref.shape[1]

    def rows(a):
        return pl.ds(pl.multiple_of(base + a * R, 8), R)

    @pl.when(left)
    def _():
        def chunk(c, _):
            lanes = pl.ds(pl.multiple_of(c * 128, 128), 128)
            acc = [jnp.zeros((R, 128), F32) for _ in range(2)]
            for a in range(R):
                acc[a % 2] = acc[a % 2] + mats_ref[rows(a), lanes] * vec_ref[a : a + 1, lanes]
            out_ref[:, lanes] = acc[0] + acc[1]
            return 0

        lax.fori_loop(0, count // 128, chunk, 0)

    @pl.when(jnp.logical_not(left))
    def _():
        def chunk(c, _):
            lanes = pl.ds(pl.multiple_of(c * 128, 128), 128)
            vec = vec_ref[:, lanes]
            for a in range(0, R, 8):
                sums = [
                    jnp.sum(mats_ref[rows(a + i), lanes] * vec, axis=0, keepdims=True) for i in range(8)
                ]
                out_ref[a : a + 8, lanes] = jnp.concatenate(sums, axis=0)
            return 0

        lax.fori_loop(0, count // 128, chunk, 0)


def both_modes(turn, mats_ref, vec_ref, mid_ref, out_ref):
    mode = lax.axis_index("cores")
    chips = MODES // 2
    left = (mode // 2 < chips // 2) if turn < chips // 2 else (mode // 2 >= chips // 2)
    even = (mode % 2) * RR
    base = jnp.where(left, even, RR - even)
    times(left, mats_ref, base, vec_ref, mid_ref)
    times(left, mats_ref, RR - base, mid_ref, out_ref)


def unit_at_ends(shape_):
    chip = lax.axis_index("cores") // 2
    edge = jnp.where(jnp.logical_or(chip == 0, chip == MODES // 2 - 1), 1.0, 0.0)
    return jnp.where(iota(shape_, 0) == 0, edge, 0.0)


def hop_kernel(mats_ref, *refs, turn):
    vec_ref, mid_ref, out_ref = refs if turn else (refs[2], refs[0], refs[1])
    if turn == 0:
        vec_ref[...] = unit_at_ends(vec_ref.shape)
    both_modes(turn, mats_ref, vec_ref, mid_ref, out_ref)


def finish_kernel(mats_ref, *refs):
    recv, mids = refs[0:3], refs[3:6]
    out2_ref, obs_ref, own_ref, other_ref, mid_ref, out_ref = refs[6:]
    mode = lax.axis_index("cores")
    both_modes(3, mats_ref, recv[2], mid_ref, out_ref)
    end1 = unit_at_ends(mid_ref.shape) + recv[0][...]
    mid1 = mids[0][...] + mids[1][...]
    end2 = recv[1][...] + recv[2][...]
    mid2 = mids[2][...] + mid_ref[...]
    predicted = jnp.sum((out2_ref[...] + out_ref[...]) * end1, axis=0, keepdims=True)
    residual = predicted - half_of(obs_ref[...], mode % 2 == 1)
    early = jnp.where(mode // 2 < MODES // 4, 1.0, 0.0) > 0.5
    even = (jnp.where(early, end1, end2), jnp.where(early, mid2, mid1) * residual)
    odd = (jnp.where(early, mid1, mid2), jnp.where(early, end2, end1) * residual)
    second = jnp.where(mode % 2 == 1, 1.0, 0.0) > 0.5
    for k in range(2):
        rows = slice(k * R, (k + 1) * R)
        own_ref[rows, :] = jnp.where(second, odd[k], even[k])
        other_ref[rows, :] = jnp.where(second, even[k], odd[k])


def spread(values, slot_ref, most_ref, turn, pay_ref):
    place = slot_ref[0:1, :] - turn * SLOTS
    fits = jnp.logical_and(place >= 0, place < SLOTS)
    key = jnp.where(fits, slot_ref[1:2, :] * SLOTS + place, -1)
    hi, lo = halves(values)
    both = jnp.concatenate([hi, lo], axis=0)
    peers = pay_ref.shape[0]
    count = values.shape[1]
    for pair in range(peers // 2):
        base = pair * 2 * SLOTS
        hot = (iota((2 * SLOTS, count), 0) + base == key).astype(BF16)
        out = dot_lanes(both, hot)
        out = out[:FEATS] + out[FEATS:]
        pay_ref[2 * pair] = out[:, :SLOTS]
        pay_ref[2 * pair + 1] = out[:, SLOTS:]
    for peer in range(peers):
        pay_ref[peer, 97:98, :] = most_ref[0:1, :]


def route_kernel(own_ref, got_ref, slot_ref, most_ref, pay_ref, val_ref):
    second = jnp.where(lax.axis_index("cores") % 2 == 1, 1.0, 0.0) > 0.5
    own = own_ref[...]
    got = got_ref[...]
    vecs = jnp.concatenate([jnp.where(second, got, own), jnp.where(second, own, got)], axis=1)
    loc = slot_ref[2:3, :].astype(F32)
    values = jnp.concatenate([vecs, loc, jnp.zeros((FEATS - 97, vecs.shape[1]), F32)], axis=0)
    val_ref[...] = values
    spread(values, slot_ref, most_ref, 0, pay_ref)


def again_kernel(turn_ref, val_ref, slot_ref, most_ref, pay_ref):
    spread(val_ref[...], slot_ref, most_ref, turn_ref[0], pay_ref)


def collect_kernel(step_ref, recv_ref, base_ref, out_ref, turns_ref):
    peers = recv_ref.shape[0]
    left = jnp.concatenate([recv_ref[s, 0:R, :] for s in range(peers)], axis=1)
    right = jnp.concatenate([recv_ref[s, R : 2 * R, :] for s in range(peers)], axis=1)
    loc = jnp.concatenate([recv_ref[s, 96:97, :] for s in range(peers)], axis=1).astype(jnp.int32)
    row_of = loc // WIDE
    lane_of = loc - row_of * WIDE
    count = loc.shape[1]

    def picked(x, key, n):
        hi = x.astype(BF16).astype(F32)
        lo = x - hi
        his, los = [], []
        for i in range(n):
            here = key == i
            his += [jnp.where(here, hi, 0.0).astype(BF16)]
            los += [jnp.where(here, lo, 0.0).astype(BF16)]
        return jnp.concatenate(his, axis=0), jnp.concatenate(los, axis=0)

    xh, xl = picked(left, row_of, GROUPS)
    yh, yl = picked(right, lane_of, WIDE)
    grad = dot_lanes(xh, yh) + (dot_lanes(xh, yl) + dot_lanes(xl, yh))
    out_ref[...] = base_ref[...] - step_ref[0] * grad
    most = jnp.max(recv_ref[:, 97, :]).astype(jnp.int32)
    turns_ref[0] = (most + SLOTS - 1) // SLOTS


def arrange_kernel(*refs):
    own = refs[:WAYS]
    other = refs[WAYS : 2 * WAYS]
    outs = refs[2 * WAYS :]
    even_first = jnp.where(lax.axis_index("cores") % 2 == 0, 1.0, 0.0)
    for w in range(WAYS):
        rows = slice(w * ROWS, (w + 1) * ROWS)
        mine = own[w][...]
        theirs = other[w][...]
        for k in range(2):
            flag = even_first if k == 0 else 1.0 - even_first
            core = jnp.where(flag > 0.5, mine, theirs)
            outs[4 * k][rows, :], outs[4 * k + 1][rows, :] = halves(core)
            outs[4 * k + 2][:, rows], outs[4 * k + 3][:, rows] = halves(core.T)


def three(a, b):
    (ah, al), (bh, bl) = a, b
    mul = functools.partial(jnp.dot, preferred_element_type=F32)
    return mul(ah, bh) + (mul(ah, bl) + mul(al, bh))


def packed_of(full):
    lane = iota((24, 128), 1)
    return jnp.where(lane < 64, full[0:24], pltpu.roll(full[24:48], 64, 1))


def whole(packed):
    both = jnp.concatenate([packed, pltpu.roll(packed, 64, 1)], axis=0)
    return jnp.where(iota((R, 128), 1) < R, both, 0.0)


def pulled(before, core, prod_ref):
    high, low, high_t, low_t = core
    if before is None:
        prod = (high[...], low[...])
    else:
        weights = halves(before[:, :R])
        for g in range(WAYS * GROUPS):
            rows = slice(g * R, (g + 1) * R)
            prod_ref[rows, :] = three(weights, (high[rows, :], low[rows, :]))
        prod = halves(prod_ref[...])
    total = jnp.zeros((R, 256), F32)
    for part, slices in ((0, range(5)), (128, range(5, WIDE))):
        cols = slice(part, part + 256)
        z = three((high_t[cols, :], low_t[cols, :]), (prod[0][:, cols], prod[1][:, cols]))
        for h in slices:
            at = h * R - part
            block = z[at : at + R]
            total = total + (pltpu.roll(block, 256 - at, 1) if at else block)
    return jnp.where(iota((R, 128), 1) < R, total[:, :128], 0.0) * (1.0 / N)


def pair_kernel(*refs, pair):
    last = pair == MODES // 2 - 1
    refs = list(refs)
    recv_ref = refs.pop(0) if pair else None
    saved = [refs.pop(0) for _ in range(pair)] if last else []
    even = [refs.pop(0) for _ in range(4)]
    odd = None if last else [refs.pop(0) for _ in range(4)]
    prod_ref = refs.pop()
    if pair:
        sum_ref = refs.pop()
        arrived = jnp.sum(recv_ref[...], axis=0)
        sum_ref[...] = arrived
        before = whole(arrived)
    else:
        before = None
    chip = lax.axis_index("cores") // 2
    live = jnp.where(chip == pair, 1.0, 0.0)
    middle = pulled(before, even, prod_ref) * live
    kept = packed_of(middle)
    if last:
        for s in saved:
            kept = kept + s[...]
        refs[0][...] = kept
        return
    out_ref, save_ref = refs
    save_ref[...] = kept
    packed = packed_of(pulled(middle, odd, prod_ref))
    for peer in range(out_ref.shape[0]):
        out_ref[peer] = packed


def final_kernel(*refs):
    pairs = MODES // 2 - 1
    sums = refs[:pairs]
    parts = refs[pairs : pairs + WAYS]
    own_ref, out_ref, prod_ref, block_ref = refs[pairs + WAYS :]
    mode = lax.axis_index("cores")
    chip = mode // 2
    first = jnp.where(mode % 2 == 0, 1.0, 0.0)
    second = 1.0 - first
    level = (parts[0][...] + parts[1][...]) + (parts[2][...] + parts[3][...])
    own = level * first
    prev = level * second
    for p in range(pairs):
        own = own + sums[p][...] * jnp.where(chip == p, second, 0.0)
        prev = prev + sums[p][...] * jnp.where(chip == p + 1, first, 0.0)
    row = iota((R, 128), 0)
    lane = iota((R, 128), 1)
    eye = jnp.where(lane == row, 1.0, 0.0)
    side = jnp.where(lane == row + 64, 1.0, 0.0)

    def start(packed, absent):
        return whole(packed) + eye * absent + side

    mats = [
        start(own, jnp.where(mode == MODES - 1, 1.0, 0.0)),
        start(prev, jnp.where(mode == 0, 1.0, 0.0)),
    ]
    for j in range(R):
        for w in range(2):
            m = mats[w]
            pivot = m[j : j + 1, :]
            scale = 1.0 / m[j : j + 1, j : j + 1]
            col = jnp.where(row[:, 0:1] > j, m[:, j : j + 1] * scale, 0.0)
            mats[w] = m - col * pivot
    tri = []
    for w in range(2):
        diag = jnp.sum(jnp.where(lane == row, mats[w], 0.0), axis=1, keepdims=True)
        tri.append(mats[w] * (1.0 / jnp.sqrt(diag)))
    carry = tri[1][:, :R]
    inv = jnp.where(lane >= 64, tri[0], 0.0)
    turned = pltpu.roll(inv, 64, 1)
    wide = jnp.concatenate([jnp.where(lane < R, turned, 0.0), jnp.zeros((R, LANES - 128), F32)], axis=1)
    for h in range(WIDE):
        block_ref[h * R : (h + 1) * R, :] = pltpu.roll(wide, h * R, 1) if h else wide
    for g in range(GROUPS):
        prod_ref[g * R : (g + 1) * R, :] = jnp.dot(
            carry, own_ref[g * R : (g + 1) * R, :], preferred_element_type=F32, precision=HIGH
        )
    out_ref[...] = dot_lanes(prod_ref[...], block_ref[...], HIGH)


def vmem():
    return pl.BlockSpec(memory_space=pltpu.VMEM)


def smem():
    return pl.BlockSpec(memory_space=pltpu.SMEM)


def call(kernel, outs, ins, scratch=(), name=None):
    return pl.pallas_call(
        kernel,
        out_shape=outs,
        in_specs=ins,
        out_specs=jax.tree.map(lambda o: smem() if o.dtype == jnp.int32 and o.size == 1 else vmem(), outs),
        scratch_shapes=list(scratch),
        compiler_params=pltpu.CompilerParams(vmem_limit_bytes=BIG),
        name=name,
    )


def shape(*dims, dtype=F32):
    return jax.ShapeDtypeStruct(dims, dtype)


def on_device(cores, indices, observed, step_size):
    peers = lax.axis_size("samp")
    count = indices.shape[0]
    slab = N // peers
    table = cores[0]
    idx = indices.T
    step = step_size.reshape(1)

    half = count // 2
    siblings = [(m, m ^ 1) for m in range(MODES)]
    other_table = lax.ppermute(table, "cores", siblings)
    steps = RR // COLS
    params = pltpu.CompilerParams(vmem_limit_bytes=BIG)
    in_specs = [
        pl.BlockSpec((MODES, count), lambda i: (0, 0)),
        pl.BlockSpec((N, COLS), lambda i: (0, i)),
    ]
    hot = [pltpu.VMEM((N, half), BF16)]
    idx, table_in = [pltpu.with_memory_space_constraint(a, pltpu.HBM) for a in (idx, table)]
    mats, slot, most = pl.pallas_call(
        functools.partial(gather_kernel, peers=peers),
        grid=(steps,),
        in_specs=in_specs,
        out_specs=[
            pl.BlockSpec((COLS, half), lambda i: (i, 0)),
            pl.BlockSpec((8, count), lambda i: (0, 0)),
            pl.BlockSpec((8, 128), lambda i: (0, 0)),
        ],
        out_shape=[shape(2 * RR, half), shape(8, count, dtype=jnp.int32), shape(8, 128)],
        scratch_shapes=hot,
        compiler_params=params,
        name="gather",
    )(idx, table_in)
    mats = pl.pallas_call(
        functools.partial(gather_kernel, peers=None),
        grid=(steps,),
        in_specs=in_specs + [pl.BlockSpec(memory_space=pl.ANY)],
        out_specs=pl.BlockSpec((COLS, half), lambda i: (i + steps, 0)),
        out_shape=shape(2 * RR, half),
        scratch_shapes=hot,
        input_output_aliases={2: 0},
        compiler_params=params,
        name="gather_other",
    )(idx, other_table, mats)

    first = lax.axis_index("samp") * slab
    kept = lax.dynamic_slice_in_dim(table, first, slab, 0)
    base = kept.reshape(GROUPS, WIDE, R, R).transpose(0, 2, 1, 3)
    base = base.reshape(ROWS, LANES)

    vec = shape(R, half)
    recv, mids = [], []
    for turn in range(3):
        mid, out = call(
            functools.partial(hop_kernel, turn=turn),
            [vec, vec],
            [vmem()] * (2 if turn else 1),
            [] if turn else [pltpu.VMEM((R, half), F32)],
            name=f"hop{turn}",
        )(mats, *recv[-1:])
        pairs = [(2 * a + h, 2 * b + h) for a, b in ((turn, turn + 1), (3 - turn, 2 - turn)) for h in range(2)]
        recv.append(lax.ppermute(out, "cores", pairs))
        mids.append(mid)
    own_vecs, other_vecs = call(
        finish_kernel,
        [shape(2 * R, half)] * 2,
        [vmem()] * 9,
        [pltpu.VMEM((R, half), F32)] * 2,
        name="finish",
    )(mats, *recv, *mids, out, observed.reshape(1, count))
    got_vecs = lax.ppermute(other_vecs, "cores", siblings)
    pay, values = call(
        route_kernel,
        (shape(peers, FEATS, SLOTS), shape(FEATS, count)),
        [vmem()] * 4,
        name="route",
    )(own_vecs, got_vecs, slot, most)

    def exchanged(block):
        return lax.all_to_all(block, "samp", 0, 0, tiled=True)

    def collected(recv, so_far):
        return call(
            collect_kernel,
            (shape(ROWS, LANES), shape(1, dtype=jnp.int32)),
            [smem(), vmem(), vmem()],
            name="collect",
        )(step, recv, so_far)

    updated, turns = collected(exchanged(pay), base)

    def more(state):
        return state[0] < turns[0]

    def another(state):
        turn, so_far = state
        pay = call(
            again_kernel,
            shape(peers, FEATS, SLOTS),
            [smem(), vmem(), vmem(), vmem()],
            name="again",
        )(turn.reshape(1), values, slot, most)
        return turn + 1, collected(exchanged(pay), so_far)[0]

    _, updated = lax.while_loop(more, another, (jnp.int32(1), updated))

    side = int(peers**0.5)

    def along(mode, peer, by):
        z, x = peer // side, peer % side
        return z * side + (x + by) % side if mode % 2 == 0 else (z + by) % side * side + x

    ring = [
        [(m * peers + p, m * peers + along(m, p, by)) for m in range(MODES) for p in range(peers)]
        for by in range(1, side)
    ]
    level = [[(p, along(1, p, by)) for p in range(peers)] for by in range(1, side)]
    own = [updated] + [lax.ppermute(updated, ("cores", "samp"), pairs) for pairs in ring]
    other = [lax.ppermute(o, "cores", siblings) for o in own]
    tall = shape(WAYS * ROWS, LANES, dtype=BF16)
    flat = shape(LANES, WAYS * ROWS, dtype=BF16)
    arranged = call(arrange_kernel, [tall, tall, flat, flat] * 2, [vmem()] * 8, name="arrange")(*own, *other)
    even, odd = list(arranged[:4]), list(arranged[4:])

    saved, sums = [], []
    recv = None
    for pair in range(MODES // 2):
        last = pair == MODES // 2 - 1
        ins = ([recv] if pair else []) + (saved if last else []) + even + ([] if last else odd)
        outs = [shape(24, 128)] if last else [shape(2 * peers, 24, 128), shape(24, 128)]
        if pair:
            outs.append(shape(24, 128))
        res = call(
            functools.partial(pair_kernel, pair=pair),
            outs,
            [vmem()] * len(ins),
            [pltpu.VMEM((WAYS * ROWS, LANES), F32)],
            name=f"pair{pair}",
        )(*ins)
        if pair:
            sums.append(res[-1])
        if last:
            parts = [res[0]] + [lax.ppermute(res[0], "samp", pairs) for pairs in level]
        else:
            saved.append(res[1])
            groups = []
            for c in (pair, pair + 2):
                for h in range(2):
                    both = [2 * (c % 4) + h, 2 * ((c + 1) % 4) + h]
                    groups.append([m * peers + j for m in both for j in range(peers)])
            recv = lax.all_to_all(
                res[0], ("cores", "samp"), 0, 0, axis_index_groups=groups, tiled=True
            )

    out = call(
        final_kernel,
        shape(ROWS, LANES),
        [vmem()] * (MODES // 2 - 1 + WAYS + 1),
        [pltpu.VMEM((ROWS, LANES), F32), pltpu.VMEM((LANES, LANES), F32)],
        name="final",
    )(*sums, *parts, updated)
    out = out.reshape(GROUPS, R, WIDE, R).transpose(0, 2, 1, 3)
    return out.reshape(1, slab, RR)


def solution(mesh):
    in_specs = (P("cores", None, None), P("samp", None), P("samp"), P())
    out_specs = P("cores", "samp", None)
    return jax.shard_map(
        on_device, mesh=mesh, in_specs=in_specs, out_specs=out_specs, check_vma=False
    )
```

```python
import functools

import jax
import jax.numpy as jnp
from jax import lax
from jax.experimental import pallas as pl
from jax.experimental.pallas import tpu as pltpu
from jax.sharding import PartitionSpec as P

R = 48
N = 512
MODES = 8
RR = R * R
GROUPS = 4
WIDE = 8
ROWS = GROUPS * R
LANES = WIDE * R
FEATS = 104
SLOTS = 128
WAYS = 4
HIGH = lax.Precision.HIGHEST
F32 = jnp.float32
BF16 = jnp.bfloat16
COLS = 768
BIG = 14 << 20


def dot_rows(a, b):
    return lax.dot_general(a, b, (((0,), (0,)), ((), ())), preferred_element_type=F32)


def dot_lanes(a, b, precision=None):
    return lax.dot_general(
        a, b, (((1,), (1,)), ((), ())), preferred_element_type=F32, precision=precision
    )


def halves(x):
    hi = x.astype(BF16)
    return hi, (x - hi.astype(F32)).astype(BF16)


def iota(shape, dim):
    return lax.broadcasted_iota(jnp.int32, shape, dim)


def ranks(row, peers, slab):
    count = row.shape[1]
    chunks = count // 128
    dest = row // slab
    hit = (iota((peers, count), 0) == dest).astype(F32)
    stacked = jnp.concatenate([hit[:, c * 128 : (c + 1) * 128] for c in range(chunks)], axis=0)
    upper = (iota((128, 128), 0) <= iota((128, 128), 1)).astype(BF16)
    inside = jnp.dot(stacked.astype(BF16), upper, preferred_element_type=F32)
    before = jnp.zeros((peers, 1), F32)
    out = []
    for c in range(chunks):
        part = inside[c * peers : (c + 1) * peers]
        mine = hit[:, c * 128 : (c + 1) * 128]
        out.append(jnp.sum(mine * (part + before), axis=0, keepdims=True))
        before = before + part[:, 127:128]
    return jnp.concatenate(out, axis=1).astype(jnp.int32) - 1, dest


def half_of(row, second):
    half = row.shape[1] // 2
    flag = jnp.where(second, 1.0, 0.0)
    return jnp.where(flag > 0.5, row[:, half:], row[:, :half])


def gather_kernel(idx_ref, table_ref, *refs, peers):
    own = peers is not None
    mats_ref, *outs, hot_ref = refs if own else refs[1:]
    step = pl.program_id(0)
    mode = lax.axis_index("cores")

    @pl.when(step == 0)
    def _():
        which = mode if own else mode + 1 - 2 * (mode % 2)
        row = idx_ref[pl.ds(which, 1), :]
        half = half_of(row, mode % 2 == 1)
        hot_ref[...] = (iota(hot_ref.shape, 0) == half).astype(BF16)
        if own:
            slot_ref, most_ref = outs
            slab = N // peers
            place, dest = ranks(row, peers, slab)
            slot_ref[0:1, :] = place
            slot_ref[1:2, :] = dest
            slot_ref[2:3, :] = row - dest * slab
            slot_ref[3:8, :] = jnp.zeros((5, row.shape[1]), jnp.int32)
            every = idx_ref[...] // slab
            most = jnp.zeros((MODES, 1), F32)
            for j in range(peers):
                most = jnp.maximum(most, jnp.sum((every == j).astype(F32), axis=1, keepdims=True))
            most_ref[...] = jnp.broadcast_to(jnp.max(most, axis=0, keepdims=True), (8, 128))

    hot = hot_ref[...]
    hi, lo = halves(table_ref[...])
    mats_ref[...] = dot_rows(hi, hot) + dot_rows(lo, hot)


def times(left, mats_ref, base, vec_ref, out_ref):
    count = vec_ref.shape[1]

    def rows(a):
        return pl.ds(pl.multiple_of(base + a * R, 8), R)

    @pl.when(left)
    def _():
        def chunk(c, _):
            lanes = pl.ds(pl.multiple_of(c * 128, 128), 128)
            acc = [jnp.zeros((R, 128), F32) for _ in range(2)]
            for a in range(R):
                acc[a % 2] = acc[a % 2] + mats_ref[rows(a), lanes] * vec_ref[a : a + 1, lanes]
            out_ref[:, lanes] = acc[0] + acc[1]
            return 0

        lax.fori_loop(0, count // 128, chunk, 0)

    @pl.when(jnp.logical_not(left))
    def _():
        def chunk(c, _):
            lanes = pl.ds(pl.multiple_of(c * 128, 128), 128)
            vec = vec_ref[:, lanes]
            for a in range(0, R, 8):
                sums = [
                    jnp.sum(mats_ref[rows(a + i), lanes] * vec, axis=0, keepdims=True) for i in range(8)
                ]
                out_ref[a : a + 8, lanes] = jnp.concatenate(sums, axis=0)
            return 0

        lax.fori_loop(0, count // 128, chunk, 0)


def both_modes(turn, mats_ref, vec_ref, mid_ref, out_ref):
    mode = lax.axis_index("cores")
    chips = MODES // 2
    left = (mode // 2 < chips // 2) if turn < chips // 2 else (mode // 2 >= chips // 2)
    even = (mode % 2) * RR
    base = jnp.where(left, even, RR - even)
    times(left, mats_ref, base, vec_ref, mid_ref)
    times(left, mats_ref, RR - base, mid_ref, out_ref)


def unit_at_ends(shape_):
    chip = lax.axis_index("cores") // 2
    edge = jnp.where(jnp.logical_or(chip == 0, chip == MODES // 2 - 1), 1.0, 0.0)
    return jnp.where(iota(shape_, 0) == 0, edge, 0.0)


def hop_kernel(mats_ref, *refs, turn):
    vec_ref, mid_ref, out_ref = refs if turn else (refs[2], refs[0], refs[1])
    if turn == 0:
        vec_ref[...] = unit_at_ends(vec_ref.shape)
    both_modes(turn, mats_ref, vec_ref, mid_ref, out_ref)


def finish_kernel(mats_ref, *refs):
    recv, mids = refs[0:3], refs[3:6]
    out2_ref, obs_ref, own_ref, other_ref, mid_ref, out_ref = refs[6:]
    mode = lax.axis_index("cores")
    both_modes(3, mats_ref, recv[2], mid_ref, out_ref)
    end1 = unit_at_ends(mid_ref.shape) + recv[0][...]
    mid1 = mids[0][...] + mids[1][...]
    end2 = recv[1][...] + recv[2][...]
    mid2 = mids[2][...] + mid_ref[...]
    predicted = jnp.sum((out2_ref[...] + out_ref[...]) * end1, axis=0, keepdims=True)
    residual = predicted - half_of(obs_ref[...], mode % 2 == 1)
    early = jnp.where(mode // 2 < MODES // 4, 1.0, 0.0) > 0.5
    even = (jnp.where(early, end1, end2), jnp.where(early, mid2, mid1) * residual)
    odd = (jnp.where(early, mid1, mid2), jnp.where(early, end2, end1) * residual)
    second = jnp.where(mode % 2 == 1, 1.0, 0.0) > 0.5
    for k in range(2):
        rows = slice(k * R, (k + 1) * R)
        own_ref[rows, :] = jnp.where(second, odd[k], even[k])
        other_ref[rows, :] = jnp.where(second, even[k], odd[k])


def spread(values, slot_ref, most_ref, turn, pay_ref):
    place = slot_ref[0:1, :] - turn * SLOTS
    fits = jnp.logical_and(place >= 0, place < SLOTS)
    key = jnp.where(fits, slot_ref[1:2, :] * SLOTS + place, -1)
    hi, lo = halves(values)
    both = jnp.concatenate([hi, lo], axis=0)
    peers = pay_ref.shape[0]
    count = values.shape[1]
    for pair in range(peers // 2):
        base = pair * 2 * SLOTS
        hot = (iota((2 * SLOTS, count), 0) + base == key).astype(BF16)
        out = dot_lanes(both, hot)
        out = out[:FEATS] + out[FEATS:]
        pay_ref[2 * pair] = out[:, :SLOTS]
        pay_ref[2 * pair + 1] = out[:, SLOTS:]
    for peer in range(peers):
        pay_ref[peer, 97:98, :] = most_ref[0:1, :]


def route_kernel(own_ref, got_ref, slot_ref, most_ref, pay_ref, val_ref):
    second = jnp.where(lax.axis_index("cores") % 2 == 1, 1.0, 0.0) > 0.5
    own = own_ref[...]
    got = got_ref[...]
    vecs = jnp.concatenate([jnp.where(second, got, own), jnp.where(second, own, got)], axis=1)
    loc = slot_ref[2:3, :].astype(F32)
    values = jnp.concatenate([vecs, loc, jnp.zeros((FEATS - 97, vecs.shape[1]), F32)], axis=0)
    val_ref[...] = values
    spread(values, slot_ref, most_ref, 0, pay_ref)


def again_kernel(turn_ref, val_ref, slot_ref, most_ref, pay_ref):
    spread(val_ref[...], slot_ref, most_ref, turn_ref[0], pay_ref)


def collect_kernel(step_ref, recv_ref, base_ref, out_ref, turns_ref):
    peers = recv_ref.shape[0]
    left = jnp.concatenate([recv_ref[s, 0:R, :] for s in range(peers)], axis=1)
    right = jnp.concatenate([recv_ref[s, R : 2 * R, :] for s in range(peers)], axis=1)
    loc = jnp.concatenate([recv_ref[s, 96:97, :] for s in range(peers)], axis=1).astype(jnp.int32)
    row_of = loc // WIDE
    lane_of = loc - row_of * WIDE
    count = loc.shape[1]

    def picked(x, key, n):
        hi = x.astype(BF16).astype(F32)
        lo = x - hi
        his, los = [], []
        for i in range(n):
            here = key == i
            his += [jnp.where(here, hi, 0.0).astype(BF16)]
            los += [jnp.where(here, lo, 0.0).astype(BF16)]
        return jnp.concatenate(his, axis=0), jnp.concatenate(los, axis=0)

    xh, xl = picked(left, row_of, GROUPS)
    yh, yl = picked(right, lane_of, WIDE)
    grad = dot_lanes(xh, yh) + (dot_lanes(xh, yl) + dot_lanes(xl, yh))
    out_ref[...] = base_ref[...] - step_ref[0] * grad
    most = jnp.max(recv_ref[:, 97, :]).astype(jnp.int32)
    turns_ref[0] = (most + SLOTS - 1) // SLOTS


def arrange_kernel(*refs):
    own = refs[:WAYS]
    other = refs[WAYS : 2 * WAYS]
    outs = refs[2 * WAYS :]
    even_first = jnp.where(lax.axis_index("cores") % 2 == 0, 1.0, 0.0)
    for w in range(WAYS):
        rows = slice(w * ROWS, (w + 1) * ROWS)
        mine = own[w][...]
        theirs = other[w][...]
        for k in range(2):
            stack_ref, high_ref, low_ref = outs[3 * k : 3 * k + 3]
            flag = even_first if k == 0 else 1.0 - even_first
            core = jnp.where(flag > 0.5, mine, theirs)
            hi, lo = halves(core)
            for g in range(GROUPS):
                at = 3 * (w * GROUPS + g) * R
                here = slice(g * R, (g + 1) * R)
                stack_ref[at : at + R, :] = hi[here]
                stack_ref[at + R : at + 2 * R, :] = hi[here]
                stack_ref[at + 2 * R : at + 3 * R, :] = lo[here]
            high_ref[:, rows], low_ref[:, rows] = halves(core.T)


def stacked(square):
    wide = jnp.concatenate([square, jnp.zeros((R, 128), F32)], axis=1)
    hi = wide.astype(BF16).astype(F32)
    lo = wide - hi
    return (hi + (pltpu.roll(lo, R, 1) + pltpu.roll(hi, 2 * R, 1)))[:, : 3 * R].astype(BF16)


def three(a, b):
    (ah, al), (bh, bl) = a, b
    mul = functools.partial(jnp.dot, preferred_element_type=F32)
    return mul(ah, bh) + (mul(ah, bl) + mul(al, bh))


def packed_of(full):
    lane = iota((24, 128), 1)
    return jnp.where(lane < 64, full[0:24], pltpu.roll(full[24:48], 64, 1))


def whole(packed):
    both = jnp.concatenate([packed, pltpu.roll(packed, 64, 1)], axis=0)
    return jnp.where(iota((R, 128), 1) < R, both, 0.0)


def pulled(before, core, prod_ref):
    stack, high_t, low_t = core
    if before is None:
        first = [stack[3 * g * R : 3 * g * R + R, :] for g in range(WAYS * GROUPS)]
        second = [stack[3 * g * R + 2 * R : 3 * g * R + 3 * R, :] for g in range(WAYS * GROUPS)]
        prod = (jnp.concatenate(first, axis=0), jnp.concatenate(second, axis=0))
    else:
        weights = stacked(before)
        for g in range(WAYS * GROUPS):
            prod_ref[g * R : (g + 1) * R, :] = jnp.dot(
                weights, stack[3 * g * R : 3 * (g + 1) * R, :], preferred_element_type=F32
            )
        prod = halves(prod_ref[...])
    total = jnp.zeros((R, 256), F32)
    for part, slices in ((0, range(5)), (128, range(5, WIDE))):
        cols = slice(part, part + 256)
        z = three((high_t[cols, :], low_t[cols, :]), (prod[0][:, cols], prod[1][:, cols]))
        for h in slices:
            at = h * R - part
            block = z[at : at + R]
            total = total + (pltpu.roll(block, 256 - at, 1) if at else block)
    return jnp.where(iota((R, 128), 1) < R, total[:, :128], 0.0) * (1.0 / N)


def pair_kernel(*refs, pair):
    last = pair == MODES // 2 - 1
    refs = list(refs)
    recv_ref = refs.pop(0) if pair else None
    saved = [refs.pop(0) for _ in range(pair)] if last else []
    even = [refs.pop(0) for _ in range(3)]
    odd = None if last else [refs.pop(0) for _ in range(3)]
    prod_ref = refs.pop()
    if pair:
        sum_ref = refs.pop()
        arrived = jnp.sum(recv_ref[...], axis=0)
        sum_ref[...] = arrived
        before = whole(arrived)
    else:
        before = None
    chip = lax.axis_index("cores") // 2
    live = jnp.where(chip == pair, 1.0, 0.0)
    middle = pulled(before, even, prod_ref) * live
    kept = packed_of(middle)
    if last:
        for s in saved:
            kept = kept + s[...]
        refs[0][...] = kept
        return
    out_ref, save_ref = refs
    save_ref[...] = kept
    packed = packed_of(pulled(middle, odd, prod_ref))
    for peer in range(out_ref.shape[0]):
        out_ref[peer] = packed


def final_kernel(*refs):
    pairs = MODES // 2 - 1
    sums = refs[:pairs]
    parts = refs[pairs : pairs + WAYS]
    own_ref, out_ref, prod_ref, block_ref = refs[pairs + WAYS :]
    mode = lax.axis_index("cores")
    chip = mode // 2
    first = jnp.where(mode % 2 == 0, 1.0, 0.0)
    second = 1.0 - first
    level = (parts[0][...] + parts[1][...]) + (parts[2][...] + parts[3][...])
    own = level * first
    prev = level * second
    for p in range(pairs):
        own = own + sums[p][...] * jnp.where(chip == p, second, 0.0)
        prev = prev + sums[p][...] * jnp.where(chip == p + 1, first, 0.0)
    row = iota((R, 128), 0)
    lane = iota((R, 128), 1)
    eye = jnp.where(lane == row, 1.0, 0.0)
    side = jnp.where(lane == row + 64, 1.0, 0.0)

    def start(packed, absent):
        return whole(packed) + eye * absent + side

    mats = [
        start(own, jnp.where(mode == MODES - 1, 1.0, 0.0)),
        start(prev, jnp.where(mode == 0, 1.0, 0.0)),
    ]
    mats = [[m[8 * t : 8 * t + 8] for t in range(R // 8)] for m in mats]
    for start_ in range(0, R, 4):
        top = start_ // 8
        below = range(top, R // 8)
        cols = [
            [{t: jnp.broadcast_to(m[t][:, start_ + k : start_ + k + 1], (8, 128)) for t in below} for k in range(4)]
            for m in mats
        ]
        for k in range(4):
            at = start_ + k - 8 * top
            for w in range(2):
                m, col = mats[w], cols[w]
                scale = 1.0 / col[k][top][at : at + 1]
                fact = {t: col[k][t] * scale for t in below}
                fact[top] = jnp.where(iota((8, 128), 0) > at, fact[top], 0.0)
                pivot = m[top][at : at + 1]
                for q in range(k + 1, 4):
                    lead = col[q][top][at : at + 1]
                    for t in below:
                        col[q][t] = col[q][t] - fact[t] * lead
                for t in below:
                    m[t] = m[t] - fact[t] * pivot
    mats = [jnp.concatenate(m, axis=0) for m in mats]
    tri = []
    for w in range(2):
        diag = jnp.sum(jnp.where(lane == row, mats[w], 0.0), axis=1, keepdims=True)
        tri.append(mats[w] * (1.0 / jnp.sqrt(diag)))
    carry = tri[1][:, :R]
    inv = jnp.where(lane >= 64, tri[0], 0.0)
    turned = pltpu.roll(inv, 64, 1)
    wide = jnp.concatenate([jnp.where(lane < R, turned, 0.0), jnp.zeros((R, LANES - 128), F32)], axis=1)
    for h in range(WIDE):
        block_ref[h * R : (h + 1) * R, :] = pltpu.roll(wide, h * R, 1) if h else wide
    for g in range(GROUPS):
        prod_ref[g * R : (g + 1) * R, :] = jnp.dot(
            carry, own_ref[g * R : (g + 1) * R, :], preferred_element_type=F32, precision=HIGH
        )
    out_ref[...] = dot_lanes(prod_ref[...], block_ref[...], HIGH)


def vmem():
    return pl.BlockSpec(memory_space=pltpu.VMEM)


def smem():
    return pl.BlockSpec(memory_space=pltpu.SMEM)


def call(kernel, outs, ins, scratch=(), name=None):
    return pl.pallas_call(
        kernel,
        out_shape=outs,
        in_specs=ins,
        out_specs=jax.tree.map(lambda o: smem() if o.dtype == jnp.int32 and o.size == 1 else vmem(), outs),
        scratch_shapes=list(scratch),
        compiler_params=pltpu.CompilerParams(vmem_limit_bytes=BIG),
        name=name,
    )


def shape(*dims, dtype=F32):
    return jax.ShapeDtypeStruct(dims, dtype)


def on_device(cores, indices, observed, step_size):
    peers = lax.axis_size("samp")
    count = indices.shape[0]
    slab = N // peers
    table = cores[0]
    idx = indices.T
    step = step_size.reshape(1)

    half = count // 2
    siblings = [(m, m ^ 1) for m in range(MODES)]
    other_table = lax.ppermute(table, "cores", siblings)
    steps = RR // COLS
    params = pltpu.CompilerParams(vmem_limit_bytes=BIG)
    in_specs = [
        pl.BlockSpec((MODES, count), lambda i: (0, 0)),
        pl.BlockSpec((N, COLS), lambda i: (0, i)),
    ]
    hot = [pltpu.VMEM((N, half), BF16)]
    idx, table_in = [pltpu.with_memory_space_constraint(a, pltpu.HBM) for a in (idx, table)]
    mats, slot, most = pl.pallas_call(
        functools.partial(gather_kernel, peers=peers),
        grid=(steps,),
        in_specs=in_specs,
        out_specs=[
            pl.BlockSpec((COLS, half), lambda i: (i, 0)),
            pl.BlockSpec((8, count), lambda i: (0, 0)),
            pl.BlockSpec((8, 128), lambda i: (0, 0)),
        ],
        out_shape=[shape(2 * RR, half), shape(8, count, dtype=jnp.int32), shape(8, 128)],
        scratch_shapes=hot,
        compiler_params=params,
        name="gather",
    )(idx, table_in)
    mats = pl.pallas_call(
        functools.partial(gather_kernel, peers=None),
        grid=(steps,),
        in_specs=in_specs + [pl.BlockSpec(memory_space=pl.ANY)],
        out_specs=pl.BlockSpec((COLS, half), lambda i: (i + steps, 0)),
        out_shape=shape(2 * RR, half),
        scratch_shapes=hot,
        input_output_aliases={2: 0},
        compiler_params=params,
        name="gather_other",
    )(idx, other_table, mats)

    first = lax.axis_index("samp") * slab
    kept = lax.dynamic_slice_in_dim(table, first, slab, 0)
    base = kept.reshape(GROUPS, WIDE, R, R).transpose(0, 2, 1, 3)
    base = base.reshape(ROWS, LANES)

    vec = shape(R, half)
    recv, mids = [], []
    for turn in range(3):
        mid, out = call(
            functools.partial(hop_kernel, turn=turn),
            [vec, vec],
            [vmem()] * (2 if turn else 1),
            [] if turn else [pltpu.VMEM((R, half), F32)],
            name=f"hop{turn}",
        )(mats, *recv[-1:])
        pairs = [(2 * a + h, 2 * b + h) for a, b in ((turn, turn + 1), (3 - turn, 2 - turn)) for h in range(2)]
        recv.append(lax.ppermute(out, "cores", pairs))
        mids.append(mid)
    own_vecs, other_vecs = call(
        finish_kernel,
        [shape(2 * R, half)] * 2,
        [vmem()] * 9,
        [pltpu.VMEM((R, half), F32)] * 2,
        name="finish",
    )(mats, *recv, *mids, out, observed.reshape(1, count))
    got_vecs = lax.ppermute(other_vecs, "cores", siblings)
    pay, values = call(
        route_kernel,
        (shape(peers, FEATS, SLOTS), shape(FEATS, count)),
        [vmem()] * 4,
        name="route",
    )(own_vecs, got_vecs, slot, most)

    def exchanged(block):
        return lax.all_to_all(block, "samp", 0, 0, tiled=True)

    def collected(recv, so_far):
        return call(
            collect_kernel,
            (shape(ROWS, LANES), shape(1, dtype=jnp.int32)),
            [smem(), vmem(), vmem()],
            name="collect",
        )(step, recv, so_far)

    updated, turns = collected(exchanged(pay), base)

    def more(state):
        return state[0] < turns[0]

    def another(state):
        turn, so_far = state
        pay = call(
            again_kernel,
            shape(peers, FEATS, SLOTS),
            [smem(), vmem(), vmem(), vmem()],
            name="again",
        )(turn.reshape(1), values, slot, most)
        return turn + 1, collected(exchanged(pay), so_far)[0]

    _, updated = lax.while_loop(more, another, (jnp.int32(1), updated))

    side = int(peers**0.5)

    def along(mode, peer, by):
        z, x = peer // side, peer % side
        return z * side + (x + by) % side if mode % 2 == 0 else (z + by) % side * side + x

    ring = [
        [(m * peers + p, m * peers + along(m, p, by)) for m in range(MODES) for p in range(peers)]
        for by in range(1, side)
    ]
    level = [[(p, along(1, p, by)) for p in range(peers)] for by in range(1, side)]
    own = [updated] + [lax.ppermute(updated, ("cores", "samp"), pairs) for pairs in ring]
    other = [lax.ppermute(o, "cores", siblings) for o in own]
    stack = shape(3 * WAYS * ROWS, LANES, dtype=BF16)
    flat = shape(LANES, WAYS * ROWS, dtype=BF16)
    arranged = call(arrange_kernel, [stack, flat, flat] * 2, [vmem()] * 8, name="arrange")(*own, *other)
    even, odd = list(arranged[:3]), list(arranged[3:])

    saved, sums = [], []
    recv = None
    for pair in range(MODES // 2):
        last = pair == MODES // 2 - 1
        ins = ([recv] if pair else []) + (saved if last else []) + even + ([] if last else odd)
        outs = [shape(24, 128)] if last else [shape(2 * peers, 24, 128), shape(24, 128)]
        if pair:
            outs.append(shape(24, 128))
        res = call(
            functools.partial(pair_kernel, pair=pair),
            outs,
            [vmem()] * len(ins),
            [pltpu.VMEM((WAYS * ROWS, LANES), F32)],
            name=f"pair{pair}",
        )(*ins)
        if pair:
            sums.append(res[-1])
        if last:
            parts = [res[0]] + [lax.ppermute(res[0], "samp", pairs) for pairs in level]
        else:
            saved.append(res[1])
            groups = []
            for c in (pair, pair + 2):
                for h in range(2):
                    both = [2 * (c % 4) + h, 2 * ((c + 1) % 4) + h]
                    groups.append([m * peers + j for m in both for j in range(peers)])
            recv = lax.all_to_all(
                res[0], ("cores", "samp"), 0, 0, axis_index_groups=groups, tiled=True
            )

    out = call(
        final_kernel,
        shape(ROWS, LANES),
        [vmem()] * (MODES // 2 - 1 + WAYS + 1),
        [pltpu.VMEM((ROWS, LANES), F32), pltpu.VMEM((LANES, LANES), F32)],
        name="final",
    )(*sums, *parts, updated)
    out = out.reshape(GROUPS, R, WIDE, R).transpose(0, 2, 1, 3)
    return out.reshape(1, slab, RR)


def solution(mesh):
    in_specs = (P("cores", None, None), P("samp", None), P("samp"), P())
    out_specs = P("cores", "samp", None)
    return jax.shard_map(
        on_device, mesh=mesh, in_specs=in_specs, out_specs=out_specs, check_vma=False
    )
```

```python
import functools

import jax
import jax.numpy as jnp
from jax import lax
from jax.experimental import pallas as pl
from jax.experimental.pallas import tpu as pltpu
from jax.sharding import PartitionSpec as P

R = 48
N = 512
MODES = 8
RR = R * R
GROUPS = 4
WIDE = 8
ROWS = GROUPS * R
LANES = WIDE * R
FEATS = 104
SLOTS = 128
WAYS = 4
PARTS = 2
HIGH = lax.Precision.HIGHEST
F32 = jnp.float32
BF16 = jnp.bfloat16
COLS = 768
BIG = 14 << 20


def dot_rows(a, b):
    return lax.dot_general(a, b, (((0,), (0,)), ((), ())), preferred_element_type=F32)


def dot_lanes(a, b, precision=None):
    return lax.dot_general(
        a, b, (((1,), (1,)), ((), ())), preferred_element_type=F32, precision=precision
    )


def halves(x):
    hi = x.astype(BF16)
    return hi, (x - hi.astype(F32)).astype(BF16)


def iota(shape, dim):
    return lax.broadcasted_iota(jnp.int32, shape, dim)


def ranks(row, peers, slab):
    count = row.shape[1]
    chunks = count // 128
    dest = row // slab
    hit = (iota((peers, count), 0) == dest).astype(F32)
    stacked = jnp.concatenate([hit[:, c * 128 : (c + 1) * 128] for c in range(chunks)], axis=0)
    upper = (iota((128, 128), 0) <= iota((128, 128), 1)).astype(BF16)
    inside = jnp.dot(stacked.astype(BF16), upper, preferred_element_type=F32)
    before = jnp.zeros((peers, 1), F32)
    out = []
    for c in range(chunks):
        part = inside[c * peers : (c + 1) * peers]
        mine = hit[:, c * 128 : (c + 1) * 128]
        out.append(jnp.sum(mine * (part + before), axis=0, keepdims=True))
        before = before + part[:, 127:128]
    return jnp.concatenate(out, axis=1).astype(jnp.int32) - 1, dest


def half_of(row, second):
    half = row.shape[1] // 2
    flag = jnp.where(second, 1.0, 0.0)
    return jnp.where(flag > 0.5, row[:, half:], row[:, :half])


def gather_kernel(idx_ref, table_ref, *refs, peers):
    own = peers is not None
    mats_ref, *outs, hot_ref = refs if own else refs[1:]
    step = pl.program_id(0)
    mode = lax.axis_index("cores")

    @pl.when(step == 0)
    def _():
        which = mode if own else mode + 1 - 2 * (mode % 2)
        row = idx_ref[pl.ds(which, 1), :]
        half = half_of(row, mode % 2 == 1)
        hot_ref[...] = (iota(hot_ref.shape, 0) == half).astype(BF16)
        if own:
            slot_ref, most_ref = outs
            slab = N // peers
            place, dest = ranks(row, peers, slab)
            slot_ref[0:1, :] = place
            slot_ref[1:2, :] = dest
            slot_ref[2:3, :] = row - dest * slab
            slot_ref[3:8, :] = jnp.zeros((5, row.shape[1]), jnp.int32)
            every = idx_ref[...] // slab
            most = jnp.zeros((MODES, 1), F32)
            for j in range(peers):
                most = jnp.maximum(most, jnp.sum((every == j).astype(F32), axis=1, keepdims=True))
            most_ref[...] = jnp.broadcast_to(jnp.max(most, axis=0, keepdims=True), (8, 128))

    hot = hot_ref[...]
    hi, lo = halves(table_ref[...])
    mats_ref[...] = dot_rows(hi, hot) + dot_rows(lo, hot)


def times(left, mats_ref, base, first, vec_ref, out_ref):
    count = vec_ref.shape[1]

    def rows(a):
        return pl.ds(pl.multiple_of(base + a * R, 8), R)

    @pl.when(left)
    def _():
        def chunk(c, _):
            lanes = pl.ds(pl.multiple_of(c * 128, 128), 128)
            theirs = pl.ds(pl.multiple_of(c * 128 + first, 128), 128)
            acc = [jnp.zeros((R, 128), F32) for _ in range(2)]
            for a in range(R):
                acc[a % 2] = acc[a % 2] + mats_ref[rows(a), theirs] * vec_ref[a : a + 1, lanes]
            out_ref[:, lanes] = acc[0] + acc[1]
            return 0

        lax.fori_loop(0, count // 128, chunk, 0)

    @pl.when(jnp.logical_not(left))
    def _():
        def chunk(c, _):
            lanes = pl.ds(pl.multiple_of(c * 128, 128), 128)
            theirs = pl.ds(pl.multiple_of(c * 128 + first, 128), 128)
            vec = vec_ref[:, lanes]
            for a in range(0, R, 8):
                sums = [
                    jnp.sum(mats_ref[rows(a + i), theirs] * vec, axis=0, keepdims=True) for i in range(8)
                ]
                out_ref[a : a + 8, lanes] = jnp.concatenate(sums, axis=0)
            return 0

        lax.fori_loop(0, count // 128, chunk, 0)


def both_modes(turn, part, mats_ref, vec_ref, mid_ref, out_ref):
    mode = lax.axis_index("cores")
    chips = MODES // 2
    left = (mode // 2 < chips // 2) if turn < chips // 2 else (mode // 2 >= chips // 2)
    even = (mode % 2) * RR
    base = jnp.where(left, even, RR - even)
    first = part * vec_ref.shape[1]
    times(left, mats_ref, base, first, vec_ref, mid_ref)
    times(left, mats_ref, RR - base, first, mid_ref, out_ref)


def unit_at_ends(shape_):
    chip = lax.axis_index("cores") // 2
    edge = jnp.where(jnp.logical_or(chip == 0, chip == MODES // 2 - 1), 1.0, 0.0)
    return jnp.where(iota(shape_, 0) == 0, edge, 0.0)


def hop_kernel(mats_ref, *refs, turn, part):
    vec_ref, mid_ref, out_ref = refs if turn else (refs[2], refs[0], refs[1])
    if turn == 0:
        vec_ref[...] = unit_at_ends(vec_ref.shape)
    both_modes(turn, part, mats_ref, vec_ref, mid_ref, out_ref)


def finish_kernel(mats_ref, *refs):
    refs = list(refs)

    def taken():
        parts = [refs.pop(0) for _ in range(PARTS)]
        return jnp.concatenate([p[...] for p in parts], axis=1)

    recv = [taken() for _ in range(3)]
    mids = [taken() for _ in range(3)]
    out2 = taken()
    obs_ref, own_ref, other_ref, vec_ref, mid_ref, out_ref = refs
    mode = lax.axis_index("cores")
    vec_ref[...] = recv[2]
    both_modes(3, 0, mats_ref, vec_ref, mid_ref, out_ref)
    end1 = unit_at_ends(mid_ref.shape) + recv[0]
    mid1 = mids[0] + mids[1]
    end2 = recv[1] + recv[2]
    mid2 = mids[2] + mid_ref[...]
    predicted = jnp.sum((out2 + out_ref[...]) * end1, axis=0, keepdims=True)
    residual = predicted - half_of(obs_ref[...], mode % 2 == 1)
    early = jnp.where(mode // 2 < MODES // 4, 1.0, 0.0) > 0.5
    even = (jnp.where(early, end1, end2), jnp.where(early, mid2, mid1) * residual)
    odd = (jnp.where(early, mid1, mid2), jnp.where(early, end2, end1) * residual)
    second = jnp.where(mode % 2 == 1, 1.0, 0.0) > 0.5
    for k in range(2):
        rows = slice(k * R, (k + 1) * R)
        own_ref[rows, :] = jnp.where(second, odd[k], even[k])
        other_ref[rows, :] = jnp.where(second, even[k], odd[k])


def spread(values, slot_ref, most_ref, turn, pay_ref):
    place = slot_ref[0:1, :] - turn * SLOTS
    fits = jnp.logical_and(place >= 0, place < SLOTS)
    key = jnp.where(fits, slot_ref[1:2, :] * SLOTS + place, -1)
    hi, lo = halves(values)
    both = jnp.concatenate([hi, lo], axis=0)
    peers = pay_ref.shape[0]
    count = values.shape[1]
    for pair in range(peers // 2):
        base = pair * 2 * SLOTS
        hot = (iota((2 * SLOTS, count), 0) + base == key).astype(BF16)
        out = dot_lanes(both, hot)
        out = out[:FEATS] + out[FEATS:]
        pay_ref[2 * pair] = out[:, :SLOTS]
        pay_ref[2 * pair + 1] = out[:, SLOTS:]
    for peer in range(peers):
        pay_ref[peer, 97:98, :] = most_ref[0:1, :]


def route_kernel(own_ref, got_ref, slot_ref, most_ref, pay_ref, val_ref):
    second = jnp.where(lax.axis_index("cores") % 2 == 1, 1.0, 0.0) > 0.5
    own = own_ref[...]
    got = got_ref[...]
    vecs = jnp.concatenate([jnp.where(second, got, own), jnp.where(second, own, got)], axis=1)
    loc = slot_ref[2:3, :].astype(F32)
    values = jnp.concatenate([vecs, loc, jnp.zeros((FEATS - 97, vecs.shape[1]), F32)], axis=0)
    val_ref[...] = values
    spread(values, slot_ref, most_ref, 0, pay_ref)


def again_kernel(turn_ref, val_ref, slot_ref, most_ref, pay_ref):
    spread(val_ref[...], slot_ref, most_ref, turn_ref[0], pay_ref)


def collect_kernel(step_ref, recv_ref, base_ref, out_ref, turns_ref):
    peers = recv_ref.shape[0]
    left = jnp.concatenate([recv_ref[s, 0:R, :] for s in range(peers)], axis=1)
    right = jnp.concatenate([recv_ref[s, R : 2 * R, :] for s in range(peers)], axis=1)
    loc = jnp.concatenate([recv_ref[s, 96:97, :] for s in range(peers)], axis=1).astype(jnp.int32)
    row_of = loc // WIDE
    lane_of = loc - row_of * WIDE
    count = loc.shape[1]

    def picked(x, key, n):
        hi = x.astype(BF16).astype(F32)
        lo = x - hi
        his, los = [], []
        for i in range(n):
            here = key == i
            his += [jnp.where(here, hi, 0.0).astype(BF16)]
            los += [jnp.where(here, lo, 0.0).astype(BF16)]
        return jnp.concatenate(his, axis=0), jnp.concatenate(los, axis=0)

    xh, xl = picked(left, row_of, GROUPS)
    yh, yl = picked(right, lane_of, WIDE)
    grad = dot_lanes(xh, yh) + (dot_lanes(xh, yl) + dot_lanes(xl, yh))
    out_ref[...] = base_ref[...] - step_ref[0] * grad
    most = jnp.max(recv_ref[:, 97, :]).astype(jnp.int32)
    turns_ref[0] = (most + SLOTS - 1) // SLOTS


def arrange_kernel(*refs):
    own = refs[:WAYS]
    other = refs[WAYS : 2 * WAYS]
    outs = refs[2 * WAYS :]
    even_first = jnp.where(lax.axis_index("cores") % 2 == 0, 1.0, 0.0)
    for w in range(WAYS):
        rows = slice(w * ROWS, (w + 1) * ROWS)
        mine = own[w][...]
        theirs = other[w][...]
        for k in range(2):
            stack_ref, high_ref, low_ref = outs[3 * k : 3 * k + 3]
            flag = even_first if k == 0 else 1.0 - even_first
            core = jnp.where(flag > 0.5, mine, theirs)
            hi, lo = halves(core)
            for g in range(GROUPS):
                at = 3 * (w * GROUPS + g) * R
                here = slice(g * R, (g + 1) * R)
                stack_ref[at : at + R, :] = hi[here]
                stack_ref[at + R : at + 2 * R, :] = hi[here]
                stack_ref[at + 2 * R : at + 3 * R, :] = lo[here]
            high_ref[:, rows], low_ref[:, rows] = halves(core.T)


def stacked(square):
    wide = jnp.concatenate([square, jnp.zeros((R, 128), F32)], axis=1)
    hi = wide.astype(BF16).astype(F32)
    lo = wide - hi
    return (hi + (pltpu.roll(lo, R, 1) + pltpu.roll(hi, 2 * R, 1)))[:, : 3 * R].astype(BF16)


def three(a, b):
    (ah, al), (bh, bl) = a, b
    mul = functools.partial(jnp.dot, preferred_element_type=F32)
    return mul(ah, bh) + (mul(ah, bl) + mul(al, bh))


def packed_of(full):
    lane = iota((24, 128), 1)
    return jnp.where(lane < 64, full[0:24], pltpu.roll(full[24:48], 64, 1))


def whole(packed):
    both = jnp.concatenate([packed, pltpu.roll(packed, 64, 1)], axis=0)
    return jnp.where(iota((R, 128), 1) < R, both, 0.0)


def pulled(before, core, prod_ref):
    stack, high_t, low_t = core
    if before is None:
        first = [stack[3 * g * R : 3 * g * R + R, :] for g in range(WAYS * GROUPS)]
        second = [stack[3 * g * R + 2 * R : 3 * g * R + 3 * R, :] for g in range(WAYS * GROUPS)]
        prod = (jnp.concatenate(first, axis=0), jnp.concatenate(second, axis=0))
    else:
        weights = stacked(before)
        for g in range(WAYS * GROUPS):
            prod_ref[g * R : (g + 1) * R, :] = jnp.dot(
                weights, stack[3 * g * R : 3 * (g + 1) * R, :], preferred_element_type=F32
            )
        prod = halves(prod_ref[...])
    total = jnp.zeros((R, 256), F32)
    for part, slices in ((0, range(5)), (128, range(5, WIDE))):
        cols = slice(part, part + 256)
        z = three((high_t[cols, :], low_t[cols, :]), (prod[0][:, cols], prod[1][:, cols]))
        for h in slices:
            at = h * R - part
            block = z[at : at + R]
            total = total + (pltpu.roll(block, 256 - at, 1) if at else block)
    return jnp.where(iota((R, 128), 1) < R, total[:, :128], 0.0) * (1.0 / N)


def pair_kernel(*refs, pair):
    last = pair == MODES // 2 - 1
    refs = list(refs)
    recv_ref = refs.pop(0) if pair else None
    saved = [refs.pop(0) for _ in range(pair)] if last else []
    even = [refs.pop(0) for _ in range(3)]
    odd = None if last else [refs.pop(0) for _ in range(3)]
    prod_ref = refs.pop()
    if pair:
        sum_ref = refs.pop()
        arrived = jnp.sum(recv_ref[...], axis=0)
        sum_ref[...] = arrived
        before = whole(arrived)
    else:
        before = None
    chip = lax.axis_index("cores") // 2
    live = jnp.where(chip == pair, 1.0, 0.0)
    middle = pulled(before, even, prod_ref) * live
    kept = packed_of(middle)
    if last:
        for s in saved:
            kept = kept + s[...]
        refs[0][...] = kept
        return
    out_ref, save_ref = refs
    save_ref[...] = kept
    packed = packed_of(pulled(middle, odd, prod_ref))
    for peer in range(out_ref.shape[0]):
        out_ref[peer] = packed


def final_kernel(*refs):
    pairs = MODES // 2 - 1
    sums = refs[:pairs]
    parts = refs[pairs : pairs + WAYS]
    own_ref, out_ref, prod_ref, block_ref = refs[pairs + WAYS :]
    mode = lax.axis_index("cores")
    chip = mode // 2
    first = jnp.where(mode % 2 == 0, 1.0, 0.0)
    second = 1.0 - first
    level = (parts[0][...] + parts[1][...]) + (parts[2][...] + parts[3][...])
    own = level * first
    prev = level * second
    for p in range(pairs):
        own = own + sums[p][...] * jnp.where(chip == p, second, 0.0)
        prev = prev + sums[p][...] * jnp.where(chip == p + 1, first, 0.0)
    row = iota((R, 128), 0)
    lane = iota((R, 128), 1)
    eye = jnp.where(lane == row, 1.0, 0.0)
    side = jnp.where(lane == row + 64, 1.0, 0.0)

    def start(packed, absent):
        return whole(packed) + eye * absent + side

    mats = [
        start(own, jnp.where(mode == MODES - 1, 1.0, 0.0)),
        start(prev, jnp.where(mode == 0, 1.0, 0.0)),
    ]
    mats = [[m[8 * t : 8 * t + 8] for t in range(R // 8)] for m in mats]
    for start_ in range(0, R, 4):
        top = start_ // 8
        below = range(top, R // 8)
        cols = [
            [{t: jnp.broadcast_to(m[t][:, start_ + k : start_ + k + 1], (8, 128)) for t in below} for k in range(4)]
            for m in mats
        ]
        for k in range(4):
            at = start_ + k - 8 * top
            for w in range(2):
                m, col = mats[w], cols[w]
                scale = 1.0 / col[k][top][at : at + 1]
                fact = {t: col[k][t] * scale for t in below}
                fact[top] = jnp.where(iota((8, 128), 0) > at, fact[top], 0.0)
                pivot = m[top][at : at + 1]
                for q in range(k + 1, 4):
                    lead = col[q][top][at : at + 1]
                    for t in below:
                        col[q][t] = col[q][t] - fact[t] * lead
                for t in below:
                    m[t] = m[t] - fact[t] * pivot
    mats = [jnp.concatenate(m, axis=0) for m in mats]
    tri = []
    for w in range(2):
        diag = jnp.sum(jnp.where(lane == row, mats[w], 0.0), axis=1, keepdims=True)
        tri.append(mats[w] * (1.0 / jnp.sqrt(diag)))
    carry = tri[1][:, :R]
    inv = jnp.where(lane >= 64, tri[0], 0.0)
    turned = pltpu.roll(inv, 64, 1)
    wide = jnp.concatenate([jnp.where(lane < R, turned, 0.0), jnp.zeros((R, LANES - 128), F32)], axis=1)
    for h in range(WIDE):
        block_ref[h * R : (h + 1) * R, :] = pltpu.roll(wide, h * R, 1) if h else wide
    for g in range(GROUPS):
        prod_ref[g * R : (g + 1) * R, :] = jnp.dot(
            carry, own_ref[g * R : (g + 1) * R, :], preferred_element_type=F32, precision=HIGH
        )
    out_ref[...] = dot_lanes(prod_ref[...], block_ref[...], HIGH)


def vmem():
    return pl.BlockSpec(memory_space=pltpu.VMEM)


def smem():
    return pl.BlockSpec(memory_space=pltpu.SMEM)


def call(kernel, outs, ins, scratch=(), name=None):
    return pl.pallas_call(
        kernel,
        out_shape=outs,
        in_specs=ins,
        out_specs=jax.tree.map(lambda o: smem() if o.dtype == jnp.int32 and o.size == 1 else vmem(), outs),
        scratch_shapes=list(scratch),
        compiler_params=pltpu.CompilerParams(vmem_limit_bytes=BIG),
        name=name,
    )


def shape(*dims, dtype=F32):
    return jax.ShapeDtypeStruct(dims, dtype)


def on_device(cores, indices, observed, step_size):
    peers = lax.axis_size("samp")
    count = indices.shape[0]
    slab = N // peers
    table = cores[0]
    idx = indices.T
    step = step_size.reshape(1)

    half = count // 2
    siblings = [(m, m ^ 1) for m in range(MODES)]
    other_table = lax.ppermute(table, "cores", siblings)
    steps = RR // COLS
    params = pltpu.CompilerParams(vmem_limit_bytes=BIG)
    in_specs = [
        pl.BlockSpec((MODES, count), lambda i: (0, 0)),
        pl.BlockSpec((N, COLS), lambda i: (0, i)),
    ]
    hot = [pltpu.VMEM((N, half), BF16)]
    idx, table_in = [pltpu.with_memory_space_constraint(a, pltpu.HBM) for a in (idx, table)]
    mats, slot, most = pl.pallas_call(
        functools.partial(gather_kernel, peers=peers),
        grid=(steps,),
        in_specs=in_specs,
        out_specs=[
            pl.BlockSpec((COLS, half), lambda i: (i, 0)),
            pl.BlockSpec((8, count), lambda i: (0, 0)),
            pl.BlockSpec((8, 128), lambda i: (0, 0)),
        ],
        out_shape=[shape(2 * RR, half), shape(8, count, dtype=jnp.int32), shape(8, 128)],
        scratch_shapes=hot,
        compiler_params=params,
        name="gather",
    )(idx, table_in)
    mats = pl.pallas_call(
        functools.partial(gather_kernel, peers=None),
        grid=(steps,),
        in_specs=in_specs + [pl.BlockSpec(memory_space=pl.ANY)],
        out_specs=pl.BlockSpec((COLS, half), lambda i: (i + steps, 0)),
        out_shape=shape(2 * RR, half),
        scratch_shapes=hot,
        input_output_aliases={2: 0},
        compiler_params=params,
        name="gather_other",
    )(idx, other_table, mats)

    first = lax.axis_index("samp") * slab
    kept = lax.dynamic_slice_in_dim(table, first, slab, 0)
    base = kept.reshape(GROUPS, WIDE, R, R).transpose(0, 2, 1, 3)
    base = base.reshape(ROWS, LANES)

    vec = shape(R, half // PARTS)
    recv, mids, outs = [], [], [None] * PARTS
    for turn in range(3):
        pairs = [(2 * a + h, 2 * b + h) for a, b in ((turn, turn + 1), (3 - turn, 2 - turn)) for h in range(2)]
        arrived = []
        for part in range(PARTS):
            mid, out = call(
                functools.partial(hop_kernel, turn=turn, part=part),
                [vec, vec],
                [vmem()] * (2 if turn else 1),
                [] if turn else [pltpu.VMEM(vec.shape, F32)],
                name=f"hop{turn}_{part}",
            )(mats, *([recv[-PARTS + part]] if turn else []))
            arrived.append(lax.ppermute(out, "cores", pairs))
            mids.append(mid)
            outs[part] = out
        recv += arrived
    own_vecs, other_vecs = call(
        finish_kernel,
        [shape(2 * R, half)] * 2,
        [vmem()] * (7 * PARTS + 2),
        [pltpu.VMEM((R, half), F32)] * 3,
        name="finish",
    )(mats, *recv, *mids, *outs, observed.reshape(1, count))
    got_vecs = lax.ppermute(other_vecs, "cores", siblings)
    pay, values = call(
        route_kernel,
        (shape(peers, FEATS, SLOTS), shape(FEATS, count)),
        [vmem()] * 4,
        name="route",
    )(own_vecs, got_vecs, slot, most)

    def exchanged(block):
        return lax.all_to_all(block, "samp", 0, 0, tiled=True)

    def collected(recv, so_far):
        return call(
            collect_kernel,
            (shape(ROWS, LANES), shape(1, dtype=jnp.int32)),
            [smem(), vmem(), vmem()],
            name="collect",
        )(step, recv, so_far)

    updated, turns = collected(exchanged(pay), base)

    def more(state):
        return state[0] < turns[0]

    def another(state):
        turn, so_far = state
        pay = call(
            again_kernel,
            shape(peers, FEATS, SLOTS),
            [smem(), vmem(), vmem(), vmem()],
            name="again",
        )(turn.reshape(1), values, slot, most)
        return turn + 1, collected(exchanged(pay), so_far)[0]

    _, updated = lax.while_loop(more, another, (jnp.int32(1), updated))

    side = int(peers**0.5)

    def along(mode, peer, by):
        z, x = peer // side, peer % side
        return z * side + (x + by) % side if mode % 2 == 0 else (z + by) % side * side + x

    ring = [
        [(m * peers + p, m * peers + along(m, p, by)) for m in range(MODES) for p in range(peers)]
        for by in range(1, side)
    ]
    level = [[(p, along(1, p, by)) for p in range(peers)] for by in range(1, side)]
    own = [updated] + [lax.ppermute(updated, ("cores", "samp"), pairs) for pairs in ring]
    other = [lax.ppermute(o, "cores", siblings) for o in own]
    stack = shape(3 * WAYS * ROWS, LANES, dtype=BF16)
    flat = shape(LANES, WAYS * ROWS, dtype=BF16)
    arranged = call(arrange_kernel, [stack, flat, flat] * 2, [vmem()] * 8, name="arrange")(*own, *other)
    even, odd = list(arranged[:3]), list(arranged[3:])

    saved, sums = [], []
    recv = None
    for pair in range(MODES // 2):
        last = pair == MODES // 2 - 1
        ins = ([recv] if pair else []) + (saved if last else []) + even + ([] if last else odd)
        outs = [shape(24, 128)] if last else [shape(2 * peers, 24, 128), shape(24, 128)]
        if pair:
            outs.append(shape(24, 128))
        res = call(
            functools.partial(pair_kernel, pair=pair),
            outs,
            [vmem()] * len(ins),
            [pltpu.VMEM((WAYS * ROWS, LANES), F32)],
            name=f"pair{pair}",
        )(*ins)
        if pair:
            sums.append(res[-1])
        if last:
            parts = [res[0]] + [lax.ppermute(res[0], "samp", pairs) for pairs in level]
        else:
            saved.append(res[1])
            groups = []
            for c in (pair, pair + 2):
                for h in range(2):
                    both = [2 * (c % 4) + h, 2 * ((c + 1) % 4) + h]
                    groups.append([m * peers + j for m in both for j in range(peers)])
            recv = lax.all_to_all(
                res[0], ("cores", "samp"), 0, 0, axis_index_groups=groups, tiled=True
            )

    out = call(
        final_kernel,
        shape(ROWS, LANES),
        [vmem()] * (MODES // 2 - 1 + WAYS + 1),
        [pltpu.VMEM((ROWS, LANES), F32), pltpu.VMEM((LANES, LANES), F32)],
        name="final",
    )(*sums, *parts, updated)
    out = out.reshape(GROUPS, R, WIDE, R).transpose(0, 2, 1, 3)
    return out.reshape(1, slab, RR)


def solution(mesh):
    in_specs = (P("cores", None, None), P("samp", None), P("samp"), P())
    out_specs = P("cores", "samp", None)
    return jax.shard_map(
        on_device, mesh=mesh, in_specs=in_specs, out_specs=out_specs, check_vma=False
    )
```

```python
import functools

import jax
import jax.numpy as jnp
from jax import lax
from jax.experimental import pallas as pl
from jax.experimental.pallas import tpu as pltpu
from jax.sharding import PartitionSpec as P

R = 48
N = 512
MODES = 8
RR = R * R
GROUPS = 4
WIDE = 8
ROWS = GROUPS * R
LANES = WIDE * R
FEATS = 104
SLOTS = 128
WAYS = 4
HIGH = lax.Precision.HIGHEST
F32 = jnp.float32
BF16 = jnp.bfloat16
COLS = 768
BIG = 14 << 20


def dot_rows(a, b):
    return lax.dot_general(a, b, (((0,), (0,)), ((), ())), preferred_element_type=F32)


def dot_lanes(a, b, precision=None):
    return lax.dot_general(
        a, b, (((1,), (1,)), ((), ())), preferred_element_type=F32, precision=precision
    )


def halves(x):
    hi = x.astype(BF16)
    return hi, (x - hi.astype(F32)).astype(BF16)


def iota(shape, dim):
    return lax.broadcasted_iota(jnp.int32, shape, dim)


def ranks(row, peers, slab):
    count = row.shape[1]
    chunks = count // 128
    dest = row // slab
    hit = (iota((peers, count), 0) == dest).astype(F32)
    stacked = jnp.concatenate([hit[:, c * 128 : (c + 1) * 128] for c in range(chunks)], axis=0)
    upper = (iota((128, 128), 0) <= iota((128, 128), 1)).astype(BF16)
    inside = jnp.dot(stacked.astype(BF16), upper, preferred_element_type=F32)
    before = jnp.zeros((peers, 1), F32)
    out = []
    for c in range(chunks):
        part = inside[c * peers : (c + 1) * peers]
        mine = hit[:, c * 128 : (c + 1) * 128]
        out.append(jnp.sum(mine * (part + before), axis=0, keepdims=True))
        before = before + part[:, 127:128]
    return jnp.concatenate(out, axis=1).astype(jnp.int32) - 1, dest


def half_of(row, second):
    half = row.shape[1] // 2
    flag = jnp.where(second, 1.0, 0.0)
    return jnp.where(flag > 0.5, row[:, half:], row[:, :half])


def gather_kernel(idx_ref, table_ref, *refs, peers):
    own = peers is not None
    mats_ref, *outs, hot_ref = refs if own else refs[1:]
    step = pl.program_id(0)
    mode = lax.axis_index("cores")

    @pl.when(step == 0)
    def _():
        which = mode if own else mode + 1 - 2 * (mode % 2)
        row = idx_ref[pl.ds(which, 1), :]
        half = half_of(row, mode % 2 == 1)
        hot_ref[...] = (iota(hot_ref.shape, 0) == half).astype(BF16)
        if own:
            slot_ref, most_ref = outs
            slab = N // peers
            place, dest = ranks(row, peers, slab)
            slot_ref[0:1, :] = place
            slot_ref[1:2, :] = dest
            slot_ref[2:3, :] = row - dest * slab
            slot_ref[3:8, :] = jnp.zeros((5, row.shape[1]), jnp.int32)
            every = idx_ref[...] // slab
            most = jnp.zeros((MODES, 1), F32)
            for j in range(peers):
                most = jnp.maximum(most, jnp.sum((every == j).astype(F32), axis=1, keepdims=True))
            most_ref[...] = jnp.broadcast_to(jnp.max(most, axis=0, keepdims=True), (8, 128))

    hot = hot_ref[...]
    hi, lo = halves(table_ref[...])
    mats_ref[...] = dot_rows(hi, hot) + dot_rows(lo, hot)


def times(left, mats_ref, base, vec_ref, out_ref):
    count = vec_ref.shape[1]

    def rows(a):
        return pl.ds(pl.multiple_of(base + a * R, 8), R)

    @pl.when(left)
    def _():
        def chunk(c, _):
            lanes = pl.ds(pl.multiple_of(c * 128, 128), 128)
            acc = [jnp.zeros((R, 128), F32) for _ in range(2)]
            for a in range(R):
                acc[a % 2] = acc[a % 2] + mats_ref[rows(a), lanes] * vec_ref[a : a + 1, lanes]
            out_ref[:, lanes] = acc[0] + acc[1]
            return 0

        lax.fori_loop(0, count // 128, chunk, 0)

    @pl.when(jnp.logical_not(left))
    def _():
        def chunk(c, _):
            lanes = pl.ds(pl.multiple_of(c * 128, 128), 128)
            vec = vec_ref[:, lanes]
            for a in range(0, R, 8):
                sums = [
                    jnp.sum(mats_ref[rows(a + i), lanes] * vec, axis=0, keepdims=True) for i in range(8)
                ]
                out_ref[a : a + 8, lanes] = jnp.concatenate(sums, axis=0)
            return 0

        lax.fori_loop(0, count // 128, chunk, 0)


def both_modes(turn, mats_ref, vec_ref, mid_ref, out_ref):
    mode = lax.axis_index("cores")
    chips = MODES // 2
    left = (mode // 2 < chips // 2) if turn < chips // 2 else (mode // 2 >= chips // 2)
    even = (mode % 2) * RR
    base = jnp.where(left, even, RR - even)
    times(left, mats_ref, base, vec_ref, mid_ref)
    times(left, mats_ref, RR - base, mid_ref, out_ref)


def unit_at_ends(shape_):
    chip = lax.axis_index("cores") // 2
    edge = jnp.where(jnp.logical_or(chip == 0, chip == MODES // 2 - 1), 1.0, 0.0)
    return jnp.where(iota(shape_, 0) == 0, edge, 0.0)


def hop_kernel(mats_ref, *refs, turn):
    vec_ref, mid_ref, out_ref = refs if turn else (refs[2], refs[0], refs[1])
    chip = lax.axis_index("cores") // 2
    live = jnp.logical_or(chip == turn, chip == MODES // 2 - 1 - turn)

    @pl.when(live)
    def _():
        if turn == 0:
            vec_ref[...] = unit_at_ends(vec_ref.shape)
        both_modes(turn, mats_ref, vec_ref, mid_ref, out_ref)

    @pl.when(jnp.logical_not(live))
    def _():
        mid_ref[...] = jnp.zeros(mid_ref.shape, F32)
        out_ref[...] = jnp.zeros(out_ref.shape, F32)


def finish_kernel(mats_ref, *refs):
    recv, mids = refs[0:3], refs[3:6]
    out2_ref, obs_ref, own_ref, other_ref, mid_ref, out_ref = refs[6:]
    mode = lax.axis_index("cores")
    both_modes(3, mats_ref, recv[2], mid_ref, out_ref)
    end1 = unit_at_ends(mid_ref.shape) + recv[0][...]
    mid1 = mids[0][...] + mids[1][...]
    end2 = recv[1][...] + recv[2][...]
    mid2 = mids[2][...] + mid_ref[...]
    predicted = jnp.sum((out2_ref[...] + out_ref[...]) * end1, axis=0, keepdims=True)
    residual = predicted - half_of(obs_ref[...], mode % 2 == 1)
    early = jnp.where(mode // 2 < MODES // 4, 1.0, 0.0) > 0.5
    even = (jnp.where(early, end1, end2), jnp.where(early, mid2, mid1) * residual)
    odd = (jnp.where(early, mid1, mid2), jnp.where(early, end2, end1) * residual)
    second = jnp.where(mode % 2 == 1, 1.0, 0.0) > 0.5
    for k in range(2):
        rows = slice(k * R, (k + 1) * R)
        own_ref[rows, :] = jnp.where(second, odd[k], even[k])
        other_ref[rows, :] = jnp.where(second, even[k], odd[k])


def spread(values, slot_ref, most_ref, turn, pay_ref):
    place = slot_ref[0:1, :] - turn * SLOTS
    fits = jnp.logical_and(place >= 0, place < SLOTS)
    key = jnp.where(fits, slot_ref[1:2, :] * SLOTS + place, -1)
    hi, lo = halves(values)
    both = jnp.concatenate([hi, lo], axis=0)
    peers = pay_ref.shape[0]
    count = values.shape[1]
    for pair in range(peers // 2):
        base = pair * 2 * SLOTS
        hot = (iota((2 * SLOTS, count), 0) + base == key).astype(BF16)
        out = dot_lanes(both, hot)
        out = out[:FEATS] + out[FEATS:]
        pay_ref[2 * pair] = out[:, :SLOTS]
        pay_ref[2 * pair + 1] = out[:, SLOTS:]
    for peer in range(peers):
        pay_ref[peer, 97:98, :] = most_ref[0:1, :]


def route_kernel(own_ref, got_ref, slot_ref, most_ref, pay_ref, val_ref):
    second = jnp.where(lax.axis_index("cores") % 2 == 1, 1.0, 0.0) > 0.5
    own = own_ref[...]
    got = got_ref[...]
    vecs = jnp.concatenate([jnp.where(second, got, own), jnp.where(second, own, got)], axis=1)
    loc = slot_ref[2:3, :].astype(F32)
    values = jnp.concatenate([vecs, loc, jnp.zeros((FEATS - 97, vecs.shape[1]), F32)], axis=0)
    val_ref[...] = values
    spread(values, slot_ref, most_ref, 0, pay_ref)


def again_kernel(turn_ref, val_ref, slot_ref, most_ref, pay_ref):
    spread(val_ref[...], slot_ref, most_ref, turn_ref[0], pay_ref)


def collect_kernel(step_ref, recv_ref, base_ref, out_ref, turns_ref):
    peers = recv_ref.shape[0]
    left = jnp.concatenate([recv_ref[s, 0:R, :] for s in range(peers)], axis=1)
    right = jnp.concatenate([recv_ref[s, R : 2 * R, :] for s in range(peers)], axis=1)
    loc = jnp.concatenate([recv_ref[s, 96:97, :] for s in range(peers)], axis=1).astype(jnp.int32)
    row_of = loc // WIDE
    lane_of = loc - row_of * WIDE
    count = loc.shape[1]

    def picked(x, key, n):
        hi = x.astype(BF16).astype(F32)
        lo = x - hi
        his, los = [], []
        for i in range(n):
            here = key == i
            his += [jnp.where(here, hi, 0.0).astype(BF16)]
            los += [jnp.where(here, lo, 0.0).astype(BF16)]
        return jnp.concatenate(his, axis=0), jnp.concatenate(los, axis=0)

    xh, xl = picked(left, row_of, GROUPS)
    yh, yl = picked(right, lane_of, WIDE)
    grad = dot_lanes(xh, yh) + (dot_lanes(xh, yl) + dot_lanes(xl, yh))
    out_ref[...] = base_ref[...] - step_ref[0] * grad
    most = jnp.max(recv_ref[:, 97, :]).astype(jnp.int32)
    turns_ref[0] = (most + SLOTS - 1) // SLOTS


def arrange_kernel(*refs, last):
    n = 2 if last else WAYS - 1
    own, other = refs[:n], refs[n : 2 * n]
    outs = refs[-6:]
    if last:
        slabs = [tuple(jnp.concatenate([r[...] for r in side], axis=0) for side in (own, other))]
    else:
        slabs = [(own[w][...], other[w][...]) for w in range(n)]
    even_first = jnp.where(lax.axis_index("cores") % 2 == 0, 1.0, 0.0)
    for w, (mine, theirs) in enumerate(slabs, WAYS - 1 if last else 0):
        rows = slice(w * ROWS, (w + 1) * ROWS)
        for k in range(2):
            stack_ref, high_ref, low_ref = outs[3 * k : 3 * k + 3]
            flag = even_first if k == 0 else 1.0 - even_first
            core = jnp.where(flag > 0.5, mine, theirs)
            hi, lo = halves(core)
            for g in range(GROUPS):
                at = 3 * (w * GROUPS + g) * R
                here = slice(g * R, (g + 1) * R)
                stack_ref[at : at + R, :] = hi[here]
                stack_ref[at + R : at + 2 * R, :] = hi[here]
                stack_ref[at + 2 * R : at + 3 * R, :] = lo[here]
            high_ref[:, rows], low_ref[:, rows] = halves(core.T)


def stacked(square):
    wide = jnp.concatenate([square, jnp.zeros((R, 128), F32)], axis=1)
    hi = wide.astype(BF16).astype(F32)
    lo = wide - hi
    return (hi + (pltpu.roll(lo, R, 1) + pltpu.roll(hi, 2 * R, 1)))[:, : 3 * R].astype(BF16)


def three(a, b):
    (ah, al), (bh, bl) = a, b
    mul = functools.partial(jnp.dot, preferred_element_type=F32)
    return mul(ah, bh) + (mul(ah, bl) + mul(al, bh))


def packed_of(full):
    lane = iota((24, 128), 1)
    return jnp.where(lane < 64, full[0:24], pltpu.roll(full[24:48], 64, 1))


def whole(packed):
    both = jnp.concatenate([packed, pltpu.roll(packed, 64, 1)], axis=0)
    return jnp.where(iota((R, 128), 1) < R, both, 0.0)


def pulled(before, core, prod_ref):
    stack, high_t, low_t = core
    if before is None:
        first = [stack[3 * g * R : 3 * g * R + R, :] for g in range(WAYS * GROUPS)]
        second = [stack[3 * g * R + 2 * R : 3 * g * R + 3 * R, :] for g in range(WAYS * GROUPS)]
        prod = (jnp.concatenate(first, axis=0), jnp.concatenate(second, axis=0))
    else:
        weights = stacked(before)
        for g in range(WAYS * GROUPS):
            prod_ref[g * R : (g + 1) * R, :] = jnp.dot(
                weights, stack[3 * g * R : 3 * (g + 1) * R, :], preferred_element_type=F32
            )
        prod = halves(prod_ref[...])
    total = jnp.zeros((R, 256), F32)
    for part, slices in ((0, range(5)), (128, range(5, WIDE))):
        cols = slice(part, part + 256)
        z = three((high_t[cols, :], low_t[cols, :]), (prod[0][:, cols], prod[1][:, cols]))
        for h in slices:
            at = h * R - part
            block = z[at : at + R]
            total = total + (pltpu.roll(block, 256 - at, 1) if at else block)
    return jnp.where(iota((R, 128), 1) < R, total[:, :128], 0.0) * (1.0 / N)


def pair_kernel(*refs, pair):
    last = pair == MODES // 2 - 1
    refs = list(refs)
    recv_ref = refs.pop(0) if pair else None
    saved = [refs.pop(0) for _ in range(pair)] if last else []
    even = [refs.pop(0) for _ in range(3)]
    odd = None if last else [refs.pop(0) for _ in range(3)]
    prod_ref = refs.pop()
    if pair:
        sum_ref = refs.pop()
        arrived = jnp.sum(recv_ref[...], axis=0)
        sum_ref[...] = arrived
        before = whole(arrived)
    else:
        before = None
    chip = lax.axis_index("cores") // 2
    live = jnp.where(chip == pair, 1.0, 0.0)
    middle = pulled(before, even, prod_ref) * live
    kept = packed_of(middle)
    if last:
        for s in saved:
            kept = kept + s[...]
        refs[0][...] = kept
        return
    out_ref, save_ref = refs
    save_ref[...] = kept
    packed = packed_of(pulled(middle, odd, prod_ref))
    for peer in range(out_ref.shape[0]):
        out_ref[peer] = packed


def final_kernel(*refs):
    pairs = MODES // 2 - 1
    sums = refs[:pairs]
    parts = refs[pairs : pairs + WAYS]
    own_ref, out_ref, prod_ref, block_ref = refs[pairs + WAYS :]
    mode = lax.axis_index("cores")
    chip = mode // 2
    first = jnp.where(mode % 2 == 0, 1.0, 0.0)
    second = 1.0 - first
    level = (parts[0][...] + parts[1][...]) + (parts[2][...] + parts[3][...])
    own = level * first
    prev = level * second
    for p in range(pairs):
        own = own + sums[p][...] * jnp.where(chip == p, second, 0.0)
        prev = prev + sums[p][...] * jnp.where(chip == p + 1, first, 0.0)
    row = iota((R, 128), 0)
    lane = iota((R, 128), 1)
    eye = jnp.where(lane == row, 1.0, 0.0)
    side = jnp.where(lane == row + 64, 1.0, 0.0)

    def start(packed, absent):
        return whole(packed) + eye * absent + side

    mats = [
        start(own, jnp.where(mode == MODES - 1, 1.0, 0.0)),
        start(prev, jnp.where(mode == 0, 1.0, 0.0)),
    ]
    mats = [[m[8 * t : 8 * t + 8] for t in range(R // 8)] for m in mats]
    for start_ in range(0, R, 4):
        top = start_ // 8
        below = range(top, R // 8)
        cols = [
            [{t: jnp.broadcast_to(m[t][:, start_ + k : start_ + k + 1], (8, 128)) for t in below} for k in range(4)]
            for m in mats
        ]
        for k in range(4):
            at = start_ + k - 8 * top
            for w in range(2):
                m, col = mats[w], cols[w]
                scale = 1.0 / col[k][top][at : at + 1]
                fact = {t: col[k][t] * scale for t in below}
                fact[top] = jnp.where(iota((8, 128), 0) > at, fact[top], 0.0)
                pivot = m[top][at : at + 1]
                for q in range(k + 1, 4):
                    lead = col[q][top][at : at + 1]
                    for t in below:
                        col[q][t] = col[q][t] - fact[t] * lead
                for t in below:
                    m[t] = m[t] - fact[t] * pivot
    mats = [jnp.concatenate(m, axis=0) for m in mats]
    tri = []
    for w in range(2):
        diag = jnp.sum(jnp.where(lane == row, mats[w], 0.0), axis=1, keepdims=True)
        tri.append(mats[w] * (1.0 / jnp.sqrt(diag)))
    carry = tri[1][:, :R]
    inv = jnp.where(lane >= 64, tri[0], 0.0)
    turned = pltpu.roll(inv, 64, 1)
    wide = jnp.concatenate([jnp.where(lane < R, turned, 0.0), jnp.zeros((R, LANES - 128), F32)], axis=1)
    for h in range(WIDE):
        block_ref[h * R : (h + 1) * R, :] = pltpu.roll(wide, h * R, 1) if h else wide
    for g in range(GROUPS):
        prod_ref[g * R : (g + 1) * R, :] = jnp.dot(
            carry, own_ref[g * R : (g + 1) * R, :], preferred_element_type=F32, precision=HIGH
        )
    out_ref[...] = dot_lanes(prod_ref[...], block_ref[...], HIGH)


def vmem():
    return pl.BlockSpec(memory_space=pltpu.VMEM)


def smem():
    return pl.BlockSpec(memory_space=pltpu.SMEM)


def call(kernel, outs, ins, scratch=(), name=None, aliases={}):
    return pl.pallas_call(
        kernel,
        out_shape=outs,
        in_specs=ins,
        out_specs=jax.tree.map(lambda o: smem() if o.dtype == jnp.int32 and o.size == 1 else vmem(), outs),
        scratch_shapes=list(scratch),
        input_output_aliases=aliases,
        compiler_params=pltpu.CompilerParams(vmem_limit_bytes=BIG),
        name=name,
    )


def shape(*dims, dtype=F32):
    return jax.ShapeDtypeStruct(dims, dtype)


def on_device(cores, indices, observed, step_size):
    peers = lax.axis_size("samp")
    count = indices.shape[0]
    slab = N // peers
    table = cores[0]
    idx = indices.T
    step = step_size.reshape(1)

    half = count // 2
    siblings = [(m, m ^ 1) for m in range(MODES)]
    other_table = lax.ppermute(table, "cores", siblings)
    steps = RR // COLS
    params = pltpu.CompilerParams(vmem_limit_bytes=BIG)
    in_specs = [
        pl.BlockSpec((MODES, count), lambda i: (0, 0)),
        pl.BlockSpec((N, COLS), lambda i: (0, i)),
    ]
    hot = [pltpu.VMEM((N, half), BF16)]
    idx, table_in = [pltpu.with_memory_space_constraint(a, pltpu.HBM) for a in (idx, table)]
    mats, slot, most = pl.pallas_call(
        functools.partial(gather_kernel, peers=peers),
        grid=(steps,),
        in_specs=in_specs,
        out_specs=[
            pl.BlockSpec((COLS, half), lambda i: (i, 0)),
            pl.BlockSpec((8, count), lambda i: (0, 0)),
            pl.BlockSpec((8, 128), lambda i: (0, 0)),
        ],
        out_shape=[shape(2 * RR, half), shape(8, count, dtype=jnp.int32), shape(8, 128)],
        scratch_shapes=hot,
        compiler_params=params,
        name="gather",
    )(idx, table_in)
    mats = pl.pallas_call(
        functools.partial(gather_kernel, peers=None),
        grid=(steps,),
        in_specs=in_specs + [pl.BlockSpec(memory_space=pl.ANY)],
        out_specs=pl.BlockSpec((COLS, half), lambda i: (i + steps, 0)),
        out_shape=shape(2 * RR, half),
        scratch_shapes=hot,
        input_output_aliases={2: 0},
        compiler_params=params,
        name="gather_other",
    )(idx, other_table, mats)

    first = lax.axis_index("samp") * slab
    kept = lax.dynamic_slice_in_dim(table, first, slab, 0)
    base = kept.reshape(GROUPS, WIDE, R, R).transpose(0, 2, 1, 3)
    base = base.reshape(ROWS, LANES)

    vec = shape(R, half)
    recv, mids = [], []
    for turn in range(3):
        mid, out = call(
            functools.partial(hop_kernel, turn=turn),
            [vec, vec],
            [vmem()] * (2 if turn else 1),
            [] if turn else [pltpu.VMEM((R, half), F32)],
            name=f"hop{turn}",
        )(mats, *recv[-1:])
        pairs = [(2 * a + h, 2 * b + h) for a, b in ((turn, turn + 1), (3 - turn, 2 - turn)) for h in range(2)]
        recv.append(lax.ppermute(out, "cores", pairs))
        mids.append(mid)
    own_vecs, other_vecs = call(
        finish_kernel,
        [shape(2 * R, half)] * 2,
        [vmem()] * 9,
        [pltpu.VMEM((R, half), F32)] * 2,
        name="finish",
    )(mats, *recv, *mids, out, observed.reshape(1, count))
    got_vecs = lax.ppermute(other_vecs, "cores", siblings)
    pay, values = call(
        route_kernel,
        (shape(peers, FEATS, SLOTS), shape(FEATS, count)),
        [vmem()] * 4,
        name="route",
    )(own_vecs, got_vecs, slot, most)

    def exchanged(block):
        return lax.all_to_all(block, "samp", 0, 0, tiled=True)

    def collected(recv, so_far):
        return call(
            collect_kernel,
            (shape(ROWS, LANES), shape(1, dtype=jnp.int32)),
            [smem(), vmem(), vmem()],
            name="collect",
        )(step, recv, so_far)

    updated, turns = collected(exchanged(pay), base)

    def more(state):
        return state[0] < turns[0]

    def another(state):
        turn, so_far = state
        pay = call(
            again_kernel,
            shape(peers, FEATS, SLOTS),
            [smem(), vmem(), vmem(), vmem()],
            name="again",
        )(turn.reshape(1), values, slot, most)
        return turn + 1, collected(exchanged(pay), so_far)[0]

    _, updated = lax.while_loop(more, another, (jnp.int32(1), updated))

    side = int(peers**0.5)

    def along(mode, peer, by):
        z, x = peer // side, peer % side
        return z * side + (x + by) % side if mode % 2 == 0 else (z + by) % side * side + x

    ring = [
        [(m * peers + p, m * peers + along(m, p, by)) for m in range(MODES) for p in range(peers)]
        for by in range(1, side)
    ]
    level = [[(p, along(1, p, by)) for p in range(peers)] for by in range(1, side)]
    mid = ROWS // 2

    def swapped(array):
        return lax.ppermute(array, "cores", siblings)

    ahead = lax.ppermute(updated, ("cores", "samp"), ring[0])
    behind = lax.ppermute(updated, ("cores", "samp"), ring[2])
    far = [
        lax.ppermute(ahead[:mid], ("cores", "samp"), ring[0]),
        lax.ppermute(behind[mid:], ("cores", "samp"), ring[2]),
    ]
    near = [updated, ahead, behind]
    stack = shape(3 * WAYS * ROWS, LANES, dtype=BF16)
    flat = shape(LANES, WAYS * ROWS, dtype=BF16)
    arranged = call(
        functools.partial(arrange_kernel, last=False),
        [stack, flat, flat] * 2,
        [vmem()] * 6,
        name="arrange_near",
    )(*near, *[swapped(a) for a in near])
    arranged = call(
        functools.partial(arrange_kernel, last=True),
        [stack, flat, flat] * 2,
        [vmem()] * 10,
        name="arrange_far",
        aliases={4 + i: i for i in range(6)},
    )(*far, *[swapped(a) for a in far], *arranged)
    even, odd = list(arranged[:3]), list(arranged[3:])

    saved, sums = [], []
    recv = None
    for pair in range(MODES // 2):
        last = pair == MODES // 2 - 1
        ins = ([recv] if pair else []) + (saved if last else []) + even + ([] if last else odd)
        outs = [shape(24, 128)] if last else [shape(2 * peers, 24, 128), shape(24, 128)]
        if pair:
            outs.append(shape(24, 128))
        res = call(
            functools.partial(pair_kernel, pair=pair),
            outs,
            [vmem()] * len(ins),
            [pltpu.VMEM((WAYS * ROWS, LANES), F32)],
            name=f"pair{pair}",
        )(*ins)
        if pair:
            sums.append(res[-1])
        if last:
            parts = [res[0]] + [lax.ppermute(res[0], "samp", pairs) for pairs in level]
        else:
            saved.append(res[1])
            groups = []
            for c in (pair, pair + 2):
                for h in range(2):
                    both = [2 * (c % 4) + h, 2 * ((c + 1) % 4) + h]
                    groups.append([m * peers + j for m in both for j in range(peers)])
            recv = lax.all_to_all(
                res[0], ("cores", "samp"), 0, 0, axis_index_groups=groups, tiled=True
            )

    out = call(
        final_kernel,
        shape(ROWS, LANES),
        [vmem()] * (MODES // 2 - 1 + WAYS + 1),
        [pltpu.VMEM((ROWS, LANES), F32), pltpu.VMEM((LANES, LANES), F32)],
        name="final",
    )(*sums, *parts, updated)
    out = out.reshape(GROUPS, R, WIDE, R).transpose(0, 2, 1, 3)
    return out.reshape(1, slab, RR)


def solution(mesh):
    in_specs = (P("cores", None, None), P("samp", None), P("samp"), P())
    out_specs = P("cores", "samp", None)
    return jax.shard_map(
        on_device, mesh=mesh, in_specs=in_specs, out_specs=out_specs, check_vma=False
    )
```

```python
import functools

import jax
import jax.numpy as jnp
from jax import lax
from jax.experimental import pallas as pl
from jax.experimental.pallas import tpu as pltpu
from jax.sharding import PartitionSpec as P

R = 48
N = 512
MODES = 8
RR = R * R
GROUPS = 4
WIDE = 8
ROWS = GROUPS * R
LANES = WIDE * R
FEATS = 104
SLOTS = 128
WAYS = 4
HIGH = lax.Precision.HIGHEST
F32 = jnp.float32
BF16 = jnp.bfloat16
COLS = 768
BIG = 14 << 20


def dot_rows(a, b):
    return lax.dot_general(a, b, (((0,), (0,)), ((), ())), preferred_element_type=F32)


def dot_lanes(a, b, precision=None):
    return lax.dot_general(
        a, b, (((1,), (1,)), ((), ())), preferred_element_type=F32, precision=precision
    )


def halves(x):
    hi = x.astype(BF16)
    return hi, (x - hi.astype(F32)).astype(BF16)


def iota(shape, dim):
    return lax.broadcasted_iota(jnp.int32, shape, dim)


def ranks(row, peers, slab):
    count = row.shape[1]
    chunks = count // 128
    dest = row // slab
    hit = (iota((peers, count), 0) == dest).astype(F32)
    stacked = jnp.concatenate([hit[:, c * 128 : (c + 1) * 128] for c in range(chunks)], axis=0)
    upper = (iota((128, 128), 0) <= iota((128, 128), 1)).astype(BF16)
    inside = jnp.dot(stacked.astype(BF16), upper, preferred_element_type=F32)
    before = jnp.zeros((peers, 1), F32)
    out = []
    for c in range(chunks):
        part = inside[c * peers : (c + 1) * peers]
        mine = hit[:, c * 128 : (c + 1) * 128]
        out.append(jnp.sum(mine * (part + before), axis=0, keepdims=True))
        before = before + part[:, 127:128]
    return jnp.concatenate(out, axis=1).astype(jnp.int32) - 1, dest


def half_of(row, second):
    half = row.shape[1] // 2
    flag = jnp.where(second, 1.0, 0.0)
    return jnp.where(flag > 0.5, row[:, half:], row[:, :half])


def gather_kernel(idx_ref, table_ref, *refs, peers):
    own = peers is not None
    mats_ref, *outs, hot_ref = refs if own else refs[1:]
    step = pl.program_id(0)
    mode = lax.axis_index("cores")

    @pl.when(step == 0)
    def _():
        which = mode if own else mode + 1 - 2 * (mode % 2)
        row = idx_ref[pl.ds(which, 1), :]
        half = half_of(row, mode % 2 == 1)
        hot_ref[...] = (iota(hot_ref.shape, 0) == half).astype(BF16)
        if own:
            slot_ref, most_ref = outs
            slab = N // peers
            place, dest = ranks(row, peers, slab)
            slot_ref[0:1, :] = place
            slot_ref[1:2, :] = dest
            slot_ref[2:3, :] = row - dest * slab
            slot_ref[3:8, :] = jnp.zeros((5, row.shape[1]), jnp.int32)
            every = idx_ref[...] // slab
            most = jnp.zeros((MODES, 1), F32)
            for j in range(peers):
                most = jnp.maximum(most, jnp.sum((every == j).astype(F32), axis=1, keepdims=True))
            most_ref[...] = jnp.broadcast_to(jnp.max(most, axis=0, keepdims=True), (8, 128))

    hot = hot_ref[...]
    hi, lo = halves(table_ref[...])
    mats_ref[...] = dot_rows(hi, hot) + dot_rows(lo, hot)


def times(left, mats_ref, base, vec_ref, out_ref):
    count = vec_ref.shape[1]

    def rows(a):
        return pl.ds(pl.multiple_of(base + a * R, 8), R)

    @pl.when(left)
    def _():
        def chunk(c, _):
            lanes = pl.ds(pl.multiple_of(c * 128, 128), 128)
            acc = [jnp.zeros((R, 128), F32) for _ in range(2)]
            for a in range(R):
                acc[a % 2] = acc[a % 2] + mats_ref[rows(a), lanes] * vec_ref[a : a + 1, lanes]
            out_ref[:, lanes] = acc[0] + acc[1]
            return 0

        lax.fori_loop(0, count // 128, chunk, 0)

    @pl.when(jnp.logical_not(left))
    def _():
        def chunk(c, _):
            lanes = pl.ds(pl.multiple_of(c * 128, 128), 128)
            vec = vec_ref[:, lanes]
            for a in range(0, R, 8):
                sums = [
                    jnp.sum(mats_ref[rows(a + i), lanes] * vec, axis=0, keepdims=True) for i in range(8)
                ]
                out_ref[a : a + 8, lanes] = jnp.concatenate(sums, axis=0)
            return 0

        lax.fori_loop(0, count // 128, chunk, 0)


def both_modes(turn, mats_ref, vec_ref, mid_ref, out_ref):
    mode = lax.axis_index("cores")
    chips = MODES // 2
    left = (mode // 2 < chips // 2) if turn < chips // 2 else (mode // 2 >= chips // 2)
    even = (mode % 2) * RR
    base = jnp.where(left, even, RR - even)
    times(left, mats_ref, base, vec_ref, mid_ref)
    times(left, mats_ref, RR - base, mid_ref, out_ref)


def unit_at_ends(shape_):
    chip = lax.axis_index("cores") // 2
    edge = jnp.where(jnp.logical_or(chip == 0, chip == MODES // 2 - 1), 1.0, 0.0)
    return jnp.where(iota(shape_, 0) == 0, edge, 0.0)


def hop_kernel(mats_ref, *refs, turn):
    vec_ref, mid_ref, out_ref = refs if turn else (refs[2], refs[0], refs[1])
    chip = lax.axis_index("cores") // 2
    live = jnp.logical_or(chip == turn, chip == MODES // 2 - 1 - turn)

    @pl.when(live)
    def _():
        if turn == 0:
            vec_ref[...] = unit_at_ends(vec_ref.shape)
        both_modes(turn, mats_ref, vec_ref, mid_ref, out_ref)

    @pl.when(jnp.logical_not(live))
    def _():
        mid_ref[...] = jnp.zeros(mid_ref.shape, F32)
        out_ref[...] = jnp.zeros(out_ref.shape, F32)


def finish_kernel(mats_ref, *refs):
    recv, mids = refs[0:3], refs[3:6]
    out2_ref, obs_ref, own_ref, other_ref, mid_ref, out_ref = refs[6:]
    mode = lax.axis_index("cores")
    both_modes(3, mats_ref, recv[2], mid_ref, out_ref)
    end1 = unit_at_ends(mid_ref.shape) + recv[0][...]
    mid1 = mids[0][...] + mids[1][...]
    end2 = recv[1][...] + recv[2][...]
    mid2 = mids[2][...] + mid_ref[...]
    predicted = jnp.sum((out2_ref[...] + out_ref[...]) * end1, axis=0, keepdims=True)
    residual = predicted - half_of(obs_ref[...], mode % 2 == 1)
    early = jnp.where(mode // 2 < MODES // 4, 1.0, 0.0) > 0.5
    even = (jnp.where(early, end1, end2), jnp.where(early, mid2, mid1) * residual)
    odd = (jnp.where(early, mid1, mid2), jnp.where(early, end2, end1) * residual)
    second = jnp.where(mode % 2 == 1, 1.0, 0.0) > 0.5
    for k in range(2):
        rows = slice(k * R, (k + 1) * R)
        own_ref[rows, :] = jnp.where(second, odd[k], even[k])
        other_ref[rows, :] = jnp.where(second, even[k], odd[k])


def keys(slot_ref, turn):
    place = slot_ref[0:1, :] - turn * SLOTS
    fits = jnp.logical_and(place >= 0, place < SLOTS)
    return jnp.where(fits, slot_ref[1:2, :] * SLOTS + place, -1)


def spread(values, key, pay_ref, so_far_ref=None):
    hi, lo = halves(values)
    both = jnp.concatenate([hi, lo], axis=0)
    for pair in range(pay_ref.shape[0] // 2):
        base = pair * 2 * SLOTS
        hot = (iota((2 * SLOTS, values.shape[1]), 0) + base == key).astype(BF16)
        out = dot_lanes(both, hot)
        out = out[:FEATS] + out[FEATS:]
        for k in range(2):
            part = out[:, k * SLOTS : (k + 1) * SLOTS]
            peer = 2 * pair + k
            pay_ref[peer] = part if so_far_ref is None else part + so_far_ref[peer]


def mark(most_ref, pay_ref):
    for peer in range(pay_ref.shape[0]):
        pay_ref[peer, 97:98, :] = most_ref[0:1, :]


def with_place(vecs, loc):
    pad = jnp.zeros((FEATS - 97, vecs.shape[1]), F32)
    return jnp.concatenate([vecs, loc.astype(F32), pad], axis=0)


def route_own_kernel(vecs_ref, slot_ref, pay_ref):
    second = lax.axis_index("cores") % 2 == 1
    values = with_place(vecs_ref[...], half_of(slot_ref[2:3, :], second))
    spread(values, half_of(keys(slot_ref, 0), second), pay_ref)


def route_kernel(own_ref, got_ref, slot_ref, most_ref, part_ref, pay_ref, val_ref):
    first = lax.axis_index("cores") % 2 == 0
    own = own_ref[...]
    got = got_ref[...]
    values = with_place(got, half_of(slot_ref[2:3, :], first))
    spread(values, half_of(keys(slot_ref, 0), first), pay_ref, part_ref)
    mark(most_ref, pay_ref)
    flag = jnp.where(first, 1.0, 0.0) > 0.5
    vecs = jnp.concatenate([jnp.where(flag, own, got), jnp.where(flag, got, own)], axis=1)
    val_ref[...] = with_place(vecs, slot_ref[2:3, :])


def again_kernel(turn_ref, val_ref, slot_ref, most_ref, pay_ref):
    spread(val_ref[...], keys(slot_ref, turn_ref[0]), pay_ref)
    mark(most_ref, pay_ref)


def collect_kernel(step_ref, recv_ref, base_ref, out_ref, turns_ref):
    peers = recv_ref.shape[0]
    left = jnp.concatenate([recv_ref[s, 0:R, :] for s in range(peers)], axis=1)
    right = jnp.concatenate([recv_ref[s, R : 2 * R, :] for s in range(peers)], axis=1)
    loc = jnp.concatenate([recv_ref[s, 96:97, :] for s in range(peers)], axis=1).astype(jnp.int32)
    row_of = loc // WIDE
    lane_of = loc - row_of * WIDE
    count = loc.shape[1]

    def picked(x, key, n):
        hi = x.astype(BF16).astype(F32)
        lo = x - hi
        his, los = [], []
        for i in range(n):
            here = key == i
            his += [jnp.where(here, hi, 0.0).astype(BF16)]
            los += [jnp.where(here, lo, 0.0).astype(BF16)]
        return jnp.concatenate(his, axis=0), jnp.concatenate(los, axis=0)

    xh, xl = picked(left, row_of, GROUPS)
    yh, yl = picked(right, lane_of, WIDE)
    grad = dot_lanes(xh, yh) + (dot_lanes(xh, yl) + dot_lanes(xl, yh))
    out_ref[...] = base_ref[...] - step_ref[0] * grad
    most = jnp.max(recv_ref[:, 97, :]).astype(jnp.int32)
    turns_ref[0] = (most + SLOTS - 1) // SLOTS


def arrange_kernel(*refs):
    own = refs[:WAYS]
    other = refs[WAYS : 2 * WAYS]
    outs = refs[2 * WAYS :]
    even_first = jnp.where(lax.axis_index("cores") % 2 == 0, 1.0, 0.0)
    for w in range(WAYS):
        mine = own[w][...]
        theirs = other[w][...]
        for k in range(2):
            stack_ref, turned_ref = outs[2 * k : 2 * k + 2]
            flag = even_first if k == 0 else 1.0 - even_first
            core = jnp.where(flag > 0.5, mine, theirs)
            hi, lo = halves(core)
            for g in range(GROUPS):
                at = 3 * (w * GROUPS + g) * R
                here = slice(g * R, (g + 1) * R)
                stack_ref[at : at + R, :] = hi[here]
                stack_ref[at + R : at + 2 * R, :] = hi[here]
                stack_ref[at + 2 * R : at + 3 * R, :] = lo[here]
            hi, lo = halves(core.T)
            for k3, piece in enumerate((hi, hi, lo)):
                turned_ref[:, (k3 * WAYS + w) * ROWS : (k3 * WAYS + w + 1) * ROWS] = piece


def stacked(square):
    wide = jnp.concatenate([square, jnp.zeros((R, 128), F32)], axis=1)
    hi = wide.astype(BF16).astype(F32)
    lo = wide - hi
    return (hi + (pltpu.roll(lo, R, 1) + pltpu.roll(hi, 2 * R, 1)))[:, : 3 * R].astype(BF16)


def packed_of(full):
    lane = iota((24, 128), 1)
    return jnp.where(lane < 64, full[0:24], pltpu.roll(full[24:48], 64, 1))


def whole(packed):
    both = jnp.concatenate([packed, pltpu.roll(packed, 64, 1)], axis=0)
    return jnp.where(iota((R, 128), 1) < R, both, 0.0)


def pulled(before, core, prod_ref):
    stack, turned = core
    all_rows = WAYS * ROWS
    weights = None if before is None else stacked(before)
    for g in range(WAYS * GROUPS):
        at = 3 * g * R
        if before is None:
            hi, lo = stack[at : at + R, :], stack[at + 2 * R : at + 3 * R, :]
        else:
            hi, lo = halves(
                jnp.dot(weights, stack[at : at + 3 * R, :], preferred_element_type=F32)
            )
        for k3, piece in enumerate((hi, lo, hi)):
            prod_ref[k3 * all_rows + g * R : k3 * all_rows + (g + 1) * R, :] = piece
    total = jnp.zeros((R, 256), F32)
    for part, slices in ((0, range(5)), (128, range(5, WIDE))):
        cols = slice(part, part + 256)
        z = jnp.dot(turned[cols, :], prod_ref[:, cols], preferred_element_type=F32)
        for h in slices:
            at = h * R - part
            block = z[at : at + R]
            total = total + (pltpu.roll(block, 256 - at, 1) if at else block)
    return jnp.where(iota((R, 128), 1) < R, total[:, :128], 0.0) * (1.0 / N)


def pair_kernel(*refs, pair):
    last = pair == MODES // 2 - 1
    refs = list(refs)
    recv_ref = refs.pop(0) if pair else None
    saved = [refs.pop(0) for _ in range(pair)] if last else []
    even = [refs.pop(0) for _ in range(2)]
    odd = None if last else [refs.pop(0) for _ in range(2)]
    prod_ref = refs.pop()
    if pair:
        sum_ref = refs.pop()
        arrived = jnp.sum(recv_ref[0 : recv_ref.shape[0] // 2], axis=0)
        sum_ref[...] = arrived
        before = whole(arrived)
    else:
        before = None
    chip = lax.axis_index("cores") // 2
    live = jnp.where(chip == pair, 1.0, 0.0)
    middle = pulled(before, even, prod_ref) * live
    kept = packed_of(middle)
    if last:
        for s in saved:
            kept = kept + s[...]
        refs[0][...] = kept
        return
    out_ref, save_ref = refs
    save_ref[...] = kept
    packed = packed_of(pulled(middle, odd, prod_ref))
    for peer in range(out_ref.shape[0]):
        out_ref[peer] = packed


def final_kernel(*refs):
    pairs = MODES // 2 - 1
    sums = refs[:pairs]
    parts = refs[pairs : pairs + WAYS]
    own_ref, out_ref, prod_ref, block_ref = refs[pairs + WAYS :]
    mode = lax.axis_index("cores")
    chip = mode // 2
    first = jnp.where(mode % 2 == 0, 1.0, 0.0)
    second = 1.0 - first
    level = (parts[0][...] + parts[1][...]) + (parts[2][...] + parts[3][...])
    own = level * first
    prev = level * second
    for p in range(pairs):
        own = own + sums[p][...] * jnp.where(chip == p, second, 0.0)
        prev = prev + sums[p][...] * jnp.where(chip == p + 1, first, 0.0)
    row = iota((R, 128), 0)
    lane = iota((R, 128), 1)
    eye = jnp.where(lane == row, 1.0, 0.0)
    side = jnp.where(lane == row + 64, 1.0, 0.0)

    def start(packed, absent):
        return whole(packed) + eye * absent + side

    mats = [
        start(own, jnp.where(mode == MODES - 1, 1.0, 0.0)),
        start(prev, jnp.where(mode == 0, 1.0, 0.0)),
    ]
    mats = [[m[8 * t : 8 * t + 8] for t in range(R // 8)] for m in mats]
    for start_ in range(0, R, 4):
        top = start_ // 8
        below = range(top, R // 8)
        cols = [
            [{t: jnp.broadcast_to(m[t][:, start_ + k : start_ + k + 1], (8, 128)) for t in below} for k in range(4)]
            for m in mats
        ]
        for k in range(4):
            at = start_ + k - 8 * top
            for w in range(2):
                m, col = mats[w], cols[w]
                scale = 1.0 / col[k][top][at : at + 1]
                fact = {t: col[k][t] * scale for t in below}
                fact[top] = jnp.where(iota((8, 128), 0) > at, fact[top], 0.0)
                pivot = m[top][at : at + 1]
                for q in range(k + 1, 4):
                    lead = col[q][top][at : at + 1]
                    for t in below:
                        col[q][t] = col[q][t] - fact[t] * lead
                for t in below:
                    m[t] = m[t] - fact[t] * pivot
    mats = [jnp.concatenate(m, axis=0) for m in mats]
    tri = []
    for w in range(2):
        diag = jnp.sum(jnp.where(lane == row, mats[w], 0.0), axis=1, keepdims=True)
        tri.append(mats[w] * (1.0 / jnp.sqrt(diag)))
    carry = tri[1][:, :R]
    inv = jnp.where(lane >= 64, tri[0], 0.0)
    turned = pltpu.roll(inv, 64, 1)
    wide = jnp.concatenate([jnp.where(lane < R, turned, 0.0), jnp.zeros((R, LANES - 128), F32)], axis=1)
    for h in range(WIDE):
        block_ref[h * R : (h + 1) * R, :] = pltpu.roll(wide, h * R, 1) if h else wide
    for g in range(GROUPS):
        prod_ref[g * R : (g + 1) * R, :] = jnp.dot(
            carry, own_ref[g * R : (g + 1) * R, :], preferred_element_type=F32, precision=HIGH
        )
    out_ref[...] = dot_lanes(prod_ref[...], block_ref[...], HIGH)


def vmem():
    return pl.BlockSpec(memory_space=pltpu.VMEM)


def smem():
    return pl.BlockSpec(memory_space=pltpu.SMEM)


def call(kernel, outs, ins, scratch=(), name=None):
    return pl.pallas_call(
        kernel,
        out_shape=outs,
        in_specs=ins,
        out_specs=jax.tree.map(lambda o: smem() if o.dtype == jnp.int32 and o.size == 1 else vmem(), outs),
        scratch_shapes=list(scratch),
        compiler_params=pltpu.CompilerParams(vmem_limit_bytes=BIG),
        name=name,
    )


def shape(*dims, dtype=F32):
    return jax.ShapeDtypeStruct(dims, dtype)


def on_device(cores, indices, observed, step_size):
    peers = lax.axis_size("samp")
    count = indices.shape[0]
    slab = N // peers
    table = cores[0]
    idx = indices.T
    step = step_size.reshape(1)

    half = count // 2
    siblings = [(m, m ^ 1) for m in range(MODES)]
    other_table = lax.ppermute(table, "cores", siblings)
    steps = RR // COLS
    params = pltpu.CompilerParams(vmem_limit_bytes=BIG)
    in_specs = [
        pl.BlockSpec((MODES, count), lambda i: (0, 0)),
        pl.BlockSpec((N, COLS), lambda i: (0, i)),
    ]
    hot = [pltpu.VMEM((N, half), BF16)]
    idx, table_in = [pltpu.with_memory_space_constraint(a, pltpu.HBM) for a in (idx, table)]
    mats, slot, most = pl.pallas_call(
        functools.partial(gather_kernel, peers=peers),
        grid=(steps,),
        in_specs=in_specs,
        out_specs=[
            pl.BlockSpec((COLS, half), lambda i: (i, 0)),
            pl.BlockSpec((8, count), lambda i: (0, 0)),
            pl.BlockSpec((8, 128), lambda i: (0, 0)),
        ],
        out_shape=[shape(2 * RR, half), shape(8, count, dtype=jnp.int32), shape(8, 128)],
        scratch_shapes=hot,
        compiler_params=params,
        name="gather",
    )(idx, table_in)
    mats = pl.pallas_call(
        functools.partial(gather_kernel, peers=None),
        grid=(steps,),
        in_specs=in_specs + [pl.BlockSpec(memory_space=pl.ANY)],
        out_specs=pl.BlockSpec((COLS, half), lambda i: (i + steps, 0)),
        out_shape=shape(2 * RR, half),
        scratch_shapes=hot,
        input_output_aliases={2: 0},
        compiler_params=params,
        name="gather_other",
    )(idx, other_table, mats)

    first = lax.axis_index("samp") * slab
    kept = lax.dynamic_slice_in_dim(table, first, slab, 0)
    base = kept.reshape(GROUPS, WIDE, R, R).transpose(0, 2, 1, 3)
    base = base.reshape(ROWS, LANES)

    vec = shape(R, half)
    recv, mids = [], []
    for turn in range(3):
        mid, out = call(
            functools.partial(hop_kernel, turn=turn),
            [vec, vec],
            [vmem()] * (2 if turn else 1),
            [] if turn else [pltpu.VMEM((R, half), F32)],
            name=f"hop{turn}",
        )(mats, *recv[-1:])
        pairs = [(2 * a + h, 2 * b + h) for a, b in ((turn, turn + 1), (3 - turn, 2 - turn)) for h in range(2)]
        recv.append(lax.ppermute(out, "cores", pairs))
        mids.append(mid)
    own_vecs, other_vecs = call(
        finish_kernel,
        [shape(2 * R, half)] * 2,
        [vmem()] * 9,
        [pltpu.VMEM((R, half), F32)] * 2,
        name="finish",
    )(mats, *recv, *mids, out, observed.reshape(1, count))
    got_vecs = lax.ppermute(other_vecs, "cores", siblings)
    part = call(route_own_kernel, shape(peers, FEATS, SLOTS), [vmem()] * 2, name="route_own")(own_vecs, slot)
    pay, values = call(
        route_kernel,
        (shape(peers, FEATS, SLOTS), shape(FEATS, count)),
        [vmem()] * 5,
        name="route",
    )(own_vecs, got_vecs, slot, most, part)

    def exchanged(block):
        return lax.all_to_all(block, "samp", 0, 0, tiled=True)

    def collected(recv, so_far):
        return call(
            collect_kernel,
            (shape(ROWS, LANES), shape(1, dtype=jnp.int32)),
            [smem(), vmem(), vmem()],
            name="collect",
        )(step, recv, so_far)

    updated, turns = collected(exchanged(pay), base)

    def more(state):
        return state[0] < turns[0]

    def another(state):
        turn, so_far = state
        pay = call(
            again_kernel,
            shape(peers, FEATS, SLOTS),
            [smem(), vmem(), vmem(), vmem()],
            name="again",
        )(turn.reshape(1), values, slot, most)
        return turn + 1, collected(exchanged(pay), so_far)[0]

    _, updated = lax.while_loop(more, another, (jnp.int32(1), updated))

    side = int(peers**0.5)

    def partner(mode, peer, which):
        z, x = peer // side, peer % side
        if which & 1:
            x = side - 1 - x if mode % 2 else x ^ 1
        if which & 2:
            z = side - 1 - z if mode % 2 else z ^ 1
        return z * side + x

    ring = [
        [(m * peers + p, m * peers + partner(m, p, w)) for m in range(MODES) for p in range(peers)]
        for w in range(1, WAYS)
    ]
    level = [[(p, partner(1, p, w)) for p in range(peers)] for w in range(1, WAYS)]
    own = [updated] + [lax.ppermute(updated, ("cores", "samp"), pairs) for pairs in ring]
    other = [lax.ppermute(o, "cores", siblings) for o in own]
    stack = shape(3 * WAYS * ROWS, LANES, dtype=BF16)
    flat = shape(LANES, 3 * WAYS * ROWS, dtype=BF16)
    arranged = call(arrange_kernel, [stack, flat] * 2, [vmem()] * 8, name="arrange")(*own, *other)
    even, odd = list(arranged[:2]), list(arranged[2:])

    saved, sums = [], []
    recv = None
    for pair in range(MODES // 2):
        last = pair == MODES // 2 - 1
        ins = ([recv] if pair else []) + (saved if last else []) + even + ([] if last else odd)
        outs = [shape(24, 128)] if last else [shape(2 * peers, 24, 128), shape(24, 128)]
        if pair:
            outs.append(shape(24, 128))
        res = call(
            functools.partial(pair_kernel, pair=pair),
            outs,
            [vmem()] * len(ins),
            [pltpu.VMEM((3 * WAYS * ROWS, LANES), BF16)],
            name=f"pair{pair}",
        )(*ins)
        if pair:
            sums.append(res[-1])
        if last:
            parts = [res[0]] + [lax.ppermute(res[0], "samp", pairs) for pairs in level]
        else:
            saved.append(res[1])
            groups = []
            for c in (pair, pair + 2):
                for h in range(2):
                    both = [2 * (c % 4) + h, 2 * ((c + 1) % 4) + h]
                    groups.append([m * peers + j for m in both for j in range(peers)])
            recv = lax.all_to_all(
                res[0], ("cores", "samp"), 0, 0, axis_index_groups=groups, tiled=True
            )

    out = call(
        final_kernel,
        shape(ROWS, LANES),
        [vmem()] * (MODES // 2 - 1 + WAYS + 1),
        [pltpu.VMEM((ROWS, LANES), F32), pltpu.VMEM((LANES, LANES), F32)],
        name="final",
    )(*sums, *parts, updated)
    out = out.reshape(GROUPS, R, WIDE, R).transpose(0, 2, 1, 3)
    return out.reshape(1, slab, RR)


def solution(mesh):
    in_specs = (P("cores", None, None), P("samp", None), P("samp"), P())
    out_specs = P("cores", "samp", None)
    return jax.shard_map(
        on_device, mesh=mesh, in_specs=in_specs, out_specs=out_specs, check_vma=False
    )
```

```python
import functools

import jax
import jax.numpy as jnp
from jax import lax
from jax.experimental import pallas as pl
from jax.experimental.pallas import tpu as pltpu
from jax.sharding import PartitionSpec as P

R = 48
N = 512
MODES = 8
RR = R * R
GROUPS = 4
WIDE = 8
ROWS = GROUPS * R
LANES = WIDE * R
FEATS = 104
SLOTS = 128
WAYS = 4
HIGH = lax.Precision.HIGHEST
F32 = jnp.float32
BF16 = jnp.bfloat16
COLS = 768
BIG = 14 << 20


def dot_rows(a, b):
    return lax.dot_general(a, b, (((0,), (0,)), ((), ())), preferred_element_type=F32)


def dot_lanes(a, b, precision=None):
    return lax.dot_general(
        a, b, (((1,), (1,)), ((), ())), preferred_element_type=F32, precision=precision
    )


def halves(x):
    hi = x.astype(BF16)
    return hi, (x - hi.astype(F32)).astype(BF16)


def iota(shape, dim):
    return lax.broadcasted_iota(jnp.int32, shape, dim)


def ranks(row, peers, slab):
    count = row.shape[1]
    chunks = count // 128
    dest = row // slab
    hit = (iota((peers, count), 0) == dest).astype(F32)
    stacked = jnp.concatenate([hit[:, c * 128 : (c + 1) * 128] for c in range(chunks)], axis=0)
    upper = (iota((128, 128), 0) <= iota((128, 128), 1)).astype(BF16)
    inside = jnp.dot(stacked.astype(BF16), upper, preferred_element_type=F32)
    before = jnp.zeros((peers, 1), F32)
    out = []
    for c in range(chunks):
        part = inside[c * peers : (c + 1) * peers]
        mine = hit[:, c * 128 : (c + 1) * 128]
        out.append(jnp.sum(mine * (part + before), axis=0, keepdims=True))
        before = before + part[:, 127:128]
    return jnp.concatenate(out, axis=1).astype(jnp.int32) - 1, dest


def half_of(row, second):
    half = row.shape[1] // 2
    flag = jnp.where(second, 1.0, 0.0)
    return jnp.where(flag > 0.5, row[:, half:], row[:, :half])


def gather_kernel(idx_ref, table_ref, *refs, peers):
    own = peers is not None
    mats_ref, *outs, hot_ref = refs if own else refs[1:]
    step = pl.program_id(0)
    mode = lax.axis_index("cores")

    @pl.when(step == 0)
    def _():
        which = mode if own else mode + 1 - 2 * (mode % 2)
        row = idx_ref[pl.ds(which, 1), :]
        half = half_of(row, mode % 2 == 1)
        hot_ref[...] = (iota(hot_ref.shape, 0) == half).astype(BF16)
        if own:
            slot_ref, most_ref = outs
            slab = N // peers
            place, dest = ranks(row, peers, slab)
            slot_ref[0:1, :] = place
            slot_ref[1:2, :] = dest
            slot_ref[2:3, :] = row - dest * slab
            slot_ref[3:8, :] = jnp.zeros((5, row.shape[1]), jnp.int32)
            every = idx_ref[...] // slab
            most = jnp.zeros((MODES, 1), F32)
            for j in range(peers):
                most = jnp.maximum(most, jnp.sum((every == j).astype(F32), axis=1, keepdims=True))
            most_ref[...] = jnp.broadcast_to(jnp.max(most, axis=0, keepdims=True), (8, 128))

    hot = hot_ref[...]
    hi, lo = halves(table_ref[...])
    mats_ref[...] = dot_rows(hi, hot) + dot_rows(lo, hot)


def times(left, mats_ref, base, vec_ref, out_ref):
    count = vec_ref.shape[1]

    def rows(a):
        return pl.ds(pl.multiple_of(base + a * R, 8), R)

    @pl.when(left)
    def _():
        def chunk(c, _):
            lanes = pl.ds(pl.multiple_of(c * 128, 128), 128)
            acc = [jnp.zeros((R, 128), F32) for _ in range(2)]
            for a in range(R):
                acc[a % 2] = acc[a % 2] + mats_ref[rows(a), lanes] * vec_ref[a : a + 1, lanes]
            out_ref[:, lanes] = acc[0] + acc[1]
            return 0

        lax.fori_loop(0, count // 128, chunk, 0)

    @pl.when(jnp.logical_not(left))
    def _():
        def chunk(c, _):
            lanes = pl.ds(pl.multiple_of(c * 128, 128), 128)
            vec = vec_ref[:, lanes]
            for a in range(0, R, 8):
                sums = [
                    jnp.sum(mats_ref[rows(a + i), lanes] * vec, axis=0, keepdims=True) for i in range(8)
                ]
                out_ref[a : a + 8, lanes] = jnp.concatenate(sums, axis=0)
            return 0

        lax.fori_loop(0, count // 128, chunk, 0)


def both_modes(turn, mats_ref, vec_ref, mid_ref, out_ref):
    mode = lax.axis_index("cores")
    chips = MODES // 2
    left = (mode // 2 < chips // 2) if turn < chips // 2 else (mode // 2 >= chips // 2)
    even = (mode % 2) * RR
    base = jnp.where(left, even, RR - even)
    times(left, mats_ref, base, vec_ref, mid_ref)
    times(left, mats_ref, RR - base, mid_ref, out_ref)


def unit_at_ends(shape_):
    chip = lax.axis_index("cores") // 2
    edge = jnp.where(jnp.logical_or(chip == 0, chip == MODES // 2 - 1), 1.0, 0.0)
    return jnp.where(iota(shape_, 0) == 0, edge, 0.0)


def hop_kernel(mats_ref, *refs, turn):
    vec_ref, mid_ref, out_ref = refs if turn else (refs[2], refs[0], refs[1])
    chip = lax.axis_index("cores") // 2
    live = jnp.logical_or(chip == turn, chip == MODES // 2 - 1 - turn)

    @pl.when(live)
    def _():
        if turn == 0:
            vec_ref[...] = unit_at_ends(vec_ref.shape)
        both_modes(turn, mats_ref, vec_ref, mid_ref, out_ref)

    @pl.when(jnp.logical_not(live))
    def _():
        mid_ref[...] = jnp.zeros(mid_ref.shape, F32)
        out_ref[...] = jnp.zeros(out_ref.shape, F32)


def finish_kernel(mats_ref, *refs):
    recv, mids = refs[0:3], refs[3:6]
    out2_ref, obs_ref, own_ref, other_ref, mid_ref, out_ref = refs[6:]
    mode = lax.axis_index("cores")
    both_modes(3, mats_ref, recv[2], mid_ref, out_ref)
    end1 = unit_at_ends(mid_ref.shape) + recv[0][...]
    mid1 = mids[0][...] + mids[1][...]
    end2 = recv[1][...] + recv[2][...]
    mid2 = mids[2][...] + mid_ref[...]
    predicted = jnp.sum((out2_ref[...] + out_ref[...]) * end1, axis=0, keepdims=True)
    residual = predicted - half_of(obs_ref[...], mode % 2 == 1)
    early = jnp.where(mode // 2 < MODES // 4, 1.0, 0.0) > 0.5
    even = (jnp.where(early, end1, end2), jnp.where(early, mid2, mid1) * residual)
    odd = (jnp.where(early, mid1, mid2), jnp.where(early, end2, end1) * residual)
    second = jnp.where(mode % 2 == 1, 1.0, 0.0) > 0.5
    for k in range(2):
        rows = slice(k * R, (k + 1) * R)
        own_ref[rows, :] = jnp.where(second, odd[k], even[k])
        other_ref[rows, :] = jnp.where(second, even[k], odd[k])


def keys(slot_ref, turn):
    place = slot_ref[0:1, :] - turn * SLOTS
    fits = jnp.logical_and(place >= 0, place < SLOTS)
    return jnp.where(fits, slot_ref[1:2, :] * SLOTS + place, -1)


def spread(values, key, pay_ref, so_far_ref=None):
    hi, lo = halves(values)
    both = jnp.concatenate([hi, lo], axis=0)
    for pair in range(pay_ref.shape[0] // 2):
        base = pair * 2 * SLOTS
        hot = (iota((2 * SLOTS, values.shape[1]), 0) + base == key).astype(BF16)
        out = dot_lanes(both, hot)
        out = out[:FEATS] + out[FEATS:]
        for k in range(2):
            part = out[:, k * SLOTS : (k + 1) * SLOTS]
            peer = 2 * pair + k
            pay_ref[peer] = part if so_far_ref is None else part + so_far_ref[peer]


def mark(most_ref, pay_ref):
    for peer in range(pay_ref.shape[0]):
        pay_ref[peer, 97:98, :] = most_ref[0:1, :]


def with_place(vecs, loc):
    pad = jnp.zeros((FEATS - 97, vecs.shape[1]), F32)
    return jnp.concatenate([vecs, loc.astype(F32), pad], axis=0)


def route_own_kernel(vecs_ref, slot_ref, pay_ref):
    second = lax.axis_index("cores") % 2 == 1
    values = with_place(vecs_ref[...], half_of(slot_ref[2:3, :], second))
    spread(values, half_of(keys(slot_ref, 0), second), pay_ref)


def route_kernel(own_ref, got_ref, slot_ref, most_ref, part_ref, pay_ref, val_ref):
    first = lax.axis_index("cores") % 2 == 0
    own = own_ref[...]
    got = got_ref[...]
    values = with_place(got, half_of(slot_ref[2:3, :], first))
    spread(values, half_of(keys(slot_ref, 0), first), pay_ref, part_ref)
    mark(most_ref, pay_ref)
    flag = jnp.where(first, 1.0, 0.0) > 0.5
    vecs = jnp.concatenate([jnp.where(flag, own, got), jnp.where(flag, got, own)], axis=1)
    val_ref[...] = with_place(vecs, slot_ref[2:3, :])


def again_kernel(turn_ref, val_ref, slot_ref, most_ref, pay_ref):
    spread(val_ref[...], keys(slot_ref, turn_ref[0]), pay_ref)
    mark(most_ref, pay_ref)


def collect_kernel(step_ref, recv_ref, base_ref, out_ref, turns_ref):
    peers = recv_ref.shape[0]
    left = jnp.concatenate([recv_ref[s, 0:R, :] for s in range(peers)], axis=1)
    right = jnp.concatenate([recv_ref[s, R : 2 * R, :] for s in range(peers)], axis=1)
    loc = jnp.concatenate([recv_ref[s, 96:97, :] for s in range(peers)], axis=1).astype(jnp.int32)
    row_of = loc // WIDE
    lane_of = loc - row_of * WIDE
    count = loc.shape[1]

    def picked(x, key, n):
        hi = x.astype(BF16).astype(F32)
        lo = x - hi
        his, los = [], []
        for i in range(n):
            here = key == i
            his += [jnp.where(here, hi, 0.0).astype(BF16)]
            los += [jnp.where(here, lo, 0.0).astype(BF16)]
        return jnp.concatenate(his, axis=0), jnp.concatenate(los, axis=0)

    xh, xl = picked(left, row_of, GROUPS)
    yh, yl = picked(right, lane_of, WIDE)
    grad = dot_lanes(xh, yh) + (dot_lanes(xh, yl) + dot_lanes(xl, yh))
    out_ref[...] = base_ref[...] - step_ref[0] * grad
    most = jnp.max(recv_ref[:, 97, :]).astype(jnp.int32)
    turns_ref[0] = (most + SLOTS - 1) // SLOTS


def arrange_kernel(*refs):
    own = refs[:WAYS]
    other = refs[WAYS : 2 * WAYS]
    outs = refs[2 * WAYS :]
    even_first = jnp.where(lax.axis_index("cores") % 2 == 0, 1.0, 0.0)
    for w in range(WAYS):
        mine = own[w][...]
        theirs = other[w][...]
        for k in range(2):
            stack_ref, turned_ref = outs[2 * k : 2 * k + 2]
            flag = even_first if k == 0 else 1.0 - even_first
            core = jnp.where(flag > 0.5, mine, theirs)
            hi, lo = halves(core)
            for g in range(GROUPS):
                at = 3 * (w * GROUPS + g) * R
                here = slice(g * R, (g + 1) * R)
                stack_ref[at : at + R, :] = hi[here]
                stack_ref[at + R : at + 2 * R, :] = hi[here]
                stack_ref[at + 2 * R : at + 3 * R, :] = lo[here]
            hi, lo = halves(core.T)
            for k3, piece in enumerate((hi, hi, lo)):
                turned_ref[:, (k3 * WAYS + w) * ROWS : (k3 * WAYS + w + 1) * ROWS] = piece


def stacked(square):
    wide = jnp.concatenate([square, jnp.zeros((R, 128), F32)], axis=1)
    hi = wide.astype(BF16).astype(F32)
    lo = wide - hi
    return (hi + (pltpu.roll(lo, R, 1) + pltpu.roll(hi, 2 * R, 1)))[:, : 3 * R].astype(BF16)


def packed_of(full):
    lane = iota((24, 128), 1)
    return jnp.where(lane < 64, full[0:24], pltpu.roll(full[24:48], 64, 1))


def whole(packed):
    both = jnp.concatenate([packed, pltpu.roll(packed, 64, 1)], axis=0)
    return jnp.where(iota((R, 128), 1) < R, both, 0.0)


def pulled(before, core, prod_ref):
    stack, turned = core
    all_rows = WAYS * ROWS
    weights = None if before is None else stacked(before)
    for g in range(WAYS * GROUPS):
        at = 3 * g * R
        if before is None:
            hi, lo = stack[at : at + R, :], stack[at + 2 * R : at + 3 * R, :]
        else:
            hi, lo = halves(
                jnp.dot(weights, stack[at : at + 3 * R, :], preferred_element_type=F32)
            )
        for k3, piece in enumerate((hi, lo, hi)):
            prod_ref[k3 * all_rows + g * R : k3 * all_rows + (g + 1) * R, :] = piece
    total = jnp.zeros((R, 256), F32)
    for part, slices in ((0, range(5)), (128, range(5, WIDE))):
        cols = slice(part, part + 256)
        z = jnp.dot(turned[cols, :], prod_ref[:, cols], preferred_element_type=F32)
        for h in slices:
            at = h * R - part
            block = z[at : at + R]
            total = total + (pltpu.roll(block, 256 - at, 1) if at else block)
    return jnp.where(iota((R, 128), 1) < R, total[:, :128], 0.0) * (1.0 / N)


def pair_kernel(*refs, pair):
    last = pair == MODES // 2 - 1
    refs = list(refs)
    recv_ref = refs.pop(0) if pair else None
    saved = [refs.pop(0) for _ in range(pair)] if last else []
    even = [refs.pop(0) for _ in range(2)]
    odd = None if last else [refs.pop(0) for _ in range(2)]
    prod_ref = refs.pop()
    if pair:
        sum_ref = refs.pop()
        sum_ref[...] = jnp.sum(recv_ref[0 : recv_ref.shape[0] // 2], axis=0)
    kept_ref = refs.pop()
    live = lax.axis_index("cores") // 2 == pair

    @pl.when(live)
    def _():
        middle = pulled(whole(sum_ref[...]) if pair else None, even, prod_ref)
        kept_ref[...] = packed_of(middle)
        if not last:
            packed = packed_of(pulled(middle, odd, prod_ref))
            for peer in range(refs[0].shape[0]):
                refs[0][peer] = packed

    @pl.when(jnp.logical_not(live))
    def _():
        kept = jnp.zeros((24, 128), F32)
        for s in saved:
            kept = kept + s[...]
        kept_ref[...] = kept
        if not last:
            refs[0][...] = jnp.zeros(refs[0].shape, F32)


def final_kernel(*refs):
    pairs = MODES // 2 - 1
    sums = refs[:pairs]
    parts = refs[pairs : pairs + WAYS]
    own_ref, out_ref, prod_ref, block_ref = refs[pairs + WAYS :]
    mode = lax.axis_index("cores")
    chip = mode // 2
    first = jnp.where(mode % 2 == 0, 1.0, 0.0)
    second = 1.0 - first
    level = (parts[0][...] + parts[1][...]) + (parts[2][...] + parts[3][...])
    own = level * first
    prev = level * second
    for p in range(pairs):
        own = own + sums[p][...] * jnp.where(chip == p, second, 0.0)
        prev = prev + sums[p][...] * jnp.where(chip == p + 1, first, 0.0)
    row = iota((R, 128), 0)
    lane = iota((R, 128), 1)
    eye = jnp.where(lane == row, 1.0, 0.0)
    side = jnp.where(lane == row + 64, 1.0, 0.0)

    def start(packed, absent):
        return whole(packed) + eye * absent + side

    mats = [
        start(own, jnp.where(mode == MODES - 1, 1.0, 0.0)),
        start(prev, jnp.where(mode == 0, 1.0, 0.0)),
    ]
    mats = [[m[8 * t : 8 * t + 8] for t in range(R // 8)] for m in mats]
    for start_ in range(0, R, 4):
        top = start_ // 8
        below = range(top, R // 8)
        cols = [
            [{t: jnp.broadcast_to(m[t][:, start_ + k : start_ + k + 1], (8, 128)) for t in below} for k in range(4)]
            for m in mats
        ]
        for k in range(4):
            at = start_ + k - 8 * top
            for w in range(2):
                m, col = mats[w], cols[w]
                scale = 1.0 / col[k][top][at : at + 1]
                fact = {t: col[k][t] * scale for t in below}
                fact[top] = jnp.where(iota((8, 128), 0) > at, fact[top], 0.0)
                pivot = m[top][at : at + 1]
                for q in range(k + 1, 4):
                    lead = col[q][top][at : at + 1]
                    for t in below:
                        col[q][t] = col[q][t] - fact[t] * lead
                for t in below:
                    m[t] = m[t] - fact[t] * pivot
    mats = [jnp.concatenate(m, axis=0) for m in mats]
    tri = []
    for w in range(2):
        diag = jnp.sum(jnp.where(lane == row, mats[w], 0.0), axis=1, keepdims=True)
        tri.append(mats[w] * (1.0 / jnp.sqrt(diag)))
    carry = tri[1][:, :R]
    inv = jnp.where(lane >= 64, tri[0], 0.0)
    turned = pltpu.roll(inv, 64, 1)
    wide = jnp.concatenate([jnp.where(lane < R, turned, 0.0), jnp.zeros((R, LANES - 128), F32)], axis=1)
    for h in range(WIDE):
        block_ref[h * R : (h + 1) * R, :] = pltpu.roll(wide, h * R, 1) if h else wide
    for g in range(GROUPS):
        prod_ref[g * R : (g + 1) * R, :] = jnp.dot(
            carry, own_ref[g * R : (g + 1) * R, :], preferred_element_type=F32, precision=HIGH
        )
    out_ref[...] = dot_lanes(prod_ref[...], block_ref[...], HIGH)


def vmem():
    return pl.BlockSpec(memory_space=pltpu.VMEM)


def smem():
    return pl.BlockSpec(memory_space=pltpu.SMEM)


def call(kernel, outs, ins, scratch=(), name=None):
    return pl.pallas_call(
        kernel,
        out_shape=outs,
        in_specs=ins,
        out_specs=jax.tree.map(lambda o: smem() if o.dtype == jnp.int32 and o.size == 1 else vmem(), outs),
        scratch_shapes=list(scratch),
        compiler_params=pltpu.CompilerParams(vmem_limit_bytes=BIG),
        name=name,
    )


def shape(*dims, dtype=F32):
    return jax.ShapeDtypeStruct(dims, dtype)


def on_device(cores, indices, observed, step_size):
    peers = lax.axis_size("samp")
    count = indices.shape[0]
    slab = N // peers
    table = cores[0]
    idx = indices.T
    step = step_size.reshape(1)

    half = count // 2
    siblings = [(m, m ^ 1) for m in range(MODES)]
    other_table = lax.ppermute(table, "cores", siblings)
    steps = RR // COLS
    params = pltpu.CompilerParams(vmem_limit_bytes=BIG)
    in_specs = [
        pl.BlockSpec((MODES, count), lambda i: (0, 0)),
        pl.BlockSpec((N, COLS), lambda i: (0, i)),
    ]
    hot = [pltpu.VMEM((N, half), BF16)]
    idx, table_in = [pltpu.with_memory_space_constraint(a, pltpu.HBM) for a in (idx, table)]
    mats, slot, most = pl.pallas_call(
        functools.partial(gather_kernel, peers=peers),
        grid=(steps,),
        in_specs=in_specs,
        out_specs=[
            pl.BlockSpec((COLS, half), lambda i: (i, 0)),
            pl.BlockSpec((8, count), lambda i: (0, 0)),
            pl.BlockSpec((8, 128), lambda i: (0, 0)),
        ],
        out_shape=[shape(2 * RR, half), shape(8, count, dtype=jnp.int32), shape(8, 128)],
        scratch_shapes=hot,
        compiler_params=params,
        name="gather",
    )(idx, table_in)
    mats = pl.pallas_call(
        functools.partial(gather_kernel, peers=None),
        grid=(steps,),
        in_specs=in_specs + [pl.BlockSpec(memory_space=pl.ANY)],
        out_specs=pl.BlockSpec((COLS, half), lambda i: (i + steps, 0)),
        out_shape=shape(2 * RR, half),
        scratch_shapes=hot,
        input_output_aliases={2: 0},
        compiler_params=params,
        name="gather_other",
    )(idx, other_table, mats)

    first = lax.axis_index("samp") * slab
    kept = lax.dynamic_slice_in_dim(table, first, slab, 0)
    base = kept.reshape(GROUPS, WIDE, R, R).transpose(0, 2, 1, 3)
    base = base.reshape(ROWS, LANES)

    vec = shape(R, half)
    recv, mids = [], []
    for turn in range(3):
        mid, out = call(
            functools.partial(hop_kernel, turn=turn),
            [vec, vec],
            [vmem()] * (2 if turn else 1),
            [] if turn else [pltpu.VMEM((R, half), F32)],
            name=f"hop{turn}",
        )(mats, *recv[-1:])
        pairs = [(2 * a + h, 2 * b + h) for a, b in ((turn, turn + 1), (3 - turn, 2 - turn)) for h in range(2)]
        recv.append(lax.ppermute(out, "cores", pairs))
        mids.append(mid)
    own_vecs, other_vecs = call(
        finish_kernel,
        [shape(2 * R, half)] * 2,
        [vmem()] * 9,
        [pltpu.VMEM((R, half), F32)] * 2,
        name="finish",
    )(mats, *recv, *mids, out, observed.reshape(1, count))
    got_vecs = lax.ppermute(other_vecs, "cores", siblings)
    part = call(route_own_kernel, shape(peers, FEATS, SLOTS), [vmem()] * 2, name="route_own")(own_vecs, slot)
    pay, values = call(
        route_kernel,
        (shape(peers, FEATS, SLOTS), shape(FEATS, count)),
        [vmem()] * 5,
        name="route",
    )(own_vecs, got_vecs, slot, most, part)

    def exchanged(block):
        return lax.all_to_all(block, "samp", 0, 0, tiled=True)

    def collected(recv, so_far):
        return call(
            collect_kernel,
            (shape(ROWS, LANES), shape(1, dtype=jnp.int32)),
            [smem(), vmem(), vmem()],
            name="collect",
        )(step, recv, so_far)

    updated, turns = collected(exchanged(pay), base)

    def more(state):
        return state[0] < turns[0]

    def another(state):
        turn, so_far = state
        pay = call(
            again_kernel,
            shape(peers, FEATS, SLOTS),
            [smem(), vmem(), vmem(), vmem()],
            name="again",
        )(turn.reshape(1), values, slot, most)
        return turn + 1, collected(exchanged(pay), so_far)[0]

    _, updated = lax.while_loop(more, another, (jnp.int32(1), updated))

    side = int(peers**0.5)

    def partner(mode, peer, by):
        z, x = peer // side, peer % side
        return (z + by) % side * side + x if mode % 2 else z * side + (x + by) % side

    ring = [
        [(m * peers + p, m * peers + partner(m, p, w)) for m in range(MODES) for p in range(peers)]
        for w in range(1, WAYS)
    ]
    level = [[(p, partner(1, p, w)) for p in range(peers)] for w in range(1, WAYS)]
    own = [updated] + [lax.ppermute(updated, ("cores", "samp"), pairs) for pairs in ring]
    other = [lax.ppermute(o, "cores", siblings) for o in own]
    stack = shape(3 * WAYS * ROWS, LANES, dtype=BF16)
    flat = shape(LANES, 3 * WAYS * ROWS, dtype=BF16)
    arranged = call(arrange_kernel, [stack, flat] * 2, [vmem()] * 8, name="arrange")(*own, *other)
    even, odd = list(arranged[:2]), list(arranged[2:])

    saved, sums = [], []
    recv = None
    for pair in range(MODES // 2):
        last = pair == MODES // 2 - 1
        ins = ([recv] if pair else []) + (saved if last else []) + even + ([] if last else odd)
        outs = [shape(24, 128)] if last else [shape(2 * peers, 24, 128), shape(24, 128)]
        if pair:
            outs.append(shape(24, 128))
        res = call(
            functools.partial(pair_kernel, pair=pair),
            outs,
            [vmem()] * len(ins),
            [pltpu.VMEM((3 * WAYS * ROWS, LANES), BF16)],
            name=f"pair{pair}",
        )(*ins)
        if pair:
            sums.append(res[-1])
        if last:
            parts = [res[0]] + [lax.ppermute(res[0], "samp", pairs) for pairs in level]
        else:
            saved.append(res[1])
            groups = []
            for c in (pair, pair + 2):
                for h in range(2):
                    both = [2 * (c % 4) + h, 2 * ((c + 1) % 4) + h]
                    groups.append([m * peers + j for m in both for j in range(peers)])
            recv = lax.all_to_all(
                res[0], ("cores", "samp"), 0, 0, axis_index_groups=groups, tiled=True
            )

    out = call(
        final_kernel,
        shape(ROWS, LANES),
        [vmem()] * (MODES // 2 - 1 + WAYS + 1),
        [pltpu.VMEM((ROWS, LANES), F32), pltpu.VMEM((LANES, LANES), F32)],
        name="final",
    )(*sums, *parts, updated)
    out = out.reshape(GROUPS, R, WIDE, R).transpose(0, 2, 1, 3)
    return out.reshape(1, slab, RR)


def solution(mesh):
    in_specs = (P("cores", None, None), P("samp", None), P("samp"), P())
    out_specs = P("cores", "samp", None)
    return jax.shard_map(
        on_device, mesh=mesh, in_specs=in_specs, out_specs=out_specs, check_vma=False
    )
```

```python
import functools

import jax
import jax.numpy as jnp
from jax import lax
from jax.experimental import pallas as pl
from jax.experimental.pallas import tpu as pltpu
from jax.sharding import PartitionSpec as P

R = 48
N = 512
MODES = 8
RR = R * R
GROUPS = 4
WIDE = 8
ROWS = GROUPS * R
LANES = WIDE * R
FEATS = 104
SLOTS = 128
WAYS = 4
HIGH = lax.Precision.HIGHEST
F32 = jnp.float32
BF16 = jnp.bfloat16
COLS = 768
BIG = 14 << 20


def dot_rows(a, b):
    return lax.dot_general(a, b, (((0,), (0,)), ((), ())), preferred_element_type=F32)


def dot_lanes(a, b, precision=None):
    return lax.dot_general(
        a, b, (((1,), (1,)), ((), ())), preferred_element_type=F32, precision=precision
    )


def halves(x):
    hi = x.astype(BF16)
    return hi, (x - hi.astype(F32)).astype(BF16)


def iota(shape, dim):
    return lax.broadcasted_iota(jnp.int32, shape, dim)


def ranks(row, peers, slab):
    count = row.shape[1]
    chunks = count // 128
    dest = row // slab
    hit = (iota((peers, count), 0) == dest).astype(F32)
    stacked = jnp.concatenate([hit[:, c * 128 : (c + 1) * 128] for c in range(chunks)], axis=0)
    upper = (iota((128, 128), 0) <= iota((128, 128), 1)).astype(BF16)
    inside = jnp.dot(stacked.astype(BF16), upper, preferred_element_type=F32)
    before = jnp.zeros((peers, 1), F32)
    out = []
    for c in range(chunks):
        part = inside[c * peers : (c + 1) * peers]
        mine = hit[:, c * 128 : (c + 1) * 128]
        out.append(jnp.sum(mine * (part + before), axis=0, keepdims=True))
        before = before + part[:, 127:128]
    return jnp.concatenate(out, axis=1).astype(jnp.int32) - 1, dest


def half_of(row, second):
    half = row.shape[1] // 2
    flag = jnp.where(second, 1.0, 0.0)
    return jnp.where(flag > 0.5, row[:, half:], row[:, :half])


def gather_kernel(idx_ref, table_ref, *refs, peers):
    own = peers is not None
    mats_ref, *outs, hot_ref = refs if own else refs[1:]
    step = pl.program_id(0)
    mode = lax.axis_index("cores")

    @pl.when(step == 0)
    def _():
        which = mode if own else mode + 1 - 2 * (mode % 2)
        row = idx_ref[pl.ds(which, 1), :]
        half = half_of(row, mode % 2 == 1)
        hot_ref[...] = (iota(hot_ref.shape, 0) == half).astype(BF16)
        if own:
            slot_ref, most_ref = outs
            slab = N // peers
            place, dest = ranks(row, peers, slab)
            slot_ref[0:1, :] = place
            slot_ref[1:2, :] = dest
            slot_ref[2:3, :] = row - dest * slab
            slot_ref[3:8, :] = jnp.zeros((5, row.shape[1]), jnp.int32)
            every = idx_ref[...] // slab
            most = jnp.zeros((MODES, 1), F32)
            for j in range(peers):
                most = jnp.maximum(most, jnp.sum((every == j).astype(F32), axis=1, keepdims=True))
            most_ref[...] = jnp.broadcast_to(jnp.max(most, axis=0, keepdims=True), (8, 128))

    hot = hot_ref[...]
    hi, lo = halves(table_ref[...])
    mats_ref[...] = dot_rows(hi, hot) + dot_rows(lo, hot)


def times(left, mats_ref, base, vec_ref, out_ref):
    count = vec_ref.shape[1]

    def rows(a):
        return pl.ds(pl.multiple_of(base + a * R, 8), R)

    @pl.when(left)
    def _():
        def chunk(c, _):
            lanes = pl.ds(pl.multiple_of(c * 128, 128), 128)
            acc = [jnp.zeros((R, 128), F32) for _ in range(2)]
            for a in range(R):
                acc[a % 2] = acc[a % 2] + mats_ref[rows(a), lanes] * vec_ref[a : a + 1, lanes]
            out_ref[:, lanes] = acc[0] + acc[1]
            return 0

        lax.fori_loop(0, count // 128, chunk, 0)

    @pl.when(jnp.logical_not(left))
    def _():
        def chunk(c, _):
            lanes = pl.ds(pl.multiple_of(c * 128, 128), 128)
            vec = vec_ref[:, lanes]
            for a in range(0, R, 8):
                sums = [
                    jnp.sum(mats_ref[rows(a + i), lanes] * vec, axis=0, keepdims=True) for i in range(8)
                ]
                out_ref[a : a + 8, lanes] = jnp.concatenate(sums, axis=0)
            return 0

        lax.fori_loop(0, count // 128, chunk, 0)


def both_modes(turn, mats_ref, vec_ref, mid_ref, out_ref):
    mode = lax.axis_index("cores")
    chips = MODES // 2
    left = (mode // 2 < chips // 2) if turn < chips // 2 else (mode // 2 >= chips // 2)
    even = (mode % 2) * RR
    base = jnp.where(left, even, RR - even)
    times(left, mats_ref, base, vec_ref, mid_ref)
    times(left, mats_ref, RR - base, mid_ref, out_ref)


def unit_at_ends(shape_):
    chip = lax.axis_index("cores") // 2
    edge = jnp.where(jnp.logical_or(chip == 0, chip == MODES // 2 - 1), 1.0, 0.0)
    return jnp.where(iota(shape_, 0) == 0, edge, 0.0)


def hop_kernel(mats_ref, *refs, turn):
    vec_ref, mid_ref, out_ref = refs if turn else (refs[2], refs[0], refs[1])
    chip = lax.axis_index("cores") // 2
    live = jnp.logical_or(chip == turn, chip == MODES // 2 - 1 - turn)

    @pl.when(live)
    def _():
        if turn == 0:
            vec_ref[...] = unit_at_ends(vec_ref.shape)
        both_modes(turn, mats_ref, vec_ref, mid_ref, out_ref)

    @pl.when(jnp.logical_not(live))
    def _():
        mid_ref[...] = jnp.zeros(mid_ref.shape, F32)
        out_ref[...] = jnp.zeros(out_ref.shape, F32)


def finish_kernel(mats_ref, *refs):
    recv, mids = refs[0:3], refs[3:6]
    out2_ref, obs_ref, own_ref, other_ref, mid_ref, out_ref = refs[6:]
    mode = lax.axis_index("cores")
    both_modes(3, mats_ref, recv[2], mid_ref, out_ref)
    end1 = unit_at_ends(mid_ref.shape) + recv[0][...]
    mid1 = mids[0][...] + mids[1][...]
    end2 = recv[1][...] + recv[2][...]
    mid2 = mids[2][...] + mid_ref[...]
    predicted = jnp.sum((out2_ref[...] + out_ref[...]) * end1, axis=0, keepdims=True)
    residual = predicted - half_of(obs_ref[...], mode % 2 == 1)
    early = jnp.where(mode // 2 < MODES // 4, 1.0, 0.0) > 0.5
    even = (jnp.where(early, end1, end2), jnp.where(early, mid2, mid1) * residual)
    odd = (jnp.where(early, mid1, mid2), jnp.where(early, end2, end1) * residual)
    second = jnp.where(mode % 2 == 1, 1.0, 0.0) > 0.5
    for k in range(2):
        rows = slice(k * R, (k + 1) * R)
        own_ref[rows, :] = jnp.where(second, odd[k], even[k])
        other_ref[rows, :] = jnp.where(second, even[k], odd[k])


def keys(slot_ref, turn):
    place = slot_ref[0:1, :] - turn * SLOTS
    fits = jnp.logical_and(place >= 0, place < SLOTS)
    return jnp.where(fits, slot_ref[1:2, :] * SLOTS + place, -1)


def spread(values, key, pay_ref, so_far_ref=None):
    hi, lo = halves(values)
    both = jnp.concatenate([hi, lo], axis=0)
    for pair in range(pay_ref.shape[0] // 2):
        base = pair * 2 * SLOTS
        hot = (iota((2 * SLOTS, values.shape[1]), 0) + base == key).astype(BF16)
        out = dot_lanes(both, hot)
        out = out[:FEATS] + out[FEATS:]
        for k in range(2):
            part = out[:, k * SLOTS : (k + 1) * SLOTS]
            peer = 2 * pair + k
            pay_ref[peer] = part if so_far_ref is None else part + so_far_ref[peer]


def mark(most_ref, pay_ref):
    for peer in range(pay_ref.shape[0]):
        pay_ref[peer, 97:98, :] = most_ref[0:1, :]


def with_place(vecs, loc):
    pad = jnp.zeros((FEATS - 97, vecs.shape[1]), F32)
    return jnp.concatenate([vecs, loc.astype(F32), pad], axis=0)


def route_own_kernel(vecs_ref, slot_ref, pay_ref):
    second = lax.axis_index("cores") % 2 == 1
    values = with_place(vecs_ref[...], half_of(slot_ref[2:3, :], second))
    spread(values, half_of(keys(slot_ref, 0), second), pay_ref)


def route_kernel(own_ref, got_ref, slot_ref, most_ref, part_ref, pay_ref, val_ref):
    first = lax.axis_index("cores") % 2 == 0
    own = own_ref[...]
    got = got_ref[...]
    values = with_place(got, half_of(slot_ref[2:3, :], first))
    spread(values, half_of(keys(slot_ref, 0), first), pay_ref, part_ref)
    mark(most_ref, pay_ref)
    flag = jnp.where(first, 1.0, 0.0) > 0.5
    vecs = jnp.concatenate([jnp.where(flag, own, got), jnp.where(flag, got, own)], axis=1)
    val_ref[...] = with_place(vecs, slot_ref[2:3, :])


def again_kernel(turn_ref, val_ref, slot_ref, most_ref, pay_ref):
    spread(val_ref[...], keys(slot_ref, turn_ref[0]), pay_ref)
    mark(most_ref, pay_ref)


def collect_kernel(step_ref, recv_ref, base_ref, out_ref, turns_ref):
    peers = recv_ref.shape[0]
    left = jnp.concatenate([recv_ref[s, 0:R, :] for s in range(peers)], axis=1)
    right = jnp.concatenate([recv_ref[s, R : 2 * R, :] for s in range(peers)], axis=1)
    loc = jnp.concatenate([recv_ref[s, 96:97, :] for s in range(peers)], axis=1).astype(jnp.int32)
    row_of = loc // WIDE
    lane_of = loc - row_of * WIDE
    count = loc.shape[1]

    def picked(x, key, n):
        hi = x.astype(BF16).astype(F32)
        lo = x - hi
        his, los = [], []
        for i in range(n):
            here = key == i
            his += [jnp.where(here, hi, 0.0).astype(BF16)]
            los += [jnp.where(here, lo, 0.0).astype(BF16)]
        return jnp.concatenate(his, axis=0), jnp.concatenate(los, axis=0)

    xh, xl = picked(left, row_of, GROUPS)
    yh, yl = picked(right, lane_of, WIDE)
    grad = dot_lanes(xh, yh) + (dot_lanes(xh, yl) + dot_lanes(xl, yh))
    out_ref[...] = base_ref[...] - step_ref[0] * grad
    most = jnp.max(recv_ref[:, 97, :]).astype(jnp.int32)
    turns_ref[0] = (most + SLOTS - 1) // SLOTS


def arrange(refs):
    own = refs[:WAYS]
    other = refs[WAYS : 2 * WAYS]
    outs = refs[2 * WAYS :]
    even_first = jnp.where(lax.axis_index("cores") % 2 == 0, 1.0, 0.0)
    for w in range(WAYS):
        mine = own[w][...]
        theirs = other[w][...]
        for k in range(2):
            stack_ref, turned_ref = outs[2 * k : 2 * k + 2]
            flag = even_first if k == 0 else 1.0 - even_first
            core = jnp.where(flag > 0.5, mine, theirs)
            hi, lo = halves(core)
            for g in range(GROUPS):
                at = 3 * (w * GROUPS + g) * R
                here = slice(g * R, (g + 1) * R)
                stack_ref[at : at + R, :] = hi[here]
                stack_ref[at + R : at + 2 * R, :] = hi[here]
                stack_ref[at + 2 * R : at + 3 * R, :] = lo[here]
            hi, lo = halves(core.T)
            for k3, piece in enumerate((hi, hi, lo)):
                turned_ref[:, (k3 * WAYS + w) * ROWS : (k3 * WAYS + w + 1) * ROWS] = piece


def stacked(square):
    wide = jnp.concatenate([square, jnp.zeros((R, 128), F32)], axis=1)
    hi = wide.astype(BF16).astype(F32)
    lo = wide - hi
    return (hi + (pltpu.roll(lo, R, 1) + pltpu.roll(hi, 2 * R, 1)))[:, : 3 * R].astype(BF16)


def packed_of(full):
    lane = iota((24, 128), 1)
    return jnp.where(lane < 64, full[0:24], pltpu.roll(full[24:48], 64, 1))


def whole(packed):
    both = jnp.concatenate([packed, pltpu.roll(packed, 64, 1)], axis=0)
    return jnp.where(iota((R, 128), 1) < R, both, 0.0)


def pulled(before, core, prod_ref):
    stack, turned = core
    all_rows = WAYS * ROWS
    weights = None if before is None else stacked(before)
    for g in range(WAYS * GROUPS):
        at = 3 * g * R
        if before is None:
            hi, lo = stack[at : at + R, :], stack[at + 2 * R : at + 3 * R, :]
        else:
            hi, lo = halves(
                jnp.dot(weights, stack[at : at + 3 * R, :], preferred_element_type=F32)
            )
        for k3, piece in enumerate((hi, lo, hi)):
            prod_ref[k3 * all_rows + g * R : k3 * all_rows + (g + 1) * R, :] = piece
    total = jnp.zeros((R, 256), F32)
    for part, slices in ((0, range(5)), (128, range(5, WIDE))):
        cols = slice(part, part + 256)
        z = jnp.dot(turned[cols, :], prod_ref[:, cols], preferred_element_type=F32)
        for h in slices:
            at = h * R - part
            block = z[at : at + R]
            total = total + (pltpu.roll(block, 256 - at, 1) if at else block)
    return jnp.where(iota((R, 128), 1) < R, total[:, :128], 0.0) * (1.0 / N)


def pair_kernel(*refs, pair):
    last = pair == MODES // 2 - 1
    refs = list(refs)
    recv_ref = refs.pop(0) if pair else None
    saved = [refs.pop(0) for _ in range(pair)] if last else []
    prod_ref = refs.pop()
    if pair:
        even = [refs.pop(0) for _ in range(2)]
        odd = None if last else [refs.pop(0) for _ in range(2)]
        sum_ref = refs.pop()
        sum_ref[...] = jnp.sum(recv_ref[0 : recv_ref.shape[0] // 2], axis=0)
    else:
        cores = refs[2 * WAYS : 2 * WAYS + 4]
        arrange(refs[: 2 * WAYS + 4])
        even, odd = cores[:2], cores[2:]
        refs = refs[2 * WAYS + 4 :]
    kept_ref = refs.pop()
    live = lax.axis_index("cores") // 2 == pair

    @pl.when(live)
    def _():
        middle = pulled(whole(sum_ref[...]) if pair else None, even, prod_ref)
        kept_ref[...] = packed_of(middle)
        if not last:
            packed = packed_of(pulled(middle, odd, prod_ref))
            for peer in range(refs[0].shape[0]):
                refs[0][peer] = packed

    @pl.when(jnp.logical_not(live))
    def _():
        kept = jnp.zeros((24, 128), F32)
        for s in saved:
            kept = kept + s[...]
        kept_ref[...] = kept
        if not last:
            refs[0][...] = jnp.zeros(refs[0].shape, F32)


def factored(packed, absent):
    row = iota((R, 128), 0)
    lane = iota((R, 128), 1)
    eye = jnp.where(lane == row, 1.0, 0.0)
    full = whole(packed) + eye * absent + jnp.where(lane == row + 64, 1.0, 0.0)
    m = [full[8 * t : 8 * t + 8] for t in range(R // 8)]
    for begin in range(0, R, 4):
        top = begin // 8
        below = range(top, R // 8)
        col = [
            {t: jnp.broadcast_to(m[t][:, begin + k : begin + k + 1], (8, 128)) for t in below} for k in range(4)
        ]
        for k in range(4):
            at = begin + k - 8 * top
            scale = 1.0 / col[k][top][at : at + 1]
            fact = {t: col[k][t] * scale for t in below}
            fact[top] = jnp.where(iota((8, 128), 0) > at, fact[top], 0.0)
            pivot = m[top][at : at + 1]
            for q in range(k + 1, 4):
                lead = col[q][top][at : at + 1]
                for t in below:
                    col[q][t] = col[q][t] - fact[t] * lead
            for t in below:
                m[t] = m[t] - fact[t] * pivot
    m = jnp.concatenate(m, axis=0)
    diag = jnp.sum(jnp.where(lane == row, m, 0.0), axis=1, keepdims=True)
    return m * (1.0 / jnp.sqrt(diag))


def from_left(tri, in_ref, out_ref):
    for g in range(GROUPS):
        rows = slice(g * R, (g + 1) * R)
        out_ref[rows, :] = jnp.dot(
            tri[:, :R], in_ref[rows, :], preferred_element_type=F32, precision=HIGH
        )


def from_right(tri, in_ref, out_ref, block_ref):
    inv = jnp.where(iota((R, 128), 1) < R, pltpu.roll(tri, 64, 1), 0.0)
    wide = jnp.concatenate([inv, jnp.zeros((R, LANES - 128), F32)], axis=1)
    for h in range(WIDE):
        block_ref[h * R : (h + 1) * R, :] = pltpu.roll(wide, h * R, 1) if h else wide
    out_ref[...] = dot_lanes(in_ref[...], block_ref[...], HIGH)


def applied(tri, left, in_ref, out_ref, block_ref):
    @pl.when(left)
    def _():
        from_left(tri, in_ref, out_ref)

    @pl.when(jnp.logical_not(left))
    def _():
        from_right(tri, in_ref, out_ref, block_ref)


def known_kernel(*refs):
    *sums, core_ref, out_ref, block_ref = refs
    mode = lax.axis_index("cores")
    chip = mode // 2
    first = jnp.where(mode % 2 == 0, 1.0, 0.0)
    known = jnp.zeros((24, 128), F32)
    for p, s in enumerate(sums):
        known = known + s[...] * jnp.where(chip == p, 1.0 - first, 0.0)
        known = known + s[...] * jnp.where(chip == p + 1, first, 0.0)
    absent = jnp.where(jnp.logical_or(mode == 0, mode == MODES - 1), 1.0, 0.0)
    applied(factored(known, absent), mode % 2 == 0, core_ref, out_ref, block_ref)


def final_kernel(a_ref, b_ref, c_ref, d_ref, core_ref, out_ref, block_ref):
    level = (a_ref[...] + b_ref[...]) + (c_ref[...] + d_ref[...])
    odd = lax.axis_index("cores") % 2 == 1
    applied(factored(level, 0.0), odd, core_ref, out_ref, block_ref)


def vmem():
    return pl.BlockSpec(memory_space=pltpu.VMEM)


def smem():
    return pl.BlockSpec(memory_space=pltpu.SMEM)


def call(kernel, outs, ins, scratch=(), name=None):
    return pl.pallas_call(
        kernel,
        out_shape=outs,
        in_specs=ins,
        out_specs=jax.tree.map(lambda o: smem() if o.dtype == jnp.int32 and o.size == 1 else vmem(), outs),
        scratch_shapes=list(scratch),
        compiler_params=pltpu.CompilerParams(vmem_limit_bytes=BIG),
        name=name,
    )


def shape(*dims, dtype=F32):
    return jax.ShapeDtypeStruct(dims, dtype)


def on_device(cores, indices, observed, step_size):
    peers = lax.axis_size("samp")
    count = indices.shape[0]
    slab = N // peers
    table = cores[0]
    idx = indices.T
    step = step_size.reshape(1)

    half = count // 2
    siblings = [(m, m ^ 1) for m in range(MODES)]
    other_table = lax.ppermute(table, "cores", siblings)
    steps = RR // COLS
    params = pltpu.CompilerParams(vmem_limit_bytes=BIG)
    in_specs = [
        pl.BlockSpec((MODES, count), lambda i: (0, 0)),
        pl.BlockSpec((N, COLS), lambda i: (0, i)),
    ]
    hot = [pltpu.VMEM((N, half), BF16)]
    idx, table_in = [pltpu.with_memory_space_constraint(a, pltpu.HBM) for a in (idx, table)]
    mats, slot, most = pl.pallas_call(
        functools.partial(gather_kernel, peers=peers),
        grid=(steps,),
        in_specs=in_specs,
        out_specs=[
            pl.BlockSpec((COLS, half), lambda i: (i, 0)),
            pl.BlockSpec((8, count), lambda i: (0, 0)),
            pl.BlockSpec((8, 128), lambda i: (0, 0)),
        ],
        out_shape=[shape(2 * RR, half), shape(8, count, dtype=jnp.int32), shape(8, 128)],
        scratch_shapes=hot,
        compiler_params=params,
        name="gather",
    )(idx, table_in)
    mats = pl.pallas_call(
        functools.partial(gather_kernel, peers=None),
        grid=(steps,),
        in_specs=in_specs + [pl.BlockSpec(memory_space=pl.ANY)],
        out_specs=pl.BlockSpec((COLS, half), lambda i: (i + steps, 0)),
        out_shape=shape(2 * RR, half),
        scratch_shapes=hot,
        input_output_aliases={2: 0},
        compiler_params=params,
        name="gather_other",
    )(idx, other_table, mats)

    first = lax.axis_index("samp") * slab
    kept = lax.dynamic_slice_in_dim(table, first, slab, 0)
    base = kept.reshape(GROUPS, WIDE, R, R).transpose(0, 2, 1, 3)
    base = base.reshape(ROWS, LANES)

    vec = shape(R, half)
    recv, mids = [], []
    for turn in range(3):
        mid, out = call(
            functools.partial(hop_kernel, turn=turn),
            [vec, vec],
            [vmem()] * (2 if turn else 1),
            [] if turn else [pltpu.VMEM((R, half), F32)],
            name=f"hop{turn}",
        )(mats, *recv[-1:])
        pairs = [(2 * a + h, 2 * b + h) for a, b in ((turn, turn + 1), (3 - turn, 2 - turn)) for h in range(2)]
        recv.append(lax.ppermute(out, "cores", pairs))
        mids.append(mid)
    own_vecs, other_vecs = call(
        finish_kernel,
        [shape(2 * R, half)] * 2,
        [vmem()] * 9,
        [pltpu.VMEM((R, half), F32)] * 2,
        name="finish",
    )(mats, *recv, *mids, out, observed.reshape(1, count))
    got_vecs = lax.ppermute(other_vecs, "cores", siblings)
    part = call(route_own_kernel, shape(peers, FEATS, SLOTS), [vmem()] * 2, name="route_own")(own_vecs, slot)
    pay, values = call(
        route_kernel,
        (shape(peers, FEATS, SLOTS), shape(FEATS, count)),
        [vmem()] * 5,
        name="route",
    )(own_vecs, got_vecs, slot, most, part)

    def exchanged(block):
        return lax.all_to_all(block, "samp", 0, 0, tiled=True)

    def collected(recv, so_far):
        return call(
            collect_kernel,
            (shape(ROWS, LANES), shape(1, dtype=jnp.int32)),
            [smem(), vmem(), vmem()],
            name="collect",
        )(step, recv, so_far)

    updated, turns = collected(exchanged(pay), base)

    def more(state):
        return state[0] < turns[0]

    def another(state):
        turn, so_far = state
        pay = call(
            again_kernel,
            shape(peers, FEATS, SLOTS),
            [smem(), vmem(), vmem(), vmem()],
            name="again",
        )(turn.reshape(1), values, slot, most)
        return turn + 1, collected(exchanged(pay), so_far)[0]

    _, updated = lax.while_loop(more, another, (jnp.int32(1), updated))

    side = int(peers**0.5)

    def partner(mode, peer, by):
        z, x = peer // side, peer % side
        return (z + by) % side * side + x if mode % 2 else z * side + (x + by) % side

    ring = [
        [(m * peers + p, m * peers + partner(m, p, w)) for m in range(MODES) for p in range(peers)]
        for w in range(1, WAYS)
    ]
    level = [[(p, partner(1, p, w)) for p in range(peers)] for w in range(1, WAYS)]
    own = [updated] + [lax.ppermute(updated, ("cores", "samp"), pairs) for pairs in ring]
    other = [lax.ppermute(o, "cores", siblings) for o in own]
    stack = shape(3 * WAYS * ROWS, LANES, dtype=BF16)
    flat = shape(LANES, 3 * WAYS * ROWS, dtype=BF16)

    saved, sums = [], []
    recv = None
    for pair in range(MODES // 2):
        last = pair == MODES // 2 - 1
        outs = [shape(24, 128)] if last else [shape(2 * peers, 24, 128), shape(24, 128)]
        if pair:
            ins = [recv] + (saved + even if last else even + odd)
            outs.append(shape(24, 128))
        else:
            ins = own + other
            outs = [stack, flat] * 2 + outs
        res = call(
            functools.partial(pair_kernel, pair=pair),
            outs,
            [vmem()] * len(ins),
            [pltpu.VMEM((3 * WAYS * ROWS, LANES), BF16)],
            name=f"pair{pair}",
        )(*ins)
        if pair:
            sums.append(res[-1])
        else:
            even, odd, res = list(res[:2]), list(res[2:4]), res[4:]
        if last:
            parts = [res[0]] + [lax.ppermute(res[0], "samp", pairs) for pairs in level]
        else:
            saved.append(res[1])
            groups = []
            for c in (pair, pair + 2):
                for h in range(2):
                    both = [2 * (c % 4) + h, 2 * ((c + 1) % 4) + h]
                    groups.append([m * peers + j for m in both for j in range(peers)])
            recv = lax.all_to_all(
                res[0], ("cores", "samp"), 0, 0, axis_index_groups=groups, tiled=True
            )

    block = [pltpu.VMEM((LANES, LANES), F32)]
    ahead = call(known_kernel, shape(ROWS, LANES), [vmem()] * (MODES // 2), block, name="known")(*sums, updated)
    out = call(final_kernel, shape(ROWS, LANES), [vmem()] * (WAYS + 1), block, name="final")(*parts, ahead)
    out = out.reshape(GROUPS, R, WIDE, R).transpose(0, 2, 1, 3)
    return out.reshape(1, slab, RR)


def solution(mesh):
    in_specs = (P("cores", None, None), P("samp", None), P("samp"), P())
    out_specs = P("cores", "samp", None)
    return jax.shard_map(
        on_device, mesh=mesh, in_specs=in_specs, out_specs=out_specs, check_vma=False
    )
```

```python
import functools

import jax
import jax.numpy as jnp
from jax import lax
from jax.experimental import pallas as pl
from jax.experimental.pallas import tpu as pltpu
from jax.sharding import PartitionSpec as P

R = 48
N = 512
MODES = 8
RR = R * R
GROUPS = 4
WIDE = 8
ROWS = GROUPS * R
LANES = WIDE * R
FEATS = 104
SLOTS = 128
WAYS = 4
HIGH = lax.Precision.HIGHEST
F32 = jnp.float32
BF16 = jnp.bfloat16
COLS = 768
BIG = 14 << 20


def dot_rows(a, b):
    return lax.dot_general(a, b, (((0,), (0,)), ((), ())), preferred_element_type=F32)


def dot_lanes(a, b, precision=None):
    return lax.dot_general(
        a, b, (((1,), (1,)), ((), ())), preferred_element_type=F32, precision=precision
    )


def halves(x):
    hi = x.astype(BF16)
    return hi, (x - hi.astype(F32)).astype(BF16)


def iota(shape, dim):
    return lax.broadcasted_iota(jnp.int32, shape, dim)


def ranks(row, peers, slab):
    count = row.shape[1]
    chunks = count // 128
    dest = row // slab
    hit = (iota((peers, count), 0) == dest).astype(F32)
    stacked = jnp.concatenate([hit[:, c * 128 : (c + 1) * 128] for c in range(chunks)], axis=0)
    upper = (iota((128, 128), 0) <= iota((128, 128), 1)).astype(BF16)
    inside = jnp.dot(stacked.astype(BF16), upper, preferred_element_type=F32)
    before = jnp.zeros((peers, 1), F32)
    out = []
    for c in range(chunks):
        part = inside[c * peers : (c + 1) * peers]
        mine = hit[:, c * 128 : (c + 1) * 128]
        out.append(jnp.sum(mine * (part + before), axis=0, keepdims=True))
        before = before + part[:, 127:128]
    return jnp.concatenate(out, axis=1).astype(jnp.int32) - 1, dest


def half_of(row, second):
    half = row.shape[1] // 2
    flag = jnp.where(second, 1.0, 0.0)
    return jnp.where(flag > 0.5, row[:, half:], row[:, :half])


def one_hot(row, second, hot_ref):
    hot_ref[...] = (iota(hot_ref.shape, 0) == half_of(row, second)).astype(BF16)


def gathered(table, hot):
    hi, lo = halves(table)
    return dot_rows(hi, hot) + dot_rows(lo, hot)


def gather_kernel(idx_ref, table_ref, mats_ref, slot_ref, most_ref, hot_ref, *, peers):
    step = pl.program_id(0)
    mode = lax.axis_index("cores")

    @pl.when(step == 0)
    def _():
        row = idx_ref[pl.ds(mode, 1), :]
        one_hot(row, mode % 2 == 1, hot_ref)
        slab = N // peers
        place, dest = ranks(row, peers, slab)
        slot_ref[0:1, :] = place
        slot_ref[1:2, :] = dest
        slot_ref[2:3, :] = row - dest * slab
        slot_ref[3:8, :] = jnp.zeros((5, row.shape[1]), jnp.int32)
        every = idx_ref[...] // slab
        most = jnp.zeros((MODES, 1), F32)
        for j in range(peers):
            most = jnp.maximum(most, jnp.sum((every == j).astype(F32), axis=1, keepdims=True))
        most_ref[...] = jnp.broadcast_to(jnp.max(most, axis=0, keepdims=True), (8, 128))

    rows = pl.ds(pl.multiple_of(step * COLS, COLS), COLS)
    mats_ref[rows, :] = gathered(table_ref[...], hot_ref[...])


def gather_other_kernel(idx_ref, table_ref, _, mats_ref, hot_ref):
    mode = lax.axis_index("cores")
    second = mode % 2
    one_hot(idx_ref[pl.ds(mode + 1 - 2 * second, 1), :], second == 1, hot_ref)
    for at in range(0, RR, COLS):
        mats_ref[RR + at : RR + at + COLS, :] = gathered(table_ref[:, at : at + COLS], hot_ref[...])


def times(left, mats_ref, base, vec_ref, out_ref):
    count = vec_ref.shape[1]

    def rows(a):
        return pl.ds(pl.multiple_of(base + a * R, 8), R)

    @pl.when(left)
    def _():
        def chunk(c, _):
            lanes = pl.ds(pl.multiple_of(c * 128, 128), 128)
            acc = [jnp.zeros((R, 128), F32) for _ in range(2)]
            for a in range(R):
                acc[a % 2] = acc[a % 2] + mats_ref[rows(a), lanes] * vec_ref[a : a + 1, lanes]
            out_ref[:, lanes] = acc[0] + acc[1]
            return 0

        lax.fori_loop(0, count // 128, chunk, 0)

    @pl.when(jnp.logical_not(left))
    def _():
        def chunk(c, _):
            lanes = pl.ds(pl.multiple_of(c * 128, 128), 128)
            vec = vec_ref[:, lanes]
            for a in range(0, R, 8):
                sums = [
                    jnp.sum(mats_ref[rows(a + i), lanes] * vec, axis=0, keepdims=True) for i in range(8)
                ]
                out_ref[a : a + 8, lanes] = jnp.concatenate(sums, axis=0)
            return 0

        lax.fori_loop(0, count // 128, chunk, 0)


def both_modes(turn, mats_ref, vec_ref, mid_ref, out_ref):
    mode = lax.axis_index("cores")
    chips = MODES // 2
    left = (mode // 2 < chips // 2) if turn < chips // 2 else (mode // 2 >= chips // 2)
    even = (mode % 2) * RR
    base = jnp.where(left, even, RR - even)
    times(left, mats_ref, base, vec_ref, mid_ref)
    times(left, mats_ref, RR - base, mid_ref, out_ref)


def unit_at_ends(shape_):
    chip = lax.axis_index("cores") // 2
    edge = jnp.where(jnp.logical_or(chip == 0, chip == MODES // 2 - 1), 1.0, 0.0)
    return jnp.where(iota(shape_, 0) == 0, edge, 0.0)


def hop_kernel(mats_ref, *refs, turn):
    vec_ref, mid_ref, out_ref = refs if turn else (refs[2], refs[0], refs[1])
    chip = lax.axis_index("cores") // 2
    live = jnp.logical_or(chip == turn, chip == MODES // 2 - 1 - turn)

    @pl.when(live)
    def _():
        if turn == 0:
            vec_ref[...] = unit_at_ends(vec_ref.shape)
        both_modes(turn, mats_ref, vec_ref, mid_ref, out_ref)

    @pl.when(jnp.logical_not(live))
    def _():
        mid_ref[...] = jnp.zeros(mid_ref.shape, F32)
        out_ref[...] = jnp.zeros(out_ref.shape, F32)


def finish_kernel(mats_ref, *refs):
    recv, mids = refs[0:3], refs[3:6]
    out2_ref, obs_ref, own_ref, other_ref, mid_ref, out_ref = refs[6:]
    mode = lax.axis_index("cores")
    both_modes(3, mats_ref, recv[2], mid_ref, out_ref)
    end1 = unit_at_ends(mid_ref.shape) + recv[0][...]
    mid1 = mids[0][...] + mids[1][...]
    end2 = recv[1][...] + recv[2][...]
    mid2 = mids[2][...] + mid_ref[...]
    predicted = jnp.sum((out2_ref[...] + out_ref[...]) * end1, axis=0, keepdims=True)
    residual = predicted - half_of(obs_ref[...], mode % 2 == 1)
    early = jnp.where(mode // 2 < MODES // 4, 1.0, 0.0) > 0.5
    even = (jnp.where(early, end1, end2), jnp.where(early, mid2, mid1) * residual)
    odd = (jnp.where(early, mid1, mid2), jnp.where(early, end2, end1) * residual)
    second = jnp.where(mode % 2 == 1, 1.0, 0.0) > 0.5
    for k in range(2):
        rows = slice(k * R, (k + 1) * R)
        own_ref[rows, :] = jnp.where(second, odd[k], even[k])
        other_ref[rows, :] = jnp.where(second, even[k], odd[k])


def keys(slot_ref, turn):
    place = slot_ref[0:1, :] - turn * SLOTS
    fits = jnp.logical_and(place >= 0, place < SLOTS)
    return jnp.where(fits, slot_ref[1:2, :] * SLOTS + place, -1)


def spread(values, key, pay_ref, so_far_ref=None):
    hi, lo = halves(values)
    both = jnp.concatenate([hi, lo], axis=0)
    for pair in range(pay_ref.shape[0] // 2):
        base = pair * 2 * SLOTS
        hot = (iota((2 * SLOTS, values.shape[1]), 0) + base == key).astype(BF16)
        out = dot_lanes(both, hot)
        out = out[:FEATS] + out[FEATS:]
        for k in range(2):
            part = out[:, k * SLOTS : (k + 1) * SLOTS]
            peer = 2 * pair + k
            pay_ref[peer] = part if so_far_ref is None else part + so_far_ref[peer]


def mark(most_ref, pay_ref):
    for peer in range(pay_ref.shape[0]):
        pay_ref[peer, 97:98, :] = most_ref[0:1, :]


def with_place(vecs, loc):
    pad = jnp.zeros((FEATS - 97, vecs.shape[1]), F32)
    return jnp.concatenate([vecs, loc.astype(F32), pad], axis=0)


def route_own_kernel(vecs_ref, slot_ref, pay_ref):
    second = lax.axis_index("cores") % 2 == 1
    values = with_place(vecs_ref[...], half_of(slot_ref[2:3, :], second))
    spread(values, half_of(keys(slot_ref, 0), second), pay_ref)


def route_kernel(own_ref, got_ref, slot_ref, most_ref, part_ref, pay_ref, val_ref):
    first = lax.axis_index("cores") % 2 == 0
    own = own_ref[...]
    got = got_ref[...]
    values = with_place(got, half_of(slot_ref[2:3, :], first))
    spread(values, half_of(keys(slot_ref, 0), first), pay_ref, part_ref)
    mark(most_ref, pay_ref)
    flag = jnp.where(first, 1.0, 0.0) > 0.5
    vecs = jnp.concatenate([jnp.where(flag, own, got), jnp.where(flag, got, own)], axis=1)
    val_ref[...] = with_place(vecs, slot_ref[2:3, :])


def again_kernel(turn_ref, val_ref, slot_ref, most_ref, pay_ref):
    spread(val_ref[...], keys(slot_ref, turn_ref[0]), pay_ref)
    mark(most_ref, pay_ref)


def collect_kernel(step_ref, recv_ref, base_ref, out_ref, turns_ref):
    peers = recv_ref.shape[0]
    left = jnp.concatenate([recv_ref[s, 0:R, :] for s in range(peers)], axis=1)
    right = jnp.concatenate([recv_ref[s, R : 2 * R, :] for s in range(peers)], axis=1)
    loc = jnp.concatenate([recv_ref[s, 96:97, :] for s in range(peers)], axis=1).astype(jnp.int32)
    row_of = loc // WIDE
    lane_of = loc - row_of * WIDE
    count = loc.shape[1]

    def picked(x, key, n):
        hi = x.astype(BF16).astype(F32)
        lo = x - hi
        his, los = [], []
        for i in range(n):
            here = key == i
            his += [jnp.where(here, hi, 0.0).astype(BF16)]
            los += [jnp.where(here, lo, 0.0).astype(BF16)]
        return jnp.concatenate(his, axis=0), jnp.concatenate(los, axis=0)

    xh, xl = picked(left, row_of, GROUPS)
    yh, yl = picked(right, lane_of, WIDE)
    grad = dot_lanes(xh, yh) + (dot_lanes(xh, yl) + dot_lanes(xl, yh))
    out_ref[...] = base_ref[...] - step_ref[0] * grad
    most = jnp.max(recv_ref[:, 97, :]).astype(jnp.int32)
    turns_ref[0] = (most + SLOTS - 1) // SLOTS


def arrange(refs):
    own = refs[:WAYS]
    other = refs[WAYS : 2 * WAYS]
    outs = refs[2 * WAYS :]
    even_first = jnp.where(lax.axis_index("cores") % 2 == 0, 1.0, 0.0)
    for w in range(WAYS):
        mine = own[w][...]
        theirs = other[w][...]
        for k in range(2):
            stack_ref, turned_ref = outs[2 * k : 2 * k + 2]
            flag = even_first if k == 0 else 1.0 - even_first
            core = jnp.where(flag > 0.5, mine, theirs)
            hi, lo = halves(core)
            for g in range(GROUPS):
                at = 3 * (w * GROUPS + g) * R
                here = slice(g * R, (g + 1) * R)
                stack_ref[at : at + R, :] = hi[here]
                stack_ref[at + R : at + 2 * R, :] = hi[here]
                stack_ref[at + 2 * R : at + 3 * R, :] = lo[here]
            hi, lo = halves(core.T)
            for k3, piece in enumerate((hi, hi, lo)):
                turned_ref[:, (k3 * WAYS + w) * ROWS : (k3 * WAYS + w + 1) * ROWS] = piece


def stacked(square):
    wide = jnp.concatenate([square, jnp.zeros((R, 128), F32)], axis=1)
    hi = wide.astype(BF16).astype(F32)
    lo = wide - hi
    return (hi + (pltpu.roll(lo, R, 1) + pltpu.roll(hi, 2 * R, 1)))[:, : 3 * R].astype(BF16)


def packed_of(full):
    lane = iota((24, 128), 1)
    return jnp.where(lane < 64, full[0:24], pltpu.roll(full[24:48], 64, 1))


def whole(packed):
    both = jnp.concatenate([packed, pltpu.roll(packed, 64, 1)], axis=0)
    return jnp.where(iota((R, 128), 1) < R, both, 0.0)


def pulled(before, core, prod_ref):
    stack, turned = core
    all_rows = WAYS * ROWS
    weights = None if before is None else stacked(before)
    for g in range(WAYS * GROUPS):
        at = 3 * g * R
        if before is None:
            hi, lo = stack[at : at + R, :], stack[at + 2 * R : at + 3 * R, :]
        else:
            hi, lo = halves(
                jnp.dot(weights, stack[at : at + 3 * R, :], preferred_element_type=F32)
            )
        for k3, piece in enumerate((hi, lo, hi)):
            prod_ref[k3 * all_rows + g * R : k3 * all_rows + (g + 1) * R, :] = piece
    total = jnp.zeros((R, 256), F32)
    for part, slices in ((0, range(5)), (128, range(5, WIDE))):
        cols = slice(part, part + 256)
        z = jnp.dot(turned[cols, :], prod_ref[:, cols], preferred_element_type=F32)
        for h in slices:
            at = h * R - part
            block = z[at : at + R]
            total = total + (pltpu.roll(block, 256 - at, 1) if at else block)
    return jnp.where(iota((R, 128), 1) < R, total[:, :128], 0.0) * (1.0 / N)


def pair_kernel(*refs, pair):
    last = pair == MODES // 2 - 1
    refs = list(refs)
    recv_ref = refs.pop(0) if pair else None
    saved = [refs.pop(0) for _ in range(pair)] if last else []
    prod_ref = refs.pop()
    if pair:
        even = [refs.pop(0) for _ in range(2)]
        odd = None if last else [refs.pop(0) for _ in range(2)]
        sum_ref = refs.pop()
        sum_ref[...] = jnp.sum(recv_ref[0 : recv_ref.shape[0] // 2], axis=0)
    else:
        cores = refs[2 * WAYS : 2 * WAYS + 4]
        arrange(refs[: 2 * WAYS + 4])
        even, odd = cores[:2], cores[2:]
        refs = refs[2 * WAYS + 4 :]
    kept_ref = refs.pop()
    live = lax.axis_index("cores") // 2 == pair

    @pl.when(live)
    def _():
        middle = pulled(whole(sum_ref[...]) if pair else None, even, prod_ref)
        kept_ref[...] = packed_of(middle)
        if not last:
            packed = packed_of(pulled(middle, odd, prod_ref))
            for peer in range(refs[0].shape[0]):
                refs[0][peer] = packed

    @pl.when(jnp.logical_not(live))
    def _():
        kept = jnp.zeros((24, 128), F32)
        for s in saved:
            kept = kept + s[...]
        kept_ref[...] = kept
        if not last:
            refs[0][...] = jnp.zeros(refs[0].shape, F32)


def factored(packed, absent):
    row = iota((R, 128), 0)
    lane = iota((R, 128), 1)
    eye = jnp.where(lane == row, 1.0, 0.0)
    full = whole(packed) + eye * absent + jnp.where(lane == row + 64, 1.0, 0.0)
    m = [full[8 * t : 8 * t + 8] for t in range(R // 8)]
    for begin in range(0, R, 4):
        top = begin // 8
        below = range(top, R // 8)
        col = [
            {t: jnp.broadcast_to(m[t][:, begin + k : begin + k + 1], (8, 128)) for t in below} for k in range(4)
        ]
        for k in range(4):
            at = begin + k - 8 * top
            scale = 1.0 / col[k][top][at : at + 1]
            fact = {t: col[k][t] * scale for t in below}
            fact[top] = jnp.where(iota((8, 128), 0) > at, fact[top], 0.0)
            pivot = m[top][at : at + 1]
            for q in range(k + 1, 4):
                lead = col[q][top][at : at + 1]
                for t in below:
                    col[q][t] = col[q][t] - fact[t] * lead
            for t in below:
                m[t] = m[t] - fact[t] * pivot
    m = jnp.concatenate(m, axis=0)
    diag = jnp.sum(jnp.where(lane == row, m, 0.0), axis=1, keepdims=True)
    return m * (1.0 / jnp.sqrt(diag))


def from_left(tri, in_ref, out_ref):
    for g in range(GROUPS):
        rows = slice(g * R, (g + 1) * R)
        out_ref[rows, :] = jnp.dot(
            tri[:, :R], in_ref[rows, :], preferred_element_type=F32, precision=HIGH
        )


def from_right(tri, in_ref, out_ref, block_ref):
    inv = jnp.where(iota((R, 128), 1) < R, pltpu.roll(tri, 64, 1), 0.0)
    wide = jnp.concatenate([inv, jnp.zeros((R, LANES - 128), F32)], axis=1)
    for h in range(WIDE):
        block_ref[h * R : (h + 1) * R, :] = pltpu.roll(wide, h * R, 1) if h else wide
    out_ref[...] = dot_lanes(in_ref[...], block_ref[...], HIGH)


def applied(tri, left, in_ref, out_ref, block_ref):
    @pl.when(left)
    def _():
        from_left(tri, in_ref, out_ref)

    @pl.when(jnp.logical_not(left))
    def _():
        from_right(tri, in_ref, out_ref, block_ref)


def known_kernel(*refs):
    *sums, core_ref, out_ref, block_ref = refs
    mode = lax.axis_index("cores")
    chip = mode // 2
    first = jnp.where(mode % 2 == 0, 1.0, 0.0)
    known = jnp.zeros((24, 128), F32)
    for p, s in enumerate(sums):
        known = known + s[...] * jnp.where(chip == p, 1.0 - first, 0.0)
        known = known + s[...] * jnp.where(chip == p + 1, first, 0.0)
    absent = jnp.where(jnp.logical_or(mode == 0, mode == MODES - 1), 1.0, 0.0)
    applied(factored(known, absent), mode % 2 == 0, core_ref, out_ref, block_ref)


def final_kernel(a_ref, b_ref, c_ref, d_ref, core_ref, out_ref, block_ref):
    level = (a_ref[...] + b_ref[...]) + (c_ref[...] + d_ref[...])
    odd = lax.axis_index("cores") % 2 == 1
    applied(factored(level, 0.0), odd, core_ref, out_ref, block_ref)


def vmem():
    return pl.BlockSpec(memory_space=pltpu.VMEM)


def smem():
    return pl.BlockSpec(memory_space=pltpu.SMEM)


def call(kernel, outs, ins, scratch=(), name=None, aliases={}):
    return pl.pallas_call(
        kernel,
        out_shape=outs,
        in_specs=ins,
        out_specs=jax.tree.map(lambda o: smem() if o.dtype == jnp.int32 and o.size == 1 else vmem(), outs),
        scratch_shapes=list(scratch),
        input_output_aliases=aliases,
        compiler_params=pltpu.CompilerParams(vmem_limit_bytes=BIG),
        name=name,
    )


def shape(*dims, dtype=F32):
    return jax.ShapeDtypeStruct(dims, dtype)


def on_device(cores, indices, observed, step_size):
    peers = lax.axis_size("samp")
    count = indices.shape[0]
    slab = N // peers
    table = cores[0]
    idx = indices.T
    step = step_size.reshape(1)

    half = count // 2
    siblings = [(m, m ^ 1) for m in range(MODES)]
    other_table = lax.ppermute(table, "cores", siblings)
    hot = [pltpu.VMEM((N, half), BF16)]
    mats, slot, most = pl.pallas_call(
        functools.partial(gather_kernel, peers=peers),
        grid=(RR // COLS,),
        in_specs=[
            pl.BlockSpec((MODES, count), lambda i: (0, 0)),
            pl.BlockSpec((N, COLS), lambda i: (0, i)),
        ],
        out_specs=[vmem(), vmem(), vmem()],
        out_shape=[shape(2 * RR, half), shape(8, count, dtype=jnp.int32), shape(8, 128)],
        scratch_shapes=hot,
        compiler_params=pltpu.CompilerParams(vmem_limit_bytes=BIG),
        name="gather",
    )(*[pltpu.with_memory_space_constraint(a, pltpu.HBM) for a in (idx, table)])
    mats = call(
        gather_other_kernel, shape(2 * RR, half), [vmem()] * 3, hot, name="gather_other", aliases={2: 0}
    )(idx, other_table, mats)

    first = lax.axis_index("samp") * slab
    kept = lax.dynamic_slice_in_dim(table, first, slab, 0)
    base = kept.reshape(GROUPS, WIDE, R, R).transpose(0, 2, 1, 3)
    base = base.reshape(ROWS, LANES)

    vec = shape(R, half)
    recv, mids = [], []
    for turn in range(3):
        mid, out = call(
            functools.partial(hop_kernel, turn=turn),
            [vec, vec],
            [vmem()] * (2 if turn else 1),
            [] if turn else [pltpu.VMEM((R, half), F32)],
            name=f"hop{turn}",
        )(mats, *recv[-1:])
        pairs = [(2 * a + h, 2 * b + h) for a, b in ((turn, turn + 1), (3 - turn, 2 - turn)) for h in range(2)]
        recv.append(lax.ppermute(out, "cores", pairs))
        mids.append(mid)
    own_vecs, other_vecs = call(
        finish_kernel,
        [shape(2 * R, half)] * 2,
        [vmem()] * 9,
        [pltpu.VMEM((R, half), F32)] * 2,
        name="finish",
    )(mats, *recv, *mids, out, observed.reshape(1, count))
    got_vecs = lax.ppermute(other_vecs, "cores", siblings)
    part = call(route_own_kernel, shape(peers, FEATS, SLOTS), [vmem()] * 2, name="route_own")(own_vecs, slot)
    pay, values = call(
        route_kernel,
        (shape(peers, FEATS, SLOTS), shape(FEATS, count)),
        [vmem()] * 5,
        name="route",
    )(own_vecs, got_vecs, slot, most, part)

    def exchanged(block):
        return lax.all_to_all(block, "samp", 0, 0, tiled=True)

    def collected(recv, so_far):
        return call(
            collect_kernel,
            (shape(ROWS, LANES), shape(1, dtype=jnp.int32)),
            [smem(), vmem(), vmem()],
            name="collect",
        )(step, recv, so_far)

    updated, turns = collected(exchanged(pay), base)

    def more(state):
        return state[0] < turns[0]

    def another(state):
        turn, so_far = state
        pay = call(
            again_kernel,
            shape(peers, FEATS, SLOTS),
            [smem(), vmem(), vmem(), vmem()],
            name="again",
        )(turn.reshape(1), values, slot, most)
        return turn + 1, collected(exchanged(pay), so_far)[0]

    _, updated = lax.while_loop(more, another, (jnp.int32(1), updated))

    side = int(peers**0.5)

    def partner(mode, peer, by):
        z, x = peer // side, peer % side
        return (z + by) % side * side + x if mode % 2 else z * side + (x + by) % side

    ring = [
        [(m * peers + p, m * peers + partner(m, p, w)) for m in range(MODES) for p in range(peers)]
        for w in range(1, WAYS)
    ]
    level = [[(p, partner(1, p, w)) for p in range(peers)] for w in range(1, WAYS)]
    own = [updated] + [lax.ppermute(updated, ("cores", "samp"), pairs) for pairs in ring]
    other = [lax.ppermute(o, "cores", siblings) for o in own]
    stack = shape(3 * WAYS * ROWS, LANES, dtype=BF16)
    flat = shape(LANES, 3 * WAYS * ROWS, dtype=BF16)

    saved, sums = [], []
    recv = None
    for pair in range(MODES // 2):
        last = pair == MODES // 2 - 1
        outs = [shape(24, 128)] if last else [shape(2 * peers, 24, 128), shape(24, 128)]
        if pair:
            ins = [recv] + (saved + even if last else even + odd)
            outs.append(shape(24, 128))
        else:
            ins = own + other
            outs = [stack, flat] * 2 + outs
        res = call(
            functools.partial(pair_kernel, pair=pair),
            outs,
            [vmem()] * len(ins),
            [pltpu.VMEM((3 * WAYS * ROWS, LANES), BF16)],
            name=f"pair{pair}",
        )(*ins)
        if pair:
            sums.append(res[-1])
        else:
            even, odd, res = list(res[:2]), list(res[2:4]), res[4:]
        if last:
            parts = [res[0]] + [lax.ppermute(res[0], "samp", pairs) for pairs in level]
        else:
            saved.append(res[1])
            groups = []
            for c in (pair, pair + 2):
                for h in range(2):
                    both = [2 * (c % 4) + h, 2 * ((c + 1) % 4) + h]
                    groups.append([m * peers + j for m in both for j in range(peers)])
            recv = lax.all_to_all(
                res[0], ("cores", "samp"), 0, 0, axis_index_groups=groups, tiled=True
            )

    block = [pltpu.VMEM((LANES, LANES), F32)]
    ahead = call(known_kernel, shape(ROWS, LANES), [vmem()] * (MODES // 2), block, name="known")(*sums, updated)
    out = call(final_kernel, shape(ROWS, LANES), [vmem()] * (WAYS + 1), block, name="final")(*parts, ahead)
    out = out.reshape(GROUPS, R, WIDE, R).transpose(0, 2, 1, 3)
    return out.reshape(1, slab, RR)


def solution(mesh):
    in_specs = (P("cores", None, None), P("samp", None), P("samp"), P())
    out_specs = P("cores", "samp", None)
    return jax.shard_map(
        on_device, mesh=mesh, in_specs=in_specs, out_specs=out_specs, check_vma=False
    )
```

```python
import functools

import jax
import jax.numpy as jnp
from jax import lax
from jax.experimental import pallas as pl
from jax.experimental.pallas import tpu as pltpu
from jax.sharding import PartitionSpec as P

R = 48
N = 512
MODES = 8
RR = R * R
GROUPS = 4
WIDE = 8
ROWS = GROUPS * R
LANES = WIDE * R
FEATS = 104
SLOTS = 128
WAYS = 4
HIGH = lax.Precision.HIGHEST
F32 = jnp.float32
BF16 = jnp.bfloat16
COLS = 768
BIG = 14 << 20


def dot_rows(a, b):
    return lax.dot_general(a, b, (((0,), (0,)), ((), ())), preferred_element_type=F32)


def dot_lanes(a, b, precision=None):
    return lax.dot_general(
        a, b, (((1,), (1,)), ((), ())), preferred_element_type=F32, precision=precision
    )


def halves(x):
    hi = x.astype(BF16)
    return hi, (x - hi.astype(F32)).astype(BF16)


def iota(shape, dim):
    return lax.broadcasted_iota(jnp.int32, shape, dim)


def ranks(row, peers, slab):
    count = row.shape[1]
    chunks = count // 128
    dest = row // slab
    hit = (iota((peers, count), 0) == dest).astype(F32)
    stacked = jnp.concatenate([hit[:, c * 128 : (c + 1) * 128] for c in range(chunks)], axis=0)
    upper = (iota((128, 128), 0) <= iota((128, 128), 1)).astype(BF16)
    inside = jnp.dot(stacked.astype(BF16), upper, preferred_element_type=F32)
    before = jnp.zeros((peers, 1), F32)
    out = []
    for c in range(chunks):
        part = inside[c * peers : (c + 1) * peers]
        mine = hit[:, c * 128 : (c + 1) * 128]
        out.append(jnp.sum(mine * (part + before), axis=0, keepdims=True))
        before = before + part[:, 127:128]
    return jnp.concatenate(out, axis=1).astype(jnp.int32) - 1, dest


def half_of(row, second):
    half = row.shape[1] // 2
    flag = jnp.where(second, 1.0, 0.0)
    return jnp.where(flag > 0.5, row[:, half:], row[:, :half])


def one_hot(row, second, hot_ref):
    hot_ref[...] = (iota(hot_ref.shape, 0) == half_of(row, second)).astype(BF16)


def gathered(table, hot):
    hi, lo = halves(table)
    return dot_rows(hi, hot) + dot_rows(lo, hot)


def gather_kernel(idx_ref, table_ref, mats_ref, slot_ref, most_ref, hot_ref, *, peers):
    step = pl.program_id(0)
    mode = lax.axis_index("cores")

    @pl.when(step == 0)
    def _():
        row = idx_ref[pl.ds(mode, 1), :]
        one_hot(row, mode % 2 == 1, hot_ref)
        slab = N // peers
        place, dest = ranks(row, peers, slab)
        slot_ref[0:1, :] = place
        slot_ref[1:2, :] = dest
        slot_ref[2:3, :] = row - dest * slab
        slot_ref[3:8, :] = jnp.zeros((5, row.shape[1]), jnp.int32)
        every = idx_ref[...] // slab
        most = jnp.zeros((MODES, 1), F32)
        for j in range(peers):
            most = jnp.maximum(most, jnp.sum((every == j).astype(F32), axis=1, keepdims=True))
        most_ref[...] = jnp.broadcast_to(jnp.max(most, axis=0, keepdims=True), (8, 128))

    rows = pl.ds(pl.multiple_of(step * COLS, COLS), COLS)
    mats_ref[rows, :] = gathered(table_ref[...], hot_ref[...])


def gather_other_kernel(idx_ref, table_ref, _, mats_ref, hot_ref):
    mode = lax.axis_index("cores")
    second = mode % 2
    one_hot(idx_ref[pl.ds(mode + 1 - 2 * second, 1), :], second == 1, hot_ref)
    for at in range(0, RR, COLS):
        mats_ref[RR + at : RR + at + COLS, :] = gathered(table_ref[:, at : at + COLS], hot_ref[...])


def times(left, mats_ref, base, vec_ref, out_ref):
    count = vec_ref.shape[1]

    def rows(a):
        return pl.ds(pl.multiple_of(base + a * R, 8), R)

    @pl.when(left)
    def _():
        def chunk(c, _):
            lanes = pl.ds(pl.multiple_of(c * 128, 128), 128)
            acc = [jnp.zeros((R, 128), F32) for _ in range(2)]
            for a in range(R):
                acc[a % 2] = acc[a % 2] + mats_ref[rows(a), lanes] * vec_ref[a : a + 1, lanes]
            out_ref[:, lanes] = acc[0] + acc[1]
            return 0

        lax.fori_loop(0, count // 128, chunk, 0)

    @pl.when(jnp.logical_not(left))
    def _():
        def chunk(c, _):
            lanes = pl.ds(pl.multiple_of(c * 128, 128), 128)
            vec = vec_ref[:, lanes]
            for a in range(0, R, 8):
                sums = [
                    jnp.sum(mats_ref[rows(a + i), lanes] * vec, axis=0, keepdims=True) for i in range(8)
                ]
                out_ref[a : a + 8, lanes] = jnp.concatenate(sums, axis=0)
            return 0

        lax.fori_loop(0, count // 128, chunk, 0)


def heading(turn):
    mode = lax.axis_index("cores")
    chips = MODES // 2
    left = (mode // 2 < chips // 2) if turn < chips // 2 else (mode // 2 >= chips // 2)
    even = (mode % 2) * RR
    return left, jnp.where(left, even, RR - even)


def column(mats_ref, base):
    rows = [mats_ref[pl.ds(pl.multiple_of(base + a * R, 8), 1), :] for a in range(R)]
    return jnp.concatenate(rows, axis=0)


def row(mats_ref, base):
    return mats_ref[pl.ds(pl.multiple_of(base, 8), R), :]


def unit_at_ends(shape_):
    chip = lax.axis_index("cores") // 2
    edge = jnp.where(jnp.logical_or(chip == 0, chip == MODES // 2 - 1), 1.0, 0.0)
    return jnp.where(iota(shape_, 0) == 0, edge, 0.0)


def hop_kernel(mats_ref, *refs, turn):
    mid_ref, out_ref = refs[-2:]
    chip = lax.axis_index("cores") // 2
    live = jnp.logical_or(chip == turn, chip == MODES // 2 - 1 - turn)
    left, base = heading(turn)

    @pl.when(live)
    def _():
        if turn == 0:

            @pl.when(left)
            def _():
                mid_ref[...] = row(mats_ref, base)

            @pl.when(jnp.logical_not(left))
            def _():
                mid_ref[...] = column(mats_ref, base)
        else:
            times(left, mats_ref, base, refs[0], mid_ref)
        times(left, mats_ref, RR - base, mid_ref, out_ref)

    @pl.when(jnp.logical_not(live))
    def _():
        mid_ref[...] = jnp.zeros(mid_ref.shape, F32)
        out_ref[...] = jnp.zeros(out_ref.shape, F32)


def finish_kernel(mats_ref, *refs):
    recv, mids = refs[0:3], refs[3:6]
    out2_ref, obs_ref, own_ref, other_ref, mid_ref, part_ref = refs[6:]
    mode = lax.axis_index("cores")
    left, base = heading(3)
    times(left, mats_ref, base, recv[2], mid_ref)

    @pl.when(left)
    def _():
        part_ref[...] = column(mats_ref, RR - base)

    @pl.when(jnp.logical_not(left))
    def _():
        part_ref[...] = row(mats_ref, RR - base)

    end1 = unit_at_ends(mid_ref.shape) + recv[0][...]
    mid1 = mids[0][...] + mids[1][...]
    end2 = recv[1][...] + recv[2][...]
    mid2 = mids[2][...] + mid_ref[...]
    predicted = jnp.sum(out2_ref[...] * end1 + part_ref[...] * mid_ref[...], axis=0, keepdims=True)
    residual = predicted - half_of(obs_ref[...], mode % 2 == 1)
    early = jnp.where(mode // 2 < MODES // 4, 1.0, 0.0) > 0.5
    even = (jnp.where(early, end1, end2), jnp.where(early, mid2, mid1) * residual)
    odd = (jnp.where(early, mid1, mid2), jnp.where(early, end2, end1) * residual)
    second = jnp.where(mode % 2 == 1, 1.0, 0.0) > 0.5
    for k in range(2):
        rows = slice(k * R, (k + 1) * R)
        own_ref[rows, :] = jnp.where(second, odd[k], even[k])
        other_ref[rows, :] = jnp.where(second, even[k], odd[k])


def keys(slot_ref, turn):
    place = slot_ref[0:1, :] - turn * SLOTS
    fits = jnp.logical_and(place >= 0, place < SLOTS)
    return jnp.where(fits, slot_ref[1:2, :] * SLOTS + place, -1)


def spread(values, key, pay_ref, so_far_ref=None):
    hi, lo = halves(values)
    both = jnp.concatenate([hi, lo], axis=0)
    for pair in range(pay_ref.shape[0] // 2):
        base = pair * 2 * SLOTS
        hot = (iota((2 * SLOTS, values.shape[1]), 0) + base == key).astype(BF16)
        out = dot_lanes(both, hot)
        out = out[:FEATS] + out[FEATS:]
        for k in range(2):
            part = out[:, k * SLOTS : (k + 1) * SLOTS]
            peer = 2 * pair + k
            pay_ref[peer] = part if so_far_ref is None else part + so_far_ref[peer]


def mark(most_ref, pay_ref):
    for peer in range(pay_ref.shape[0]):
        pay_ref[peer, 97:98, :] = most_ref[0:1, :]


def with_place(vecs, loc):
    pad = jnp.zeros((FEATS - 97, vecs.shape[1]), F32)
    return jnp.concatenate([vecs, loc.astype(F32), pad], axis=0)


def route_own_kernel(vecs_ref, slot_ref, pay_ref):
    second = lax.axis_index("cores") % 2 == 1
    values = with_place(vecs_ref[...], half_of(slot_ref[2:3, :], second))
    spread(values, half_of(keys(slot_ref, 0), second), pay_ref)


def route_kernel(own_ref, got_ref, slot_ref, most_ref, part_ref, pay_ref, val_ref):
    first = lax.axis_index("cores") % 2 == 0
    own = own_ref[...]
    got = got_ref[...]
    values = with_place(got, half_of(slot_ref[2:3, :], first))
    spread(values, half_of(keys(slot_ref, 0), first), pay_ref, part_ref)
    mark(most_ref, pay_ref)
    flag = jnp.where(first, 1.0, 0.0) > 0.5
    vecs = jnp.concatenate([jnp.where(flag, own, got), jnp.where(flag, got, own)], axis=1)
    val_ref[...] = with_place(vecs, slot_ref[2:3, :])


def again_kernel(turn_ref, val_ref, slot_ref, most_ref, pay_ref):
    spread(val_ref[...], keys(slot_ref, turn_ref[0]), pay_ref)
    mark(most_ref, pay_ref)


def collect_kernel(step_ref, recv_ref, base_ref, out_ref, turns_ref):
    peers = recv_ref.shape[0]
    left = jnp.concatenate([recv_ref[s, 0:R, :] for s in range(peers)], axis=1)
    right = jnp.concatenate([recv_ref[s, R : 2 * R, :] for s in range(peers)], axis=1)
    loc = jnp.concatenate([recv_ref[s, 96:97, :] for s in range(peers)], axis=1).astype(jnp.int32)
    row_of = loc // WIDE
    lane_of = loc - row_of * WIDE
    count = loc.shape[1]

    def picked(x, key, n):
        hi = x.astype(BF16).astype(F32)
        lo = x - hi
        his, los = [], []
        for i in range(n):
            here = key == i
            his += [jnp.where(here, hi, 0.0).astype(BF16)]
            los += [jnp.where(here, lo, 0.0).astype(BF16)]
        return jnp.concatenate(his, axis=0), jnp.concatenate(los, axis=0)

    xh, xl = picked(left, row_of, GROUPS)
    yh, yl = picked(right, lane_of, WIDE)
    grad = dot_lanes(xh, yh) + (dot_lanes(xh, yl) + dot_lanes(xl, yh))
    out_ref[...] = base_ref[...] - step_ref[0] * grad
    most = jnp.max(recv_ref[:, 97, :]).astype(jnp.int32)
    turns_ref[0] = (most + SLOTS - 1) // SLOTS


def arrange(refs):
    own = refs[:WAYS]
    other = refs[WAYS : 2 * WAYS]
    outs = refs[2 * WAYS :]
    even_first = jnp.where(lax.axis_index("cores") % 2 == 0, 1.0, 0.0)
    for w in range(WAYS):
        mine = own[w][...]
        theirs = other[w][...]
        for k in range(2):
            stack_ref, turned_ref = outs[2 * k : 2 * k + 2]
            flag = even_first if k == 0 else 1.0 - even_first
            core = jnp.where(flag > 0.5, mine, theirs)
            hi, lo = halves(core)
            for g in range(GROUPS):
                at = 3 * (w * GROUPS + g) * R
                here = slice(g * R, (g + 1) * R)
                stack_ref[at : at + R, :] = hi[here]
                stack_ref[at + R : at + 2 * R, :] = hi[here]
                stack_ref[at + 2 * R : at + 3 * R, :] = lo[here]
            hi, lo = halves(core.T)
            for k3, piece in enumerate((hi, hi, lo)):
                turned_ref[:, (k3 * WAYS + w) * ROWS : (k3 * WAYS + w + 1) * ROWS] = piece


def stacked(square):
    wide = jnp.concatenate([square, jnp.zeros((R, 128), F32)], axis=1)
    hi = wide.astype(BF16).astype(F32)
    lo = wide - hi
    return (hi + (pltpu.roll(lo, R, 1) + pltpu.roll(hi, 2 * R, 1)))[:, : 3 * R].astype(BF16)


def packed_of(full):
    lane = iota((24, 128), 1)
    return jnp.where(lane < 64, full[0:24], pltpu.roll(full[24:48], 64, 1))


def whole(packed):
    both = jnp.concatenate([packed, pltpu.roll(packed, 64, 1)], axis=0)
    return jnp.where(iota((R, 128), 1) < R, both, 0.0)


def pulled(before, core, prod_ref):
    stack, turned = core
    all_rows = WAYS * ROWS
    weights = None if before is None else stacked(before)
    for g in range(WAYS * GROUPS):
        at = 3 * g * R
        if before is None:
            hi, lo = stack[at : at + R, :], stack[at + 2 * R : at + 3 * R, :]
        else:
            hi, lo = halves(
                jnp.dot(weights, stack[at : at + 3 * R, :], preferred_element_type=F32)
            )
        for k3, piece in enumerate((hi, lo, hi)):
            prod_ref[k3 * all_rows + g * R : k3 * all_rows + (g + 1) * R, :] = piece
    total = jnp.zeros((R, 256), F32)
    for part, slices in ((0, range(5)), (128, range(5, WIDE))):
        cols = slice(part, part + 256)
        z = jnp.dot(turned[cols, :], prod_ref[:, cols], preferred_element_type=F32)
        for h in slices:
            at = h * R - part
            block = z[at : at + R]
            total = total + (pltpu.roll(block, 256 - at, 1) if at else block)
    return jnp.where(iota((R, 128), 1) < R, total[:, :128], 0.0) * (1.0 / N)


def pair_kernel(*refs, pair):
    last = pair == MODES // 2 - 1
    refs = list(refs)
    recv_ref = refs.pop(0) if pair else None
    saved = [refs.pop(0) for _ in range(pair)] if last else []
    prod_ref = refs.pop()
    if pair:
        even = [refs.pop(0) for _ in range(2)]
        odd = None if last else [refs.pop(0) for _ in range(2)]
        sum_ref = refs.pop()
        sum_ref[...] = jnp.sum(recv_ref[0 : recv_ref.shape[0] // 2], axis=0)
    else:
        cores = refs[2 * WAYS : 2 * WAYS + 4]
        arrange(refs[: 2 * WAYS + 4])
        even, odd = cores[:2], cores[2:]
        refs = refs[2 * WAYS + 4 :]
    kept_ref = refs.pop()
    live = lax.axis_index("cores") // 2 == pair

    @pl.when(live)
    def _():
        middle = pulled(whole(sum_ref[...]) if pair else None, even, prod_ref)
        kept_ref[...] = packed_of(middle)
        if not last:
            packed = packed_of(pulled(middle, odd, prod_ref))
            for peer in range(refs[0].shape[0]):
                refs[0][peer] = packed

    @pl.when(jnp.logical_not(live))
    def _():
        kept = jnp.zeros((24, 128), F32)
        for s in saved:
            kept = kept + s[...]
        kept_ref[...] = kept
        if not last:
            refs[0][...] = jnp.zeros(refs[0].shape, F32)


def factored(packed, absent):
    row = iota((R, 128), 0)
    lane = iota((R, 128), 1)
    eye = jnp.where(lane == row, 1.0, 0.0)
    full = whole(packed) + eye * absent + jnp.where(lane == row + 64, 1.0, 0.0)
    m = [full[8 * t : 8 * t + 8] for t in range(R // 8)]
    for begin in range(0, R, 4):
        top = begin // 8
        below = range(top, R // 8)
        col = [
            {t: jnp.broadcast_to(m[t][:, begin + k : begin + k + 1], (8, 128)) for t in below} for k in range(4)
        ]
        for k in range(4):
            at = begin + k - 8 * top
            scale = 1.0 / col[k][top][at : at + 1]
            fact = {t: col[k][t] * scale for t in below}
            fact[top] = jnp.where(iota((8, 128), 0) > at, fact[top], 0.0)
            pivot = m[top][at : at + 1]
            for q in range(k + 1, 4):
                lead = col[q][top][at : at + 1]
                for t in below:
                    col[q][t] = col[q][t] - fact[t] * lead
            for t in below:
                m[t] = m[t] - fact[t] * pivot
    m = jnp.concatenate(m, axis=0)
    diag = jnp.sum(jnp.where(lane == row, m, 0.0), axis=1, keepdims=True)
    return m * (1.0 / jnp.sqrt(diag))


def from_left(tri, in_ref, out_ref):
    for g in range(GROUPS):
        rows = slice(g * R, (g + 1) * R)
        out_ref[rows, :] = jnp.dot(
            tri[:, :R], in_ref[rows, :], preferred_element_type=F32, precision=HIGH
        )


def from_right(tri, in_ref, out_ref, block_ref):
    inv = jnp.where(iota((R, 128), 1) < R, pltpu.roll(tri, 64, 1), 0.0)
    wide = jnp.concatenate([inv, jnp.zeros((R, LANES - 128), F32)], axis=1)
    for h in range(WIDE):
        block_ref[h * R : (h + 1) * R, :] = pltpu.roll(wide, h * R, 1) if h else wide
    out_ref[...] = dot_lanes(in_ref[...], block_ref[...], HIGH)


def applied(tri, left, in_ref, out_ref, block_ref):
    @pl.when(left)
    def _():
        from_left(tri, in_ref, out_ref)

    @pl.when(jnp.logical_not(left))
    def _():
        from_right(tri, in_ref, out_ref, block_ref)


def known_kernel(*refs):
    *sums, core_ref, out_ref, block_ref = refs
    mode = lax.axis_index("cores")
    chip = mode // 2
    first = jnp.where(mode % 2 == 0, 1.0, 0.0)
    known = jnp.zeros((24, 128), F32)
    for p, s in enumerate(sums):
        known = known + s[...] * jnp.where(chip == p, 1.0 - first, 0.0)
        known = known + s[...] * jnp.where(chip == p + 1, first, 0.0)
    absent = jnp.where(jnp.logical_or(mode == 0, mode == MODES - 1), 1.0, 0.0)
    applied(factored(known, absent), mode % 2 == 0, core_ref, out_ref, block_ref)


def final_kernel(a_ref, b_ref, c_ref, d_ref, core_ref, out_ref, block_ref):
    level = (a_ref[...] + b_ref[...]) + (c_ref[...] + d_ref[...])
    odd = lax.axis_index("cores") % 2 == 1
    applied(factored(level, 0.0), odd, core_ref, out_ref, block_ref)


def vmem():
    return pl.BlockSpec(memory_space=pltpu.VMEM)


def smem():
    return pl.BlockSpec(memory_space=pltpu.SMEM)


def call(kernel, outs, ins, scratch=(), name=None, aliases={}):
    return pl.pallas_call(
        kernel,
        out_shape=outs,
        in_specs=ins,
        out_specs=jax.tree.map(lambda o: smem() if o.dtype == jnp.int32 and o.size == 1 else vmem(), outs),
        scratch_shapes=list(scratch),
        input_output_aliases=aliases,
        compiler_params=pltpu.CompilerParams(vmem_limit_bytes=BIG),
        name=name,
    )


def shape(*dims, dtype=F32):
    return jax.ShapeDtypeStruct(dims, dtype)


def on_device(cores, indices, observed, step_size):
    peers = lax.axis_size("samp")
    count = indices.shape[0]
    slab = N // peers
    table = cores[0]
    idx = indices.T
    step = step_size.reshape(1)

    half = count // 2
    siblings = [(m, m ^ 1) for m in range(MODES)]
    other_table = lax.ppermute(table, "cores", siblings)
    hot = [pltpu.VMEM((N, half), BF16)]
    mats, slot, most = pl.pallas_call(
        functools.partial(gather_kernel, peers=peers),
        grid=(RR // COLS,),
        in_specs=[
            pl.BlockSpec((MODES, count), lambda i: (0, 0)),
            pl.BlockSpec((N, COLS), lambda i: (0, i)),
        ],
        out_specs=[vmem(), vmem(), vmem()],
        out_shape=[shape(2 * RR, half), shape(8, count, dtype=jnp.int32), shape(8, 128)],
        scratch_shapes=hot,
        compiler_params=pltpu.CompilerParams(vmem_limit_bytes=BIG),
        name="gather",
    )(*[pltpu.with_memory_space_constraint(a, pltpu.HBM) for a in (idx, table)])
    mats = call(
        gather_other_kernel, shape(2 * RR, half), [vmem()] * 3, hot, name="gather_other", aliases={2: 0}
    )(idx, other_table, mats)

    first = lax.axis_index("samp") * slab
    kept = lax.dynamic_slice_in_dim(table, first, slab, 0)
    base = kept.reshape(GROUPS, WIDE, R, R).transpose(0, 2, 1, 3)
    base = base.reshape(ROWS, LANES)

    vec = shape(R, half)
    recv, mids = [], []
    for turn in range(3):
        mid, out = call(
            functools.partial(hop_kernel, turn=turn),
            [vec, vec],
            [vmem()] * (2 if turn else 1),
            name=f"hop{turn}",
        )(mats, *recv[-1:])
        pairs = [(2 * a + h, 2 * b + h) for a, b in ((turn, turn + 1), (3 - turn, 2 - turn)) for h in range(2)]
        recv.append(lax.ppermute(out, "cores", pairs))
        mids.append(mid)
    own_vecs, other_vecs = call(
        finish_kernel,
        [shape(2 * R, half)] * 2,
        [vmem()] * 9,
        [pltpu.VMEM((R, half), F32)] * 2,
        name="finish",
    )(mats, *recv, *mids, out, observed.reshape(1, count))
    got_vecs = lax.ppermute(other_vecs, "cores", siblings)
    part = call(route_own_kernel, shape(peers, FEATS, SLOTS), [vmem()] * 2, name="route_own")(own_vecs, slot)
    pay, values = call(
        route_kernel,
        (shape(peers, FEATS, SLOTS), shape(FEATS, count)),
        [vmem()] * 5,
        name="route",
    )(own_vecs, got_vecs, slot, most, part)

    def exchanged(block):
        return lax.all_to_all(block, "samp", 0, 0, tiled=True)

    def collected(recv, so_far):
        return call(
            collect_kernel,
            (shape(ROWS, LANES), shape(1, dtype=jnp.int32)),
            [smem(), vmem(), vmem()],
            name="collect",
        )(step, recv, so_far)

    updated, turns = collected(exchanged(pay), base)

    def more(state):
        return state[0] < turns[0]

    def another(state):
        turn, so_far = state
        pay = call(
            again_kernel,
            shape(peers, FEATS, SLOTS),
            [smem(), vmem(), vmem(), vmem()],
            name="again",
        )(turn.reshape(1), values, slot, most)
        return turn + 1, collected(exchanged(pay), so_far)[0]

    _, updated = lax.while_loop(more, another, (jnp.int32(1), updated))

    side = int(peers**0.5)

    def partner(mode, peer, by):
        z, x = peer // side, peer % side
        return (z + by) % side * side + x if mode % 2 else z * side + (x + by) % side

    ring = [
        [(m * peers + p, m * peers + partner(m, p, w)) for m in range(MODES) for p in range(peers)]
        for w in range(1, WAYS)
    ]
    level = [[(p, partner(1, p, w)) for p in range(peers)] for w in range(1, WAYS)]
    own = [updated] + [lax.ppermute(updated, ("cores", "samp"), pairs) for pairs in ring]
    other = [lax.ppermute(o, "cores", siblings) for o in own]
    stack = shape(3 * WAYS * ROWS, LANES, dtype=BF16)
    flat = shape(LANES, 3 * WAYS * ROWS, dtype=BF16)

    saved, sums = [], []
    recv = None
    for pair in range(MODES // 2):
        last = pair == MODES // 2 - 1
        outs = [shape(24, 128)] if last else [shape(2 * peers, 24, 128), shape(24, 128)]
        if pair:
            ins = [recv] + (saved + even if last else even + odd)
            outs.append(shape(24, 128))
        else:
            ins = own + other
            outs = [stack, flat] * 2 + outs
        res = call(
            functools.partial(pair_kernel, pair=pair),
            outs,
            [vmem()] * len(ins),
            [pltpu.VMEM((3 * WAYS * ROWS, LANES), BF16)],
            name=f"pair{pair}",
        )(*ins)
        if pair:
            sums.append(res[-1])
        else:
            even, odd, res = list(res[:2]), list(res[2:4]), res[4:]
        if last:
            parts = [res[0]] + [lax.ppermute(res[0], "samp", pairs) for pairs in level]
        else:
            saved.append(res[1])
            groups = []
            for c in (pair, pair + 2):
                for h in range(2):
                    both = [2 * (c % 4) + h, 2 * ((c + 1) % 4) + h]
                    groups.append([m * peers + j for m in both for j in range(peers)])
            recv = lax.all_to_all(
                res[0], ("cores", "samp"), 0, 0, axis_index_groups=groups, tiled=True
            )

    block = [pltpu.VMEM((LANES, LANES), F32)]
    ahead = call(known_kernel, shape(ROWS, LANES), [vmem()] * (MODES // 2), block, name="known")(*sums, updated)
    out = call(final_kernel, shape(ROWS, LANES), [vmem()] * (WAYS + 1), block, name="final")(*parts, ahead)
    out = out.reshape(GROUPS, R, WIDE, R).transpose(0, 2, 1, 3)
    return out.reshape(1, slab, RR)


def solution(mesh):
    in_specs = (P("cores", None, None), P("samp", None), P("samp"), P())
    out_specs = P("cores", "samp", None)
    return jax.shard_map(
        on_device, mesh=mesh, in_specs=in_specs, out_specs=out_specs, check_vma=False
    )
```

```python
import functools

import jax
import jax.numpy as jnp
from jax import lax
from jax.experimental import pallas as pl
from jax.experimental.pallas import tpu as pltpu
from jax.sharding import PartitionSpec as P

R = 48
N = 512
MODES = 8
RR = R * R
GROUPS = 4
WIDE = 8
ROWS = GROUPS * R
LANES = WIDE * R
FEATS = 104
SLOTS = 128
WAYS = 4
HIGH = lax.Precision.HIGHEST
F32 = jnp.float32
BF16 = jnp.bfloat16
COLS = 768
BIG = 14 << 20


def dot_rows(a, b):
    return lax.dot_general(a, b, (((0,), (0,)), ((), ())), preferred_element_type=F32)


def dot_lanes(a, b, precision=None):
    return lax.dot_general(
        a, b, (((1,), (1,)), ((), ())), preferred_element_type=F32, precision=precision
    )


def halves(x):
    hi = x.astype(BF16)
    return hi, (x - hi.astype(F32)).astype(BF16)


def iota(shape, dim):
    return lax.broadcasted_iota(jnp.int32, shape, dim)


def ranks(row, peers, slab):
    count = row.shape[1]
    chunks = count // 128
    dest = row // slab
    hit = (iota((peers, count), 0) == dest).astype(F32)
    stacked = jnp.concatenate([hit[:, c * 128 : (c + 1) * 128] for c in range(chunks)], axis=0)
    upper = (iota((128, 128), 0) <= iota((128, 128), 1)).astype(BF16)
    inside = jnp.dot(stacked.astype(BF16), upper, preferred_element_type=F32)
    before = jnp.zeros((peers, 1), F32)
    out = []
    for c in range(chunks):
        part = inside[c * peers : (c + 1) * peers]
        mine = hit[:, c * 128 : (c + 1) * 128]
        out.append(jnp.sum(mine * (part + before), axis=0, keepdims=True))
        before = before + part[:, 127:128]
    return jnp.concatenate(out, axis=1).astype(jnp.int32) - 1, dest


def half_of(row, second):
    half = row.shape[1] // 2
    flag = jnp.where(second, 1.0, 0.0)
    return jnp.where(flag > 0.5, row[:, half:], row[:, :half])


def one_hot(row, second, hot_ref):
    hot_ref[...] = (iota(hot_ref.shape, 0) == half_of(row, second)).astype(BF16)


def gathered(table, hot):
    hi, lo = halves(table)
    return dot_rows(hi, hot) + dot_rows(lo, hot)


def gather_kernel(idx_ref, table_ref, mats_ref, slot_ref, most_ref, hot_ref, *, peers):
    step = pl.program_id(0)
    mode = lax.axis_index("cores")

    @pl.when(step == 0)
    def _():
        row = idx_ref[pl.ds(mode, 1), :]
        one_hot(row, mode % 2 == 1, hot_ref)
        slab = N // peers
        place, dest = ranks(row, peers, slab)
        slot_ref[0:1, :] = place
        slot_ref[1:2, :] = dest
        slot_ref[2:3, :] = row - dest * slab
        slot_ref[3:8, :] = jnp.zeros((5, row.shape[1]), jnp.int32)
        every = idx_ref[...] // slab
        most = jnp.zeros((MODES, 1), F32)
        for j in range(peers):
            most = jnp.maximum(most, jnp.sum((every == j).astype(F32), axis=1, keepdims=True))
        most_ref[...] = jnp.broadcast_to(jnp.max(most, axis=0, keepdims=True), (8, 128))

    rows = pl.ds(pl.multiple_of(step * COLS, COLS), COLS)
    mats_ref[rows, :] = gathered(table_ref[...], hot_ref[...])


def gather_other_kernel(idx_ref, table_ref, _, mats_ref, hot_ref):
    mode = lax.axis_index("cores")
    second = mode % 2
    one_hot(idx_ref[pl.ds(mode + 1 - 2 * second, 1), :], second == 1, hot_ref)
    for at in range(0, RR, COLS):
        mats_ref[RR + at : RR + at + COLS, :] = gathered(table_ref[:, at : at + COLS], hot_ref[...])


def times(left, mats_ref, base, vec_ref, out_ref):
    count = vec_ref.shape[1]

    def rows(a):
        return pl.ds(pl.multiple_of(base + a * R, 8), R)

    @pl.when(left)
    def _():
        def chunk(c, _):
            lanes = pl.ds(pl.multiple_of(c * 128, 128), 128)
            acc = [jnp.zeros((R, 128), F32) for _ in range(2)]
            for a in range(R):
                acc[a % 2] = acc[a % 2] + mats_ref[rows(a), lanes] * vec_ref[a : a + 1, lanes]
            out_ref[:, lanes] = acc[0] + acc[1]
            return 0

        lax.fori_loop(0, count // 128, chunk, 0)

    @pl.when(jnp.logical_not(left))
    def _():
        def chunk(c, _):
            lanes = pl.ds(pl.multiple_of(c * 128, 128), 128)
            vec = vec_ref[:, lanes]
            for a in range(0, R, 8):
                sums = [
                    jnp.sum(mats_ref[rows(a + i), lanes] * vec, axis=0, keepdims=True) for i in range(8)
                ]
                out_ref[a : a + 8, lanes] = jnp.concatenate(sums, axis=0)
            return 0

        lax.fori_loop(0, count // 128, chunk, 0)


def heading(turn):
    mode = lax.axis_index("cores")
    chips = MODES // 2
    left = (mode // 2 < chips // 2) if turn < chips // 2 else (mode // 2 >= chips // 2)
    even = (mode % 2) * RR
    return left, jnp.where(left, even, RR - even)


def column(mats_ref, base):
    rows = [mats_ref[pl.ds(pl.multiple_of(base + a * R, 8), 1), :] for a in range(R)]
    return jnp.concatenate(rows, axis=0)


def row(mats_ref, base):
    return mats_ref[pl.ds(pl.multiple_of(base, 8), R), :]


def unit_at_ends(shape_):
    chip = lax.axis_index("cores") // 2
    edge = jnp.where(jnp.logical_or(chip == 0, chip == MODES // 2 - 1), 1.0, 0.0)
    return jnp.where(iota(shape_, 0) == 0, edge, 0.0)


def hop_kernel(mats_ref, *refs, turn):
    mid_ref, out_ref = refs[-2:]
    chip = lax.axis_index("cores") // 2
    live = jnp.logical_or(chip == turn, chip == MODES // 2 - 1 - turn)
    left, base = heading(turn)

    @pl.when(live)
    def _():
        if turn == 0:

            @pl.when(left)
            def _():
                mid_ref[...] = row(mats_ref, base)

            @pl.when(jnp.logical_not(left))
            def _():
                mid_ref[...] = column(mats_ref, base)
        else:
            times(left, mats_ref, base, refs[0], mid_ref)
        times(left, mats_ref, RR - base, mid_ref, out_ref)

    @pl.when(jnp.logical_not(live))
    def _():
        mid_ref[...] = jnp.zeros(mid_ref.shape, F32)
        out_ref[...] = jnp.zeros(out_ref.shape, F32)


def finish_kernel(mats_ref, *refs):
    recv, mids = refs[0:3], refs[3:6]
    out2_ref, obs_ref, own_ref, other_ref, mid_ref, part_ref = refs[6:]
    mode = lax.axis_index("cores")
    left, base = heading(3)
    times(left, mats_ref, base, recv[2], mid_ref)

    @pl.when(left)
    def _():
        part_ref[...] = column(mats_ref, RR - base)

    @pl.when(jnp.logical_not(left))
    def _():
        part_ref[...] = row(mats_ref, RR - base)

    end1 = unit_at_ends(mid_ref.shape) + recv[0][...]
    mid1 = mids[0][...] + mids[1][...]
    end2 = recv[1][...] + recv[2][...]
    mid2 = mids[2][...] + mid_ref[...]
    predicted = jnp.sum(out2_ref[...] * end1 + part_ref[...] * mid_ref[...], axis=0, keepdims=True)
    residual = predicted - half_of(obs_ref[...], mode % 2 == 1)
    early = jnp.where(mode // 2 < MODES // 4, 1.0, 0.0) > 0.5
    even = (jnp.where(early, end1, end2), jnp.where(early, mid2, mid1) * residual)
    odd = (jnp.where(early, mid1, mid2), jnp.where(early, end2, end1) * residual)
    second = jnp.where(mode % 2 == 1, 1.0, 0.0) > 0.5
    for k in range(2):
        rows = slice(k * R, (k + 1) * R)
        own_ref[rows, :] = jnp.where(second, odd[k], even[k])
        other_ref[rows, :] = jnp.where(second, even[k], odd[k])


def keys(slot_ref, turn):
    place = slot_ref[0:1, :] - turn * SLOTS
    fits = jnp.logical_and(place >= 0, place < SLOTS)
    return jnp.where(fits, slot_ref[1:2, :] * SLOTS + place, -1)


def spread(values, key, pay_ref, so_far_ref=None):
    hi, lo = halves(values)
    both = jnp.concatenate([hi, lo], axis=0)
    for pair in range(pay_ref.shape[0] // 2):
        base = pair * 2 * SLOTS
        hot = (iota((2 * SLOTS, values.shape[1]), 0) + base == key).astype(BF16)
        out = dot_lanes(both, hot)
        out = out[:FEATS] + out[FEATS:]
        for k in range(2):
            part = out[:, k * SLOTS : (k + 1) * SLOTS]
            peer = 2 * pair + k
            pay_ref[peer] = part if so_far_ref is None else part + so_far_ref[peer]


def mark(most_ref, pay_ref):
    for peer in range(pay_ref.shape[0]):
        pay_ref[peer, 97:98, :] = most_ref[0:1, :]


def with_place(vecs, loc):
    pad = jnp.zeros((FEATS - 97, vecs.shape[1]), F32)
    return jnp.concatenate([vecs, loc.astype(F32), pad], axis=0)


def route_own_kernel(vecs_ref, slot_ref, pay_ref):
    second = lax.axis_index("cores") % 2 == 1
    values = with_place(vecs_ref[...], half_of(slot_ref[2:3, :], second))
    spread(values, half_of(keys(slot_ref, 0), second), pay_ref)


def route_kernel(own_ref, got_ref, slot_ref, most_ref, part_ref, pay_ref, val_ref):
    first = lax.axis_index("cores") % 2 == 0
    own = own_ref[...]
    got = got_ref[...]
    values = with_place(got, half_of(slot_ref[2:3, :], first))
    spread(values, half_of(keys(slot_ref, 0), first), pay_ref, part_ref)
    mark(most_ref, pay_ref)
    flag = jnp.where(first, 1.0, 0.0) > 0.5
    vecs = jnp.concatenate([jnp.where(flag, own, got), jnp.where(flag, got, own)], axis=1)
    val_ref[...] = with_place(vecs, slot_ref[2:3, :])


def again_kernel(turn_ref, val_ref, slot_ref, most_ref, pay_ref):
    spread(val_ref[...], keys(slot_ref, turn_ref[0]), pay_ref)
    mark(most_ref, pay_ref)


def collect_kernel(step_ref, recv_ref, base_ref, out_ref, turns_ref):
    peers = recv_ref.shape[0]
    left = jnp.concatenate([recv_ref[s, 0:R, :] for s in range(peers)], axis=1)
    right = jnp.concatenate([recv_ref[s, R : 2 * R, :] for s in range(peers)], axis=1)
    loc = jnp.concatenate([recv_ref[s, 96:97, :] for s in range(peers)], axis=1).astype(jnp.int32)
    row_of = loc // WIDE
    lane_of = loc - row_of * WIDE
    count = loc.shape[1]

    def picked(x, key, n):
        hi = x.astype(BF16).astype(F32)
        lo = x - hi
        his, los = [], []
        for i in range(n):
            here = key == i
            his += [jnp.where(here, hi, 0.0).astype(BF16)]
            los += [jnp.where(here, lo, 0.0).astype(BF16)]
        return jnp.concatenate(his, axis=0), jnp.concatenate(los, axis=0)

    xh, xl = picked(left, row_of, GROUPS)
    yh, yl = picked(right, lane_of, WIDE)
    grad = dot_lanes(xh, yh) + (dot_lanes(xh, yl) + dot_lanes(xl, yh))
    out_ref[...] = base_ref[...] - step_ref[0] * grad
    most = jnp.max(recv_ref[:, 97, :]).astype(jnp.int32)
    turns_ref[0] = (most + SLOTS - 1) // SLOTS


def arrange(refs):
    own = refs[:WAYS]
    other = refs[WAYS : 2 * WAYS]
    outs = refs[2 * WAYS :]
    even_first = jnp.where(lax.axis_index("cores") % 2 == 0, 1.0, 0.0)
    for w in range(WAYS):
        mine = own[w][...]
        theirs = other[w][...]
        for k in range(2):
            stack_ref, turned_ref = outs[2 * k : 2 * k + 2]
            flag = even_first if k == 0 else 1.0 - even_first
            core = jnp.where(flag > 0.5, mine, theirs)
            hi, lo = halves(core)
            for g in range(GROUPS):
                at = 3 * (w * GROUPS + g) * R
                here = slice(g * R, (g + 1) * R)
                stack_ref[at : at + R, :] = hi[here]
                stack_ref[at + R : at + 2 * R, :] = hi[here]
                stack_ref[at + 2 * R : at + 3 * R, :] = lo[here]
            hi, lo = halves(core.T)
            for k3, piece in enumerate((hi, hi, lo)):
                turned_ref[:, (k3 * WAYS + w) * ROWS : (k3 * WAYS + w + 1) * ROWS] = piece


def stacked(square):
    wide = jnp.concatenate([square, jnp.zeros((R, 128), F32)], axis=1)
    hi = wide.astype(BF16).astype(F32)
    lo = wide - hi
    return (hi + (pltpu.roll(lo, R, 1) + pltpu.roll(hi, 2 * R, 1)))[:, : 3 * R].astype(BF16)


def packed_of(full):
    lane = iota((24, 128), 1)
    return jnp.where(lane < 64, full[0:24], pltpu.roll(full[24:48], 64, 1))


def whole(packed):
    both = jnp.concatenate([packed, pltpu.roll(packed, 64, 1)], axis=0)
    return jnp.where(iota((R, 128), 1) < R, both, 0.0)


def pulled(before, core, prod_ref):
    stack, turned = core
    all_rows = WAYS * ROWS
    weights = None if before is None else stacked(before)
    for g in range(WAYS * GROUPS):
        at = 3 * g * R
        if before is None:
            hi, lo = stack[at : at + R, :], stack[at + 2 * R : at + 3 * R, :]
        else:
            hi, lo = halves(
                jnp.dot(weights, stack[at : at + 3 * R, :], preferred_element_type=F32)
            )
        for k3, piece in enumerate((hi, lo, hi)):
            prod_ref[k3 * all_rows + g * R : k3 * all_rows + (g + 1) * R, :] = piece
    total = jnp.zeros((R, 256), F32)
    for part, slices in ((0, range(5)), (128, range(5, WIDE))):
        cols = slice(part, part + 256)
        z = jnp.dot(turned[cols, :], prod_ref[:, cols], preferred_element_type=F32)
        for h in slices:
            at = h * R - part
            block = z[at : at + R]
            total = total + (pltpu.roll(block, 256 - at, 1) if at else block)
    return jnp.where(iota((R, 128), 1) < R, total[:, :128], 0.0) * (1.0 / N)


def pair_kernel(*refs, pair):
    last = pair == MODES // 2 - 1
    refs = list(refs)
    recv_ref = refs.pop(0) if pair else None
    saved = [refs.pop(0) for _ in range(pair)] if last else []
    prod_ref = refs.pop()
    if pair:
        even = [refs.pop(0) for _ in range(2)]
        odd = None if last else [refs.pop(0) for _ in range(2)]
        sum_ref = refs.pop()
        sum_ref[...] = jnp.sum(recv_ref[0 : recv_ref.shape[0] // 2], axis=0)
    else:
        cores = refs[2 * WAYS : 2 * WAYS + 4]
        arrange(refs[: 2 * WAYS + 4])
        even, odd = cores[:2], cores[2:]
        refs = refs[2 * WAYS + 4 :]
    kept_ref = refs.pop()
    live = lax.axis_index("cores") // 2 == pair

    @pl.when(live)
    def _():
        middle = pulled(whole(sum_ref[...]) if pair else None, even, prod_ref)
        kept_ref[...] = packed_of(middle)
        if not last:
            packed = packed_of(pulled(middle, odd, prod_ref))
            for peer in range(refs[0].shape[0]):
                refs[0][peer] = packed

    @pl.when(jnp.logical_not(live))
    def _():
        kept = jnp.zeros((24, 128), F32)
        for s in saved:
            kept = kept + s[...]
        kept_ref[...] = kept
        if not last:
            refs[0][...] = jnp.zeros(refs[0].shape, F32)


def factored(packed, absent):
    row = iota((R, 128), 0)
    lane = iota((R, 128), 1)
    eye = jnp.where(lane == row, 1.0, 0.0)
    full = whole(packed) + eye * absent + jnp.where(lane == row + 64, 1.0, 0.0)
    m = [full[8 * t : 8 * t + 8] for t in range(R // 8)]
    for begin in range(0, R, 4):
        top = begin // 8
        below = range(top, R // 8)
        col = [
            {t: jnp.broadcast_to(m[t][:, begin + k : begin + k + 1], (8, 128)) for t in below} for k in range(4)
        ]
        for k in range(4):
            at = begin + k - 8 * top
            scale = 1.0 / col[k][top][at : at + 1]
            fact = {t: col[k][t] * scale for t in below}
            fact[top] = jnp.where(iota((8, 128), 0) > at, fact[top], 0.0)
            pivot = m[top][at : at + 1]
            for q in range(k + 1, 4):
                lead = col[q][top][at : at + 1]
                for t in below:
                    col[q][t] = col[q][t] - fact[t] * lead
            for t in below:
                m[t] = m[t] - fact[t] * pivot
    m = jnp.concatenate(m, axis=0)
    diag = jnp.sum(jnp.where(lane == row, m, 0.0), axis=1, keepdims=True)
    return m * (1.0 / jnp.sqrt(diag))


def from_left(tri, in_ref, out_ref):
    for g in range(GROUPS):
        rows = slice(g * R, (g + 1) * R)
        out_ref[rows, :] = jnp.dot(
            tri[:, :R], in_ref[rows, :], preferred_element_type=F32, precision=HIGH
        )


def from_right(tri, in_ref, out_ref, block_ref):
    inv = jnp.where(iota((R, 128), 1) < R, pltpu.roll(tri, 64, 1), 0.0)
    wide = jnp.concatenate([inv, jnp.zeros((R, LANES - 128), F32)], axis=1)
    for h in range(WIDE):
        block_ref[h * R : (h + 1) * R, :] = pltpu.roll(wide, h * R, 1) if h else wide
    out_ref[...] = dot_lanes(in_ref[...], block_ref[...], HIGH)


def applied(tri, left, in_ref, out_ref, block_ref):
    @pl.when(left)
    def _():
        from_left(tri, in_ref, out_ref)

    @pl.when(jnp.logical_not(left))
    def _():
        from_right(tri, in_ref, out_ref, block_ref)


def known_kernel(*refs):
    *sums, core_ref, out_ref, block_ref = refs
    mode = lax.axis_index("cores")
    chip = mode // 2
    first = jnp.where(mode % 2 == 0, 1.0, 0.0)
    known = jnp.zeros((24, 128), F32)
    for p, s in enumerate(sums):
        known = known + s[...] * jnp.where(chip == p, 1.0 - first, 0.0)
        known = known + s[...] * jnp.where(chip == p + 1, first, 0.0)
    absent = jnp.where(jnp.logical_or(mode == 0, mode == MODES - 1), 1.0, 0.0)
    applied(factored(known, absent), mode % 2 == 0, core_ref, out_ref, block_ref)


def final_kernel(a_ref, b_ref, c_ref, d_ref, core_ref, out_ref, block_ref, flat_ref):
    level = (a_ref[...] + b_ref[...]) + (c_ref[...] + d_ref[...])
    odd = lax.axis_index("cores") % 2 == 1
    applied(factored(level, 0.0), odd, core_ref, flat_ref, block_ref)
    for g in range(GROUPS):
        for h in range(WIDE):
            out_ref[g * WIDE + h] = flat_ref[g * R : (g + 1) * R, h * R : (h + 1) * R]


def vmem():
    return pl.BlockSpec(memory_space=pltpu.VMEM)


def smem():
    return pl.BlockSpec(memory_space=pltpu.SMEM)


def call(kernel, outs, ins, scratch=(), name=None, aliases={}):
    return pl.pallas_call(
        kernel,
        out_shape=outs,
        in_specs=ins,
        out_specs=jax.tree.map(lambda o: smem() if o.dtype == jnp.int32 and o.size == 1 else vmem(), outs),
        scratch_shapes=list(scratch),
        input_output_aliases=aliases,
        compiler_params=pltpu.CompilerParams(vmem_limit_bytes=BIG),
        name=name,
    )


def shape(*dims, dtype=F32):
    return jax.ShapeDtypeStruct(dims, dtype)


def on_device(cores, indices, observed, step_size):
    peers = lax.axis_size("samp")
    count = indices.shape[0]
    slab = N // peers
    table = cores[0]
    idx = indices.T
    step = step_size.reshape(1)

    half = count // 2
    siblings = [(m, m ^ 1) for m in range(MODES)]
    other_table = lax.ppermute(table, "cores", siblings)
    hot = [pltpu.VMEM((N, half), BF16)]
    mats, slot, most = pl.pallas_call(
        functools.partial(gather_kernel, peers=peers),
        grid=(RR // COLS,),
        in_specs=[
            pl.BlockSpec((MODES, count), lambda i: (0, 0)),
            pl.BlockSpec((N, COLS), lambda i: (0, i)),
        ],
        out_specs=[vmem(), vmem(), vmem()],
        out_shape=[shape(2 * RR, half), shape(8, count, dtype=jnp.int32), shape(8, 128)],
        scratch_shapes=hot,
        compiler_params=pltpu.CompilerParams(vmem_limit_bytes=BIG),
        name="gather",
    )(*[pltpu.with_memory_space_constraint(a, pltpu.HBM) for a in (idx, table)])
    mats = call(
        gather_other_kernel, shape(2 * RR, half), [vmem()] * 3, hot, name="gather_other", aliases={2: 0}
    )(idx, other_table, mats)

    first = lax.axis_index("samp") * slab
    kept = lax.dynamic_slice_in_dim(table, first, slab, 0)
    base = kept.reshape(GROUPS, WIDE, R, R).transpose(0, 2, 1, 3)
    base = base.reshape(ROWS, LANES)

    vec = shape(R, half)
    recv, mids = [], []
    for turn in range(3):
        mid, out = call(
            functools.partial(hop_kernel, turn=turn),
            [vec, vec],
            [vmem()] * (2 if turn else 1),
            name=f"hop{turn}",
        )(mats, *recv[-1:])
        pairs = [(2 * a + h, 2 * b + h) for a, b in ((turn, turn + 1), (3 - turn, 2 - turn)) for h in range(2)]
        recv.append(lax.ppermute(out, "cores", pairs))
        mids.append(mid)
    own_vecs, other_vecs = call(
        finish_kernel,
        [shape(2 * R, half)] * 2,
        [vmem()] * 9,
        [pltpu.VMEM((R, half), F32)] * 2,
        name="finish",
    )(mats, *recv, *mids, out, observed.reshape(1, count))
    got_vecs = lax.ppermute(other_vecs, "cores", siblings)
    part = call(route_own_kernel, shape(peers, FEATS, SLOTS), [vmem()] * 2, name="route_own")(own_vecs, slot)
    pay, values = call(
        route_kernel,
        (shape(peers, FEATS, SLOTS), shape(FEATS, count)),
        [vmem()] * 5,
        name="route",
    )(own_vecs, got_vecs, slot, most, part)

    def exchanged(block):
        return lax.all_to_all(block, "samp", 0, 0, tiled=True)

    def collected(recv, so_far):
        return call(
            collect_kernel,
            (shape(ROWS, LANES), shape(1, dtype=jnp.int32)),
            [smem(), vmem(), vmem()],
            name="collect",
        )(step, recv, so_far)

    updated, turns = collected(exchanged(pay), base)

    def more(state):
        return state[0] < turns[0]

    def another(state):
        turn, so_far = state
        pay = call(
            again_kernel,
            shape(peers, FEATS, SLOTS),
            [smem(), vmem(), vmem(), vmem()],
            name="again",
        )(turn.reshape(1), values, slot, most)
        return turn + 1, collected(exchanged(pay), so_far)[0]

    _, updated = lax.while_loop(more, another, (jnp.int32(1), updated))

    side = int(peers**0.5)

    def partner(mode, peer, by):
        z, x = peer // side, peer % side
        return (z + by) % side * side + x if mode % 2 else z * side + (x + by) % side

    ring = [
        [(m * peers + p, m * peers + partner(m, p, w)) for m in range(MODES) for p in range(peers)]
        for w in range(1, WAYS)
    ]
    level = [[(p, partner(1, p, w)) for p in range(peers)] for w in range(1, WAYS)]
    own = [updated] + [lax.ppermute(updated, ("cores", "samp"), pairs) for pairs in ring]
    other = [lax.ppermute(o, "cores", siblings) for o in own]
    stack = shape(3 * WAYS * ROWS, LANES, dtype=BF16)
    flat = shape(LANES, 3 * WAYS * ROWS, dtype=BF16)

    saved, sums = [], []
    recv = None
    for pair in range(MODES // 2):
        last = pair == MODES // 2 - 1
        outs = [shape(24, 128)] if last else [shape(2 * peers, 24, 128), shape(24, 128)]
        if pair:
            ins = [recv] + (saved + even if last else even + odd)
            outs.append(shape(24, 128))
        else:
            ins = own + other
            outs = [stack, flat] * 2 + outs
        res = call(
            functools.partial(pair_kernel, pair=pair),
            outs,
            [vmem()] * len(ins),
            [pltpu.VMEM((3 * WAYS * ROWS, LANES), BF16)],
            name=f"pair{pair}",
        )(*ins)
        if pair:
            sums.append(res[-1])
        else:
            even, odd, res = list(res[:2]), list(res[2:4]), res[4:]
        if last:
            parts = [res[0]] + [lax.ppermute(res[0], "samp", pairs) for pairs in level]
        else:
            saved.append(res[1])
            groups = []
            for c in (pair, pair + 2):
                for h in range(2):
                    both = [2 * (c % 4) + h, 2 * ((c + 1) % 4) + h]
                    groups.append([m * peers + j for m in both for j in range(peers)])
            recv = lax.all_to_all(
                res[0], ("cores", "samp"), 0, 0, axis_index_groups=groups, tiled=True
            )

    block = [pltpu.VMEM((LANES, LANES), F32)]
    ahead = call(known_kernel, shape(ROWS, LANES), [vmem()] * (MODES // 2), block, name="known")(*sums, updated)
    block.append(pltpu.VMEM((ROWS, LANES), F32))
    out = call(final_kernel, shape(slab, R, R), [vmem()] * (WAYS + 1), block, name="final")(*parts, ahead)
    return out.reshape(1, slab, RR)


def solution(mesh):
    in_specs = (P("cores", None, None), P("samp", None), P("samp"), P())
    out_specs = P("cores", "samp", None)
    return jax.shard_map(
        on_device, mesh=mesh, in_specs=in_specs, out_specs=out_specs, check_vma=False
    )
```

```python
import functools

import jax
import jax.numpy as jnp
from jax import lax
from jax.experimental import pallas as pl
from jax.experimental.pallas import tpu as pltpu
from jax.sharding import PartitionSpec as P

R = 48
N = 512
MODES = 8
RR = R * R
GROUPS = 4
WIDE = 8
ROWS = GROUPS * R
LANES = WIDE * R
FEATS = 104
SLOTS = 128
WAYS = 4
HIGH = lax.Precision.HIGHEST
F32 = jnp.float32
BF16 = jnp.bfloat16
COLS = 768
BIG = 14 << 20


def dot_rows(a, b):
    return lax.dot_general(a, b, (((0,), (0,)), ((), ())), preferred_element_type=F32)


def dot_lanes(a, b, precision=None):
    return lax.dot_general(
        a, b, (((1,), (1,)), ((), ())), preferred_element_type=F32, precision=precision
    )


def halves(x):
    hi = x.astype(BF16)
    return hi, (x - hi.astype(F32)).astype(BF16)


def iota(shape, dim):
    return lax.broadcasted_iota(jnp.int32, shape, dim)


def ranks(row, peers, slab):
    count = row.shape[1]
    chunks = count // 128
    dest = row // slab
    hit = (iota((peers, count), 0) == dest).astype(F32)
    stacked = jnp.concatenate([hit[:, c * 128 : (c + 1) * 128] for c in range(chunks)], axis=0)
    upper = (iota((128, 128), 0) <= iota((128, 128), 1)).astype(BF16)
    inside = jnp.dot(stacked.astype(BF16), upper, preferred_element_type=F32)
    before = jnp.zeros((peers, 1), F32)
    out = []
    for c in range(chunks):
        part = inside[c * peers : (c + 1) * peers]
        mine = hit[:, c * 128 : (c + 1) * 128]
        out.append(jnp.sum(mine * (part + before), axis=0, keepdims=True))
        before = before + part[:, 127:128]
    return jnp.concatenate(out, axis=1).astype(jnp.int32) - 1, dest


def half_of(row, second):
    half = row.shape[1] // 2
    flag = jnp.where(second, 1.0, 0.0)
    return jnp.where(flag > 0.5, row[:, half:], row[:, :half])


def one_hot(row, second, hot_ref):
    hot_ref[...] = (iota(hot_ref.shape, 0) == half_of(row, second)).astype(BF16)


def gathered(table, hot):
    hi, lo = halves(table)
    return dot_rows(hi, hot) + dot_rows(lo, hot)


def gather_kernel(idx_ref, table_ref, mats_ref, slot_ref, most_ref, hot_ref, *, peers):
    step = pl.program_id(0)
    mode = lax.axis_index("cores")

    @pl.when(step == 0)
    def _():
        row = idx_ref[pl.ds(mode, 1), :]
        one_hot(row, mode % 2 == 1, hot_ref)
        slab = N // peers
        place, dest = ranks(row, peers, slab)
        slot_ref[0:1, :] = place
        slot_ref[1:2, :] = dest
        slot_ref[2:3, :] = row - dest * slab
        slot_ref[3:8, :] = jnp.zeros((5, row.shape[1]), jnp.int32)
        every = idx_ref[...] // slab
        most = jnp.zeros((MODES, 1), F32)
        for j in range(peers):
            most = jnp.maximum(most, jnp.sum((every == j).astype(F32), axis=1, keepdims=True))
        most_ref[...] = jnp.broadcast_to(jnp.max(most, axis=0, keepdims=True), (8, 128))

    rows = pl.ds(pl.multiple_of(step * COLS, COLS), COLS)
    mats_ref[rows, :] = gathered(table_ref[...], hot_ref[...])


def gather_other_kernel(idx_ref, table_ref, _, mats_ref, hot_ref):
    mode = lax.axis_index("cores")
    second = mode % 2
    one_hot(idx_ref[pl.ds(mode + 1 - 2 * second, 1), :], second == 1, hot_ref)
    for at in range(0, RR, COLS):
        mats_ref[RR + at : RR + at + COLS, :] = gathered(table_ref[:, at : at + COLS], hot_ref[...])


def times(left, mats_ref, base, vec_ref, out_ref):
    count = vec_ref.shape[1]

    def rows(a):
        return pl.ds(pl.multiple_of(base + a * R, 8), R)

    @pl.when(left)
    def _():
        def chunk(c, _):
            lanes = pl.ds(pl.multiple_of(c * 128, 128), 128)
            acc = [jnp.zeros((R, 128), F32) for _ in range(2)]
            for a in range(R):
                acc[a % 2] = acc[a % 2] + mats_ref[rows(a), lanes] * vec_ref[a : a + 1, lanes]
            out_ref[:, lanes] = acc[0] + acc[1]
            return 0

        lax.fori_loop(0, count // 128, chunk, 0)

    @pl.when(jnp.logical_not(left))
    def _():
        def chunk(c, _):
            lanes = pl.ds(pl.multiple_of(c * 128, 128), 128)
            vec = vec_ref[:, lanes]
            for a in range(0, R, 8):
                sums = [
                    jnp.sum(mats_ref[rows(a + i), lanes] * vec, axis=0, keepdims=True) for i in range(8)
                ]
                out_ref[a : a + 8, lanes] = jnp.concatenate(sums, axis=0)
            return 0

        lax.fori_loop(0, count // 128, chunk, 0)


def heading(turn):
    mode = lax.axis_index("cores")
    chips = MODES // 2
    left = (mode // 2 < chips // 2) if turn < chips // 2 else (mode // 2 >= chips // 2)
    even = (mode % 2) * RR
    return left, jnp.where(left, even, RR - even)


def column(mats_ref, base):
    rows = [mats_ref[pl.ds(pl.multiple_of(base + a * R, 8), 1), :] for a in range(R)]
    return jnp.concatenate(rows, axis=0)


def row(mats_ref, base):
    return mats_ref[pl.ds(pl.multiple_of(base, 8), R), :]


def unit_at_ends(shape_):
    chip = lax.axis_index("cores") // 2
    edge = jnp.where(jnp.logical_or(chip == 0, chip == MODES // 2 - 1), 1.0, 0.0)
    return jnp.where(iota(shape_, 0) == 0, edge, 0.0)


def hop_kernel(mats_ref, *refs, turn):
    mid_ref, out_ref = refs[-2:]
    chip = lax.axis_index("cores") // 2
    live = jnp.logical_or(chip == turn, chip == MODES // 2 - 1 - turn)
    left, base = heading(turn)

    @pl.when(live)
    def _():
        if turn == 0:

            @pl.when(left)
            def _():
                mid_ref[...] = row(mats_ref, base)

            @pl.when(jnp.logical_not(left))
            def _():
                mid_ref[...] = column(mats_ref, base)
        else:
            times(left, mats_ref, base, refs[0], mid_ref)
        times(left, mats_ref, RR - base, mid_ref, out_ref)

    @pl.when(jnp.logical_not(live))
    def _():
        mid_ref[...] = jnp.zeros(mid_ref.shape, F32)
        out_ref[...] = jnp.zeros(out_ref.shape, F32)


def finish_kernel(mats_ref, *refs):
    recv, mids = refs[0:3], refs[3:6]
    out2_ref, obs_ref, own_ref, other_ref, mid_ref, part_ref = refs[6:]
    mode = lax.axis_index("cores")
    left, base = heading(3)
    times(left, mats_ref, base, recv[2], mid_ref)

    @pl.when(left)
    def _():
        part_ref[...] = column(mats_ref, RR - base)

    @pl.when(jnp.logical_not(left))
    def _():
        part_ref[...] = row(mats_ref, RR - base)

    end1 = unit_at_ends(mid_ref.shape) + recv[0][...]
    mid1 = mids[0][...] + mids[1][...]
    end2 = recv[1][...] + recv[2][...]
    mid2 = mids[2][...] + mid_ref[...]
    predicted = jnp.sum(out2_ref[...] * end1 + part_ref[...] * mid_ref[...], axis=0, keepdims=True)
    residual = predicted - half_of(obs_ref[...], mode % 2 == 1)
    early = jnp.where(mode // 2 < MODES // 4, 1.0, 0.0) > 0.5
    even = (jnp.where(early, end1, end2), jnp.where(early, mid2, mid1) * residual)
    odd = (jnp.where(early, mid1, mid2), jnp.where(early, end2, end1) * residual)
    second = jnp.where(mode % 2 == 1, 1.0, 0.0) > 0.5
    for k in range(2):
        rows = slice(k * R, (k + 1) * R)
        own_ref[rows, :] = jnp.where(second, odd[k], even[k])
        other_ref[rows, :] = jnp.where(second, even[k], odd[k])


def keys(slot_ref, turn):
    place = slot_ref[0:1, :] - turn * SLOTS
    fits = jnp.logical_and(place >= 0, place < SLOTS)
    return jnp.where(fits, slot_ref[1:2, :] * SLOTS + place, -1)


def spread(values, key, pay_ref, so_far_ref=None):
    hi, lo = halves(values)
    both = jnp.concatenate([hi, lo], axis=0)
    for pair in range(pay_ref.shape[0] // 2):
        base = pair * 2 * SLOTS
        hot = (iota((2 * SLOTS, values.shape[1]), 0) + base == key).astype(BF16)
        out = dot_lanes(both, hot)
        out = out[:FEATS] + out[FEATS:]
        for k in range(2):
            part = out[:, k * SLOTS : (k + 1) * SLOTS]
            peer = 2 * pair + k
            pay_ref[peer] = part if so_far_ref is None else part + so_far_ref[peer]


def mark(most_ref, pay_ref):
    for peer in range(pay_ref.shape[0]):
        pay_ref[peer, 97:98, :] = most_ref[0:1, :]


def with_place(vecs, loc):
    pad = jnp.zeros((FEATS - 97, vecs.shape[1]), F32)
    return jnp.concatenate([vecs, loc.astype(F32), pad], axis=0)


def route_own_kernel(vecs_ref, slot_ref, pay_ref):
    second = lax.axis_index("cores") % 2 == 1
    values = with_place(vecs_ref[...], half_of(slot_ref[2:3, :], second))
    spread(values, half_of(keys(slot_ref, 0), second), pay_ref)


def route_kernel(own_ref, got_ref, slot_ref, most_ref, part_ref, pay_ref, val_ref):
    first = lax.axis_index("cores") % 2 == 0
    own = own_ref[...]
    got = got_ref[...]
    values = with_place(got, half_of(slot_ref[2:3, :], first))
    spread(values, half_of(keys(slot_ref, 0), first), pay_ref, part_ref)
    mark(most_ref, pay_ref)
    flag = jnp.where(first, 1.0, 0.0) > 0.5
    vecs = jnp.concatenate([jnp.where(flag, own, got), jnp.where(flag, got, own)], axis=1)
    val_ref[...] = with_place(vecs, slot_ref[2:3, :])


def again_kernel(turn_ref, val_ref, slot_ref, most_ref, pay_ref):
    spread(val_ref[...], keys(slot_ref, turn_ref[0]), pay_ref)
    mark(most_ref, pay_ref)


def collect_kernel(step_ref, recv_ref, base_ref, out_ref, turns_ref):
    peers = recv_ref.shape[0]
    left = jnp.concatenate([recv_ref[s, 0:R, :] for s in range(peers)], axis=1)
    right = jnp.concatenate([recv_ref[s, R : 2 * R, :] for s in range(peers)], axis=1)
    loc = jnp.concatenate([recv_ref[s, 96:97, :] for s in range(peers)], axis=1).astype(jnp.int32)
    row_of = loc // WIDE
    lane_of = loc - row_of * WIDE
    count = loc.shape[1]

    def picked(x, key, n):
        hi = x.astype(BF16).astype(F32)
        lo = x - hi
        his, los = [], []
        for i in range(n):
            here = key == i
            his += [jnp.where(here, hi, 0.0).astype(BF16)]
            los += [jnp.where(here, lo, 0.0).astype(BF16)]
        return jnp.concatenate(his, axis=0), jnp.concatenate(los, axis=0)

    xh, xl = picked(left, row_of, GROUPS)
    yh, yl = picked(right, lane_of, WIDE)
    grad = dot_lanes(xh, yh) + (dot_lanes(xh, yl) + dot_lanes(xl, yh))
    out_ref[...] = base_ref[...] - step_ref[0] * grad
    most = jnp.max(recv_ref[:, 97, :]).astype(jnp.int32)
    turns_ref[0] = (most + SLOTS - 1) // SLOTS


def arrange(refs):
    own = refs[:WAYS]
    other = refs[WAYS : 2 * WAYS]
    outs = refs[2 * WAYS :]
    even_first = jnp.where(lax.axis_index("cores") % 2 == 0, 1.0, 0.0)
    for w in range(WAYS):
        mine = own[w][...]
        theirs = other[w][...]
        for k in range(2):
            stack_ref, turned_ref = outs[2 * k : 2 * k + 2]
            flag = even_first if k == 0 else 1.0 - even_first
            core = jnp.where(flag > 0.5, mine, theirs)
            hi, lo = halves(core)
            for g in range(GROUPS):
                at = 3 * (w * GROUPS + g) * R
                here = slice(g * R, (g + 1) * R)
                stack_ref[at : at + R, :] = hi[here]
                stack_ref[at + R : at + 2 * R, :] = hi[here]
                stack_ref[at + 2 * R : at + 3 * R, :] = lo[here]
            hi, lo = halves(core.T)
            for k3, piece in enumerate((hi, hi, lo)):
                turned_ref[:, (k3 * WAYS + w) * ROWS : (k3 * WAYS + w + 1) * ROWS] = piece


def stacked(square):
    wide = jnp.concatenate([square, jnp.zeros((R, 128), F32)], axis=1)
    hi = wide.astype(BF16).astype(F32)
    lo = wide - hi
    return (hi + (pltpu.roll(lo, R, 1) + pltpu.roll(hi, 2 * R, 1)))[:, : 3 * R].astype(BF16)


def packed_of(full):
    lane = iota((24, 128), 1)
    return jnp.where(lane < 64, full[0:24], pltpu.roll(full[24:48], 64, 1))


def whole(packed):
    both = jnp.concatenate([packed, pltpu.roll(packed, 64, 1)], axis=0)
    return jnp.where(iota((R, 128), 1) < R, both, 0.0)


def pulled(before, core, prod_ref):
    stack, turned = core
    all_rows = WAYS * ROWS
    weights = None if before is None else stacked(before)
    for g in range(WAYS * GROUPS):
        at = 3 * g * R
        if before is None:
            hi, lo = stack[at : at + R, :], stack[at + 2 * R : at + 3 * R, :]
        else:
            hi, lo = halves(
                jnp.dot(weights, stack[at : at + 3 * R, :], preferred_element_type=F32)
            )
        for k3, piece in enumerate((hi, lo, hi)):
            prod_ref[k3 * all_rows + g * R : k3 * all_rows + (g + 1) * R, :] = piece
    total = jnp.zeros((R, 256), F32)
    for part, slices in ((0, range(5)), (128, range(5, WIDE))):
        cols = slice(part, part + 256)
        z = jnp.dot(turned[cols, :], prod_ref[:, cols], preferred_element_type=F32)
        for h in slices:
            at = h * R - part
            block = z[at : at + R]
            total = total + (pltpu.roll(block, 256 - at, 1) if at else block)
    return jnp.where(iota((R, 128), 1) < R, total[:, :128], 0.0) * (1.0 / N)


def pair_kernel(*refs, pair):
    last = pair == MODES // 2 - 1
    refs = list(refs)
    recv_ref = refs.pop(0) if pair else None
    saved = [refs.pop(0) for _ in range(pair)] if last else []
    prod_ref = refs.pop()
    if pair:
        even = [refs.pop(0) for _ in range(2)]
        odd = None if last else [refs.pop(0) for _ in range(2)]
        sum_ref = refs.pop()
        sum_ref[...] = jnp.sum(recv_ref[0 : recv_ref.shape[0] // 2], axis=0)
    else:
        cores = refs[2 * WAYS : 2 * WAYS + 4]
        slabs = refs[: 2 * WAYS + 4]
        even, odd = cores[:2], cores[2:]
        refs = refs[2 * WAYS + 4 :]
    kept_ref = refs.pop()
    live = lax.axis_index("cores") // 2 == pair

    @pl.when(live)
    def _():
        if not pair:
            arrange(slabs)
        middle = pulled(whole(sum_ref[...]) if pair else None, even, prod_ref)
        kept_ref[...] = packed_of(middle)
        if not last:
            packed = packed_of(pulled(middle, odd, prod_ref))
            for peer in range(refs[0].shape[0]):
                refs[0][peer] = packed

    @pl.when(jnp.logical_not(live))
    def _():
        if not pair:
            arrange(slabs)
        kept = jnp.zeros((24, 128), F32)
        for s in saved:
            kept = kept + s[...]
        kept_ref[...] = kept
        if not last:
            refs[0][...] = jnp.zeros(refs[0].shape, F32)


def factored(packed, absent):
    row = iota((R, 128), 0)
    lane = iota((R, 128), 1)
    eye = jnp.where(lane == row, 1.0, 0.0)
    full = whole(packed) + eye * absent + jnp.where(lane == row + 64, 1.0, 0.0)
    m = [full[8 * t : 8 * t + 8] for t in range(R // 8)]
    for begin in range(0, R, 4):
        top = begin // 8
        below = range(top, R // 8)
        col = [
            {t: jnp.broadcast_to(m[t][:, begin + k : begin + k + 1], (8, 128)) for t in below} for k in range(4)
        ]
        for k in range(4):
            at = begin + k - 8 * top
            scale = 1.0 / col[k][top][at : at + 1]
            fact = {t: col[k][t] * scale for t in below}
            fact[top] = jnp.where(iota((8, 128), 0) > at, fact[top], 0.0)
            pivot = m[top][at : at + 1]
            for q in range(k + 1, 4):
                lead = col[q][top][at : at + 1]
                for t in below:
                    col[q][t] = col[q][t] - fact[t] * lead
            for t in below:
                m[t] = m[t] - fact[t] * pivot
    m = jnp.concatenate(m, axis=0)
    diag = jnp.sum(jnp.where(lane == row, m, 0.0), axis=1, keepdims=True)
    return m * (1.0 / jnp.sqrt(diag))


def from_left(tri, in_ref, out_ref):
    for g in range(GROUPS):
        rows = slice(g * R, (g + 1) * R)
        out_ref[rows, :] = jnp.dot(
            tri[:, :R], in_ref[rows, :], preferred_element_type=F32, precision=HIGH
        )


def from_right(tri, in_ref, out_ref, block_ref):
    inv = jnp.where(iota((R, 128), 1) < R, pltpu.roll(tri, 64, 1), 0.0)
    wide = jnp.concatenate([inv, jnp.zeros((R, LANES - 128), F32)], axis=1)
    for h in range(WIDE):
        block_ref[h * R : (h + 1) * R, :] = pltpu.roll(wide, h * R, 1) if h else wide
    out_ref[...] = dot_lanes(in_ref[...], block_ref[...], HIGH)


def applied(tri, left, in_ref, out_ref, block_ref):
    @pl.when(left)
    def _():
        from_left(tri, in_ref, out_ref)

    @pl.when(jnp.logical_not(left))
    def _():
        from_right(tri, in_ref, out_ref, block_ref)


def known_kernel(*refs):
    *sums, core_ref, out_ref, block_ref = refs
    mode = lax.axis_index("cores")
    chip = mode // 2
    first = jnp.where(mode % 2 == 0, 1.0, 0.0)
    known = jnp.zeros((24, 128), F32)
    for p, s in enumerate(sums):
        known = known + s[...] * jnp.where(chip == p, 1.0 - first, 0.0)
        known = known + s[...] * jnp.where(chip == p + 1, first, 0.0)
    absent = jnp.where(jnp.logical_or(mode == 0, mode == MODES - 1), 1.0, 0.0)
    applied(factored(known, absent), mode % 2 == 0, core_ref, out_ref, block_ref)


def final_kernel(a_ref, b_ref, c_ref, d_ref, core_ref, out_ref, block_ref, flat_ref):
    level = (a_ref[...] + b_ref[...]) + (c_ref[...] + d_ref[...])
    odd = lax.axis_index("cores") % 2 == 1
    applied(factored(level, 0.0), odd, core_ref, flat_ref, block_ref)
    for g in range(GROUPS):
        for h in range(WIDE):
            out_ref[g * WIDE + h] = flat_ref[g * R : (g + 1) * R, h * R : (h + 1) * R]


def vmem():
    return pl.BlockSpec(memory_space=pltpu.VMEM)


def smem():
    return pl.BlockSpec(memory_space=pltpu.SMEM)


def call(kernel, outs, ins, scratch=(), name=None, aliases={}):
    return pl.pallas_call(
        kernel,
        out_shape=outs,
        in_specs=ins,
        out_specs=jax.tree.map(lambda o: smem() if o.dtype == jnp.int32 and o.size == 1 else vmem(), outs),
        scratch_shapes=list(scratch),
        input_output_aliases=aliases,
        compiler_params=pltpu.CompilerParams(vmem_limit_bytes=BIG),
        name=name,
    )


def shape(*dims, dtype=F32):
    return jax.ShapeDtypeStruct(dims, dtype)


def on_device(cores, indices, observed, step_size):
    peers = lax.axis_size("samp")
    count = indices.shape[0]
    slab = N // peers
    table = cores[0]
    idx = indices.T
    step = step_size.reshape(1)

    half = count // 2
    siblings = [(m, m ^ 1) for m in range(MODES)]
    other_table = lax.ppermute(table, "cores", siblings)
    hot = [pltpu.VMEM((N, half), BF16)]
    mats, slot, most = pl.pallas_call(
        functools.partial(gather_kernel, peers=peers),
        grid=(RR // COLS,),
        in_specs=[
            pl.BlockSpec((MODES, count), lambda i: (0, 0)),
            pl.BlockSpec((N, COLS), lambda i: (0, i)),
        ],
        out_specs=[vmem(), vmem(), vmem()],
        out_shape=[shape(2 * RR, half), shape(8, count, dtype=jnp.int32), shape(8, 128)],
        scratch_shapes=hot,
        compiler_params=pltpu.CompilerParams(vmem_limit_bytes=BIG),
        name="gather",
    )(*[pltpu.with_memory_space_constraint(a, pltpu.HBM) for a in (idx, table)])
    mats = call(
        gather_other_kernel, shape(2 * RR, half), [vmem()] * 3, hot, name="gather_other", aliases={2: 0}
    )(idx, other_table, mats)

    first = lax.axis_index("samp") * slab
    kept = lax.dynamic_slice_in_dim(table, first, slab, 0)
    base = kept.reshape(GROUPS, WIDE, R, R).transpose(0, 2, 1, 3)
    base = base.reshape(ROWS, LANES)

    vec = shape(R, half)
    recv, mids = [], []
    for turn in range(3):
        mid, out = call(
            functools.partial(hop_kernel, turn=turn),
            [vec, vec],
            [vmem()] * (2 if turn else 1),
            name=f"hop{turn}",
        )(mats, *recv[-1:])
        pairs = [(2 * a + h, 2 * b + h) for a, b in ((turn, turn + 1), (3 - turn, 2 - turn)) for h in range(2)]
        recv.append(lax.ppermute(out, "cores", pairs))
        mids.append(mid)
    own_vecs, other_vecs = call(
        finish_kernel,
        [shape(2 * R, half)] * 2,
        [vmem()] * 9,
        [pltpu.VMEM((R, half), F32)] * 2,
        name="finish",
    )(mats, *recv, *mids, out, observed.reshape(1, count))
    got_vecs = lax.ppermute(other_vecs, "cores", siblings)
    part = call(route_own_kernel, shape(peers, FEATS, SLOTS), [vmem()] * 2, name="route_own")(own_vecs, slot)
    pay, values = call(
        route_kernel,
        (shape(peers, FEATS, SLOTS), shape(FEATS, count)),
        [vmem()] * 5,
        name="route",
    )(own_vecs, got_vecs, slot, most, part)

    def exchanged(block):
        return lax.all_to_all(block, "samp", 0, 0, tiled=True)

    def collected(recv, so_far):
        return call(
            collect_kernel,
            (shape(ROWS, LANES), shape(1, dtype=jnp.int32)),
            [smem(), vmem(), vmem()],
            name="collect",
        )(step, recv, so_far)

    updated, turns = collected(exchanged(pay), base)

    def more(state):
        return state[0] < turns[0]

    def another(state):
        turn, so_far = state
        pay = call(
            again_kernel,
            shape(peers, FEATS, SLOTS),
            [smem(), vmem(), vmem(), vmem()],
            name="again",
        )(turn.reshape(1), values, slot, most)
        return turn + 1, collected(exchanged(pay), so_far)[0]

    _, updated = lax.while_loop(more, another, (jnp.int32(1), updated))

    side = int(peers**0.5)

    def partner(mode, peer, by):
        z, x = peer // side, peer % side
        return (z + by) % side * side + x if mode % 2 else z * side + (x + by) % side

    ring = [
        [(m * peers + p, m * peers + partner(m, p, w)) for m in range(MODES) for p in range(peers)]
        for w in range(1, WAYS)
    ]
    level = [[(p, partner(1, p, w)) for p in range(peers)] for w in range(1, WAYS)]
    own = [updated] + [lax.ppermute(updated, ("cores", "samp"), pairs) for pairs in ring]
    other = [lax.ppermute(o, "cores", siblings) for o in own]
    stack = shape(3 * WAYS * ROWS, LANES, dtype=BF16)
    flat = shape(LANES, 3 * WAYS * ROWS, dtype=BF16)

    saved, sums = [], []
    recv = None
    for pair in range(MODES // 2):
        last = pair == MODES // 2 - 1
        outs = [shape(24, 128)] if last else [shape(2 * peers, 24, 128), shape(24, 128)]
        if pair:
            ins = [recv] + (saved + even if last else even + odd)
            outs.append(shape(24, 128))
        else:
            ins = own + other
            outs = [stack, flat] * 2 + outs
        res = call(
            functools.partial(pair_kernel, pair=pair),
            outs,
            [vmem()] * len(ins),
            [pltpu.VMEM((3 * WAYS * ROWS, LANES), BF16)],
            name=f"pair{pair}",
        )(*ins)
        if pair:
            sums.append(res[-1])
        else:
            even, odd, res = list(res[:2]), list(res[2:4]), res[4:]
        if last:
            parts = [res[0]] + [lax.ppermute(res[0], "samp", pairs) for pairs in level]
        else:
            saved.append(res[1])
            groups = []
            for c in (pair, pair + 2):
                for h in range(2):
                    both = [2 * (c % 4) + h, 2 * ((c + 1) % 4) + h]
                    groups.append([m * peers + j for m in both for j in range(peers)])
            recv = lax.all_to_all(
                res[0], ("cores", "samp"), 0, 0, axis_index_groups=groups, tiled=True
            )

    block = [pltpu.VMEM((LANES, LANES), F32)]
    ahead = call(known_kernel, shape(ROWS, LANES), [vmem()] * (MODES // 2), block, name="known")(*sums, updated)
    block.append(pltpu.VMEM((ROWS, LANES), F32))
    out = call(final_kernel, shape(slab, R, R), [vmem()] * (WAYS + 1), block, name="final")(*parts, ahead)
    return out.reshape(1, slab, RR)


def solution(mesh):
    in_specs = (P("cores", None, None), P("samp", None), P("samp"), P())
    out_specs = P("cores", "samp", None)
    return jax.shard_map(
        on_device, mesh=mesh, in_specs=in_specs, out_specs=out_specs, check_vma=False
    )
```
